32 devices in a mesh: grp: 2 (over x), ctg: 16 (over z, y, core).
Axes of the slice: x: 2, y: 2, z: 4, core: 2. Of those that a mesh axis runs over, the one named last changes fastest.
Arguments:
- flow_tiles: bfloat16 [128, 256, 3072], P('ctg'), may hold values from -0.109375 to 0.109375
- tile_pattern: int32 [128, 2, 24], P('ctg'), may hold values 0 or 1
- monitored: int32 [128, 256], P('ctg'), may hold values from 0 to 16383
- ratings: float32 [16384], replicated, may hold values from 0.3 to 3
- base_flow: float32 [64, 128, 256], P('grp', 'ctg'), parts along dimension 0, may hold values from -6 to 6
- unit_cost: float32 [64, 3072], P(('grp', 'ctg')), parts along dimension 0, may hold values from -6 to 6
- unit_floor: float32 [3072], replicated, may hold values from 0 to 0.5
- unit_span: float32 [3072], replicated, may hold values from 0.5 to 2
- ramp_limit: float32 [3072], replicated, may hold values from 0.05 to 0.5
- ramp_mask: int32 [3072], replicated, may hold values 0 or 1
- demand: float32 [64], P(('grp', 'ctg')), parts along dimension 0, may hold values from 1228.8 to 2457.6
- start_output: float32 [64, 3072], P(('grp', 'ctg')), parts along dimension 0, may hold values from 0 to 1.5
- start_flow_dual: float32 [64, 128, 256], P('grp', 'ctg'), parts along dimension 0, may hold values from -2 to 2
- start_ramp_dual: float32 [64, 3072], P(('grp', 'ctg')), parts along dimension 0, may hold values from -3 to 3
Outputs:
- output_levels: float32 [64, 3072], P(('grp', 'ctg')), parts along dimension 0
- flow_dual: float32 [64, 128, 256], P('grp', 'ctg'), parts along dimension 0
- ramp_dual: float32 [64, 3072], P(('grp', 'ctg')), parts along dimension 0
- balance_price: float32 [64], P(('grp', 'ctg')), parts along dimension 0
The draws below stay inside these ranges and needn't reach their ends.
There are 2 independent parts, one for each index of `grp`. The reference program is written for one: setup_inputs(seed, part) draws one part's arguments, and reference() takes and returns one part's arrays. A program takes and returns all parts, laid end to end along the dimension named above; an argument that names none is the same for every part. Nothing has to cross between parts.
All inputs are finite; a program needn't handle non-finite values. No bound on the sum of `tile_pattern` on one device may be relied on, other than what follows from the above.
Results may differ from the reference program's by a relative error of at most 0.0045.
Values may be sent and summed in bfloat16 or wider, within the bound.
A program may use at most 128 MiB of HBM per device.

```python
import math
import jax
import jax.numpy as jnp
from jax import lax

UNITS = 3072
MON = 256
LINES = 16384
ITERS = 4
CTGS = 128
HOURS = 32


def draw_base_flow(key, part):
    severity = 0.5 + jnp.arange(CTGS, dtype=jnp.float32) / CTGS
    values = jnp.clip(jax.random.normal(key, (HOURS, CTGS, MON), jnp.float32), -4.0, 4.0)
    return values * severity[None, :, None]


def set_ends(result, own_key, smallest, high):
    longest = result.shape.index(max(result.shape))
    spots = []
    for shift in (0, 1):
        where = [jax.random.randint(jax.random.fold_in(own_key, axis), (), 0, length) for axis, length in enumerate(result.shape)]
        where[longest] = (where[longest] + shift) % result.shape[longest]
        spots.append(tuple(where))
    return result.at[spots[0]].set(smallest).at[spots[1]].set(high)


def shard_levels(key, dims, shards, smallest, high):
    gain = 1.0
    for dim, shards_of in shards:
        draws = jax.random.uniform(jax.random.fold_in(jax.random.fold_in(key, 6), dim), (shards_of,), jnp.float32, smallest / len(shards), high / len(shards))
        gain = gain * jnp.repeat(jnp.exp(draws), dims[dim] // shards_of).reshape((-1,) + (1,) * (len(dims) - 1 - dim))
    return gain


def centred(key, dims, width, limit, pieces=(), held_as=jnp.bfloat16):
    level = shard_levels(key, dims, pieces, -0.22, 0.18) if pieces else 1.0
    drawn = jax.random.normal(key, dims, jnp.float32) * width * level
    return jnp.minimum(jnp.maximum(drawn, -limit), limit).astype(held_as)


def setup_inputs(seed: int = 0, part: int = 0) -> dict:
    splits = jax.random.split(jax.random.key(seed), 15)
    part_splits = jax.random.split(jax.random.fold_in(splits[14], part), 15)
    flow_tiles = centred(splits[0], (CTGS, MON, UNITS), UNITS ** -0.5, 0.109375, ((0, 16),))
    tile_pattern = set_ends((jax.random.randint(splits[1], (CTGS, MON // 128, UNITS // 128), 0, 2) < 1).astype(jnp.int32), jax.random.fold_in(splits[1], 1), 0, 1)
    monitored = set_ends(jax.random.randint(splits[2], (CTGS, MON), 0, LINES), jax.random.fold_in(splits[2], 1), 0, LINES - 1).astype(jnp.int32)
    ratings = jnp.clip(jnp.exp(jax.random.uniform(splits[3], (LINES,), jnp.float32, math.log(0.3), math.log(3.0))), 0.3, 3.0)
    base_flow = draw_base_flow(jax.random.fold_in(jax.random.fold_in(splits[14], part), 71), part)
    unit_cost = centred(part_splits[5], (HOURS, UNITS), 1.0, 6.0, ((0, 16),), jnp.float32)
    unit_floor = jnp.clip(jax.random.uniform(splits[6], (UNITS,), jnp.float32, 0.0, 0.5), 0.0, 0.5)
    unit_span = jnp.clip(jnp.exp(jax.random.uniform(splits[7], (UNITS,), jnp.float32, math.log(0.5), math.log(2.0))), 0.5, 2.0)
    ramp_limit = jnp.clip(jnp.exp(jax.random.uniform(splits[8], (UNITS,), jnp.float32, math.log(0.05), math.log(0.5))), 0.05, 0.5)
    ramp_mask = set_ends((jax.random.randint(splits[9], (UNITS,), 0, 4) < 3).astype(jnp.int32), jax.random.fold_in(splits[9], 1), 0, 1)
    demand = jnp.clip(1228.8 + 1228.8 * jax.random.uniform(part_splits[10], (HOURS,), jnp.float32) ** shard_levels(part_splits[10], (HOURS,), ((0, 16),), -0.2, 0.2), 1228.8, 2457.6)
    start_output = jnp.clip(1.5 * jax.random.uniform(part_splits[11], (HOURS, UNITS), jnp.float32) ** shard_levels(part_splits[11], (HOURS, UNITS), ((0, 16),), -0.2, 0.2), 0.0, 1.5)
    start_flow_dual = centred(part_splits[12], (HOURS, CTGS, MON), 0.3, 2.0, ((1, 16),), jnp.float32)
    start_ramp_dual = centred(part_splits[13], (HOURS, UNITS), 0.5, 3.0, ((0, 16),), jnp.float32)
    return {"flow_tiles": flow_tiles, "tile_pattern": tile_pattern, "monitored": monitored, "ratings": ratings, "base_flow": base_flow, "unit_cost": unit_cost, "unit_floor": unit_floor, "unit_span": unit_span, "ramp_limit": ramp_limit, "ramp_mask": ramp_mask, "demand": demand, "start_output": start_output, "start_flow_dual": start_flow_dual, "start_ramp_dual": start_ramp_dual}


def mask_tiles(flow_tiles, tile_pattern):
    ctg_count, line_count, unit_count = flow_tiles.shape
    blocks = flow_tiles.reshape(ctg_count, line_count // 128, 128, unit_count // 128, 128)
    gates = tile_pattern.astype(jnp.bfloat16)[:, :, None, :, None]
    return (blocks * gates).reshape(ctg_count, line_count, unit_count)

def reference(flow_tiles, tile_pattern, monitored, ratings, base_flow, unit_cost, unit_floor, unit_span, ramp_limit, ramp_mask, demand, start_output, start_flow_dual, start_ramp_dual):
    masked = mask_tiles(flow_tiles, tile_pattern).astype(jnp.float32)
    flow_limit = ratings[monitored]
    flow_lower = base_flow - flow_limit[None]
    flow_upper = base_flow + flow_limit[None]
    step_size = 0.5 / (2.0 + math.sqrt(CTGS * MON / UNITS))
    balance = 1.0 / math.sqrt(UNITS)
    ceiling = unit_floor + unit_span
    ramp_on = ramp_mask.astype(jnp.float32)
    weight = jnp.float32(1.0)
    levels = start_output
    flow_dual = start_flow_dual
    ramp_dual = start_ramp_dual
    balance_price = jnp.zeros((HOURS,), jnp.float32)
    zero_row = jnp.zeros((1, UNITS), jnp.float32)
    for iteration in range(ITERS):
        primal_step = step_size / weight
        dual_step = step_size * weight
        dual_half = lax.optimization_barrier(flow_dual.astype(jnp.bfloat16)).astype(jnp.float32)
        pulled = jnp.einsum('tkm,kmu->tu', dual_half, masked, precision=lax.Precision.HIGHEST)
        before = jnp.concatenate([zero_row, ramp_dual[:-1]], axis=0)
        gradient = unit_cost + pulled + ramp_on * (before - ramp_dual) + balance * balance_price[:, None]
        moved = jnp.clip(levels - primal_step * gradient, unit_floor, ceiling)
        extended = 2.0 * moved - levels
        extended_half = lax.optimization_barrier(extended.astype(jnp.bfloat16)).astype(jnp.float32)
        flows = jnp.einsum('kmu,tu->tkm', masked, extended_half, precision=lax.Precision.HIGHEST)
        trial = flow_dual + dual_step * flows
        dual_new = trial - dual_step * jnp.clip(trial / dual_step, flow_lower, flow_upper)
        change = ramp_on * jnp.concatenate([extended[1:] - extended[:-1], zero_row], axis=0)
        ramp_trial = ramp_dual + dual_step * change
        ramp_new = ramp_trial - dual_step * jnp.clip(ramp_trial / dual_step, -ramp_limit, ramp_limit)
        balance_row = balance * (lax.optimization_barrier(jnp.sum(extended, axis=1)) - demand)
        price_new = balance_price + dual_step * balance_row
        if iteration < ITERS - 1:
            primal_sq = jnp.sum((moved - levels) ** 2)
            dual_sq = jnp.sum((dual_new - flow_dual) ** 2) + jnp.sum((ramp_new - ramp_dual) ** 2) + jnp.sum((price_new - balance_price) ** 2)
            weight = jnp.sqrt(weight) * ((dual_sq + 1e-06) / (primal_sq + 1e-06)) ** 0.25
        levels = moved
        flow_dual = dual_new
        ramp_dual = ramp_new
        balance_price = price_new
    return (levels, flow_dual, ramp_dual, balance_price)
```

```python
import functools
import math

import jax
import jax.numpy as jnp
from jax import lax
from jax.experimental import pallas as pl
from jax.experimental.pallas import tpu as pltpu
from jax.sharding import PartitionSpec as P

ITERS = 4
ROWS = 32
LAG = 3
IN_FLIGHT = 3
REACH = 1


def send(src, dst, send_sem, recv_sem, target):
    return pltpu.make_async_remote_copy(
        src_ref=src,
        dst_ref=dst,
        send_sem=send_sem,
        recv_sem=recv_sem,
        device_id={"ctg": target},
        device_id_type=pl.DeviceIdType.MESH,
    )


def kernel(
    n, hour_rows, step_size, balance,
    tiles, pattern_hbm, index_hbm, table_hbm, base_hbm, dual_hbm, level_hbm, cost_hbm, ramp_hbm, demand_hbm,
    floor_hbm, span_hbm, ramp_limit_hbm, ramp_mask_hbm,
    out_levels, out_dual, out_ramp, out_price,
    masked, gates, pattern, pattern_rows, index, table, base_in, dual_in, unit_rows, mask_row, demand,
    dual, base, starts, limit, dual_half, flow_acc,
    start_stage, frag_in, frag_out,
    cost, levels, ramp, extended, halo_ext, halo_ramp,
    pull_out, pair_in, pull_sum, pull_in, ext_half, stats, flow_stat, price, omega,
    tile_sem, in_sem, out_sem, frag_send, frag_recv, fin_send, fin_recv,
    pair_send, pair_recv, pull_send, pull_recv, ext_send, ext_recv, pass_send, stat_send, stat_recv,
    core_sems, halo_sems,
):
    f32 = jnp.float32
    bf16 = jnp.bfloat16
    chips = n // 2
    members = ROWS // hour_rows
    groups = n // members
    chunks = chips // groups
    unit_count = tiles.shape[1]
    width = unit_count // chunks
    ctgs, lines = base_in.shape[1], base_in.shape[2]
    hours = groups * ROWS
    pairs = chunks // 2
    halves = lines // 128

    me = lax.axis_index("ctg")
    core = lax.rem(me, 2)
    chip = lax.div(me, 2)
    owner = core == 1
    partner = me + 1 - 2 * core
    my_chunk = lax.div(chip, groups)
    my_group = lax.rem(chip, groups)
    home_group = lax.div(me, members)
    home_row = lax.rem(me, members)
    my_pair = lax.div(my_chunk, 2)
    my_side = lax.rem(my_chunk, 2)
    my_rows = pl.ds(pl.multiple_of(my_group * ROWS, ROWS), ROWS)
    my_lanes = pl.ds(pl.multiple_of(my_chunk * width, 128), width)

    ahead = 1 - lax.div(my_pair, pairs // 2)

    def flip(place, length):
        return ahead * (length - 1 - place) + (1 - ahead) * place

    def skip(place, own, length):
        return place + lax.div(place + length - own, length)

    def far_pair(j):
        last = lax.div(j + 1, pairs)
        place = flip(skip(j, flip(my_pair, pairs), pairs), pairs)
        return last * my_pair + (1 - last) * place

    def near_pair(j):
        return far_pair(pairs - 1 - j)

    def far_chunk(j):
        second = lax.rem(j, 2)
        side = second * my_side + (1 - second) * (1 - my_side)
        return far_pair(lax.div(j, 2)) * 2 + side

    def sums_here(j):
        return ((j < chunks // 2) | (j == chunks - 1)) == owner

    def both_cores(c):
        gap = lax.div(c, 2) - my_pair
        return (gap <= REACH) & (gap >= -REACH)

    def block_rows(g):
        return pl.ds(pl.multiple_of(g * ROWS, ROWS), ROWS)

    def tile_copy(j):
        c = far_chunk(j)
        return pltpu.make_async_copy(
            tiles.at[:, pl.ds(pl.multiple_of(c * width, 128), width)], masked.at[c], tile_sem.at[j]
        )

    def staged(i):
        src, dst = (
            (pattern_hbm, pattern),
            (dual_hbm, dual_in),
            (demand_hbm, demand),
            (level_hbm, starts.at[0]),
            (cost_hbm, starts.at[1]),
            (ramp_hbm, starts.at[2]),
            (index_hbm, index),
            (table_hbm, table),
            (base_hbm, base_in),
            (floor_hbm.at[:, my_lanes], unit_rows.at[0]),
            (span_hbm.at[:, my_lanes], unit_rows.at[1]),
            (ramp_limit_hbm.at[:, my_lanes], unit_rows.at[2]),
            (ramp_mask_hbm.at[:, my_lanes], mask_row),
        )[i]
        return pltpu.make_async_copy(src, dst, in_sem.at[i])

    for i in range(2):
        staged(i).start()
    for j in range(IN_FLIGHT):
        tile_copy(j).start()

    barrier = pltpu.get_barrier_semaphore()

    @pl.loop(1, n)
    def _(d):
        pl.semaphore_signal(
            barrier, inc=1, device_id={"ctg": lax.rem(me + d, n)}, device_id_type=pl.DeviceIdType.MESH
        )

    for i in range(2, 13):
        staged(i).start()

    omega[...] = jnp.ones_like(omega)
    price[...] = jnp.zeros_like(price)

    tile_count = unit_count // 128
    tile_row = lax.broadcasted_iota(jnp.int32, (tile_count, unit_count), 0)
    tile_lane = lax.broadcasted_iota(jnp.int32, (tile_count, unit_count), 1)
    spread = jnp.where(lax.shift_right_logical(tile_lane, 7) == tile_row, 1.0, 0.0).astype(bf16)
    staged(0).wait()
    for k in range(ctgs):
        pattern_rows[k * halves:(k + 1) * halves, :] = pattern[k].astype(f32)
    gate_rows = jnp.dot(pattern_rows[...].astype(bf16), spread, preferred_element_type=f32)
    for c in range(chunks):
        gates[c] = gate_rows[:, c * width:(c + 1) * width]
    staged(1).wait()
    for k in range(ctgs):
        lanes = slice(k * lines, (k + 1) * lines)
        start_dual = dual_in[:, k, :]
        dual[:, lanes] = start_dual
        dual_half[:, lanes] = start_dual.astype(bf16)

    def frag_copy(c, target):
        return send(
            starts.at[:, :, pl.ds(pl.multiple_of(c * width, 128), width)],
            start_stage.at[home_row], frag_send.at[c], frag_recv.at[home_row], target,
        )

    def fin_copy(r, source_chunk, target):
        return send(
            frag_out.at[r], frag_in.at[source_chunk], fin_send.at[r], fin_recv.at[source_chunk], target
        )

    def stat_copy(slot, target_chip, sender_chip):
        return send(
            stats.at[slot, sender_chip], stats.at[slot, sender_chip],
            stat_send.at[slot % 2, target_chip], stat_recv.at[slot % 2, sender_chip], target_chip * 2 + 1,
        )

    def stat_start(slot):
        @pl.loop(1, chips)
        def _(d):
            stat_copy(slot, lax.rem(chip + d, chips), chip).start()

    def stat_wait(slot):
        @pl.loop(1, chips)
        def _(d):
            peer = lax.rem(chip + d, chips)
            stat_copy(slot, peer, chip).wait_send()
            stat_copy(slot, peer, peer).wait_recv()

    def flow_stat_copy(slot):
        return send(flow_stat.at[0], flow_stat.at[slot], core_sems.at[0], core_sems.at[1], partner)

    def omega_copy():
        return send(omega, omega, core_sems.at[2], core_sems.at[3], partner)

    def price_copy():
        return send(price, price, core_sems.at[4], core_sems.at[5], partner)

    def pair_copy(it, c):
        return send(pull_out.at[c], pair_in.at[it, c], pair_send.at[c], pair_recv.at[c], partner)

    def pull_copy(it, target_chip, sender_chip):
        c, g = lax.div(target_chip, groups), lax.rem(target_chip, groups)
        return send(
            pull_sum.at[c, block_rows(g)], pull_in.at[it, sender_chip],
            pull_send.at[target_chip], pull_recv.at[sender_chip], target_chip * 2 + 1,
        )

    def ext_copy(it, origin_chip, send_sem, target):
        c, g = lax.div(origin_chip, groups), lax.rem(origin_chip, groups)
        spot = ext_half.at[it, c, block_rows(g)]
        return send(spot, spot, send_sem, ext_recv.at[origin_chip], target)

    def ext_out(it, target):
        return ext_copy(it, chip, ext_send.at[target], target)

    def ext_pass(it, origin_chip):
        return ext_copy(it, origin_chip, pass_send.at[origin_chip], partner)

    def halo_ext_copy(it, target):
        return send(extended.at[pl.ds(0, 8)], halo_ext.at[it], halo_sems.at[0], halo_sems.at[1], target)

    def halo_ramp_copy(it, target):
        return send(ramp.at[pl.ds(ROWS - 8, 8)], halo_ramp.at[it], halo_sems.at[2], halo_sems.at[3], target)

    def product(c):
        pull_out[c] = jnp.dot(dual_half[...], masked[c], preferred_element_type=f32).astype(bf16)

    def pair_start(it, j):
        @pl.when(jnp.logical_not(sums_here(j)))
        def _():
            pair_copy(it, far_chunk(j)).start()

    def forward(it, j):
        @pl.when(sums_here(j))
        def _():
            c = far_chunk(j)
            pair_copy(it, c).wait_recv()
            for g in range(groups):
                rows = slice(g * ROWS, (g + 1) * ROWS)
                target_chip = c * groups + g
                both = (pull_out[c, rows, :].astype(f32) + pair_in[it, c, rows, :].astype(f32)).astype(bf16)

                @pl.when(target_chip != chip)
                def _():
                    pull_sum[c, rows, :] = both
                    pull_copy(it, target_chip, chip).start()

                @pl.when(target_chip == chip)
                def _():
                    pull_in[it, chip] = both

    def pull_sent(it):
        @pl.loop(0, chunks)
        def _(j):
            here = sums_here(j)
            c = far_chunk(j)

            @pl.when(jnp.logical_not(here))
            def _():
                pair_copy(it, c).wait_send()

            for g in range(groups):
                target_chip = c * groups + g

                @pl.when(here & (target_chip != chip))
                def _():
                    pull_copy(it, target_chip, chip).wait_send()

    def first_product(j):
        c = far_chunk(j)
        tile_copy(j).wait()

        @pl.when(j + IN_FLIGHT < chunks)
        def _():
            tile_copy(j + IN_FLIGHT).start()

        for r in range(ctgs * halves):
            gate = jnp.broadcast_to(gates[c, r:r + 1, :], (16, width)).astype(bf16)
            for q in range(8):
                where = slice(r * 128 + q * 16, r * 128 + q * 16 + 16)
                masked[c, where, :] = masked[c, where, :] * gate

        product(c)

    warm = chunks // 2

    @pl.loop(0, warm)
    def _(j):
        first_product(j)

    for i in range(2, 6):
        staged(i).wait()
    for r in range(hour_rows):
        starts[3, r:r + 1] = jnp.broadcast_to(demand[0:1, r:r + 1], (1, unit_count))
    pl.semaphore_wait(barrier, n - 1)

    @pl.loop(0, warm)
    def _(j):
        pair_start(0, j)

    for c in range(chunks):
        target = (c * groups + home_group) * 2 + 1

        @pl.when(target != me)
        def _():
            frag_copy(c, target).start()

        @pl.when(target == me)
        def _():
            start_stage[home_row] = starts[:, :, c * width:(c + 1) * width]

    @pl.loop(warm, chunks + warm)
    def _(j):
        @pl.when(j < chunks)
        def _():
            first_product(j)
            pair_start(0, j)

        forward(0, j - warm)

    for i in range(6, 13):
        staged(i).wait()

    row_iota = lax.broadcasted_iota(jnp.int32, (128, lines), 0)
    values = table[...].T
    part_a = values.astype(bf16)
    rest = values - part_a.astype(f32)
    part_b = rest.astype(bf16)
    part_c = (rest - part_b.astype(f32)).astype(bf16)
    for k in range(ctgs):
        which = index[k:k + 1, :]
        high = lax.shift_right_logical(which, 7)
        low = lax.bitwise_and(which, 127)
        blocks = table.shape[0] // 128
        got = jnp.zeros((128, lines), f32)
        for b in range(blocks):
            pick = jnp.where(row_iota + b * 128 == high, 1.0, 0.0).astype(bf16)
            for part in (part_a, part_b, part_c):
                got = got + jnp.dot(part[:, b * 128:(b + 1) * 128], pick, preferred_element_type=f32)
        limit[:, k * lines:(k + 1) * lines] = jnp.sum(
            jnp.where(row_iota == low, got, 0.0), axis=0, keepdims=True
        )
        base[:, k * lines:(k + 1) * lines] = base_in[:, k, :]

    block_row = lax.broadcasted_iota(jnp.int32, (ROWS, width), 0)
    lane_here = lax.broadcasted_iota(jnp.int32, (ROWS, 128), 1)
    row_here = lax.broadcasted_iota(jnp.int32, (ROWS, 128), 0) + my_group * ROWS
    diagonal = lane_here == row_here
    hour_lanes = lax.broadcasted_iota(jnp.int32, (1, 128), 1) < hours
    stat_row = lax.broadcasted_iota(jnp.int32, (4, 128), 0)

    def to_lanes(column):
        return jnp.sum(
            jnp.where(diagonal, jnp.broadcast_to(column, (ROWS, 128)), 0.0), axis=0, keepdims=True
        )

    def fold(x):
        rows, cols = x.shape
        out = None
        for r in range(0, rows, 8):
            for b in range(0, cols, 128):
                piece = x[r:r + 8, b:b + 128]
                out = piece if out is None else out + piece
        return jnp.sum(out, axis=0, keepdims=True)

    def halo_ramp_start(it):
        if groups > 1:
            @pl.when(my_group < groups - 1)
            def _():
                halo_ramp_copy(it, me + 2).start()

    @pl.when(owner)
    def _():
        for r in range(members):
            peer = my_group * members + r

            @pl.when(peer != me)
            def _():
                send(
                    starts.at[:, :, pl.ds(0, width)], start_stage.at[r],
                    frag_send.at[0], frag_recv.at[r], peer,
                ).wait_recv()

        demand_rows = []
        for r in range(members):
            rows = slice(r * hour_rows, (r + 1) * hour_rows)
            levels[rows, :] = start_stage[r, 0]
            cost[rows, :] = start_stage[r, 1]
            ramp[rows, :] = start_stage[r, 2]
            extended[rows, 0:128] = start_stage[r, 3, :, 0:128]
        lanes = to_lanes(extended[:, 0:1])
        mine = (stat_row == 0) & (jnp.full((4, 128), my_chunk) == 0)
        stats[0, chip] = jnp.where(mine, lanes, 0.0)
        stat_start(0)
        halo_ramp_start(0)

    for c in range(chunks):
        target = (c * groups + home_group) * 2 + 1

        @pl.when(target != me)
        def _():
            frag_copy(c, target).wait_send()

    def absorb(slot, sigma):
        total = stats[slot, 0]
        for q in range(1, chips):
            total = total + stats[slot, q]
        move = sigma * (balance * (total[0:1] - price[1:2]))
        move = jnp.where(hour_lanes, move, 0.0)
        price[0:1] = price[0:1] + move
        return total, jnp.sum(move * move, axis=1, keepdims=True)

    def primal(it):
        @pl.when(it > 0)
        def _():
            stat_wait(it)

        @pl.when(it == 1)
        def _():
            stat_wait(0)
            first = stats[0, 0]
            for q in range(1, chips):
                first = first + stats[0, q]
            price[1:2] = first[0:1]

        @pl.when(it > 0)
        def _():
            old = omega[0:1, 0:1]
            total, price_sq = absorb(it, step_size * old)
            sums = jnp.sum(total, axis=1, keepdims=True)
            dual_sq = sums[3:4] + sums[2:3] + price_sq
            ratio = (dual_sq + 1e-06) / (sums[1:2] + 1e-06)
            omega[...] = jnp.broadcast_to(jnp.sqrt(old) * jnp.sqrt(jnp.sqrt(ratio)), omega.shape)
            omega_copy().start()

        weight = omega[0:1, 0:1]
        tau = step_size / weight
        sigma = step_size * weight

        if groups > 1:
            @pl.when(my_group < groups - 1)
            def _():
                halo_ramp_copy(it, me + 2).wait_send()

            @pl.when(my_group > 0)
            def _():
                halo_ramp_copy(it, me - 2).wait_recv()

            @pl.when(my_group == 0)
            def _():
                halo_ramp[it] = jnp.zeros_like(halo_ramp[it])

            edge_ramp = halo_ramp[it][7:8]
        else:
            edge_ramp = jnp.zeros((1, width), f32)

        floor = unit_rows[0]
        ceiling = floor + unit_rows[1]
        ramp_limit = unit_rows[2]
        ramp_on = mask_row[...].astype(f32)
        ramp_now = ramp[...]
        before = jnp.where(block_row == 0, edge_ramp, pltpu.roll(ramp_now, 1, 0))
        price_here = jnp.sum(
            jnp.where(diagonal, jnp.broadcast_to(price[0:1], (ROWS, 128)), 0.0), axis=1, keepdims=True
        )
        known = cost[...] + ramp_on * (before - ramp_now) + balance * price_here

        @pl.loop(1, chips)
        def _(d):
            other = lax.rem(chip + d, chips)
            pull_copy(it, other, other).wait_recv()

        pulled = pull_in[it, 0].astype(f32)
        for q in range(1, chips):
            pulled = pulled + pull_in[it, q].astype(f32)

        gradient = known + pulled
        old_levels = levels[...]
        moved = jnp.clip(old_levels - tau * gradient, floor, ceiling)
        ext = 2.0 * moved - old_levels
        levels[...] = moved
        ext_half[it, my_chunk, my_rows, :] = ext.astype(bf16)
        extended[...] = ext

        @pl.loop(0, chunks)
        def _(j):
            c = far_chunk(j)
            for g in range(groups):
                other = c * groups + g

                @pl.when(other != chip)
                def _():
                    ext_out(it, other * 2 + 1).start()

                @pl.when(both_cores(c))
                def _():
                    ext_out(it, other * 2).start()

        if groups > 1:
            @pl.when(my_group > 0)
            def _():
                halo_ext_copy(it, me - 2).start()
                halo_ext_copy(it, me - 2).wait_send()

            @pl.when(my_group < groups - 1)
            def _():
                halo_ext_copy(it, me + 2).wait_recv()

            @pl.when(my_group == groups - 1)
            def _():
                halo_ext[it] = jnp.zeros_like(halo_ext[it])

            edge_ext = halo_ext[it][0:1]
        else:
            edge_ext = jnp.zeros((1, width), f32)

        after = jnp.where(block_row == ROWS - 1, edge_ext, pltpu.roll(ext, ROWS - 1, 0))
        change = ramp_on * (after - ext)
        last_hour = block_row + my_group * ROWS == hours - 1
        change = jnp.where(last_hour, 0.0, change)
        trial = ramp_now + sigma * change
        ramp_new = trial - sigma * jnp.clip(trial / sigma, -ramp_limit, ramp_limit)
        ramp[...] = ramp_new

        row_sums = to_lanes(jnp.sum(ext, axis=1, keepdims=True))
        primal_sq = fold((moved - old_levels) ** 2)
        ramp_sq = fold((ramp_new - ramp_now) ** 2)
        stats[it + 1, chip] = jnp.where(
            stat_row == 0, row_sums,
            jnp.where(stat_row == 1, primal_sq, jnp.where(stat_row == 2, ramp_sq, 0.0)),
        )

        @pl.when(it == ITERS - 1)
        def _():
            stat_start(it + 1)
            for r in range(members):
                rows = slice(r * hour_rows, (r + 1) * hour_rows)
                frag_out[r, 0] = moved[rows, :]
                frag_out[r, 1] = ramp_new[rows, :]
            for r in range(members):
                target = my_group * members + r

                @pl.when(target != me)
                def _():
                    fin_copy(r, my_chunk, target).start()

                @pl.when(target == me)
                def _():
                    frag_in[my_chunk] = frag_out[r]

    def take(it, c):
        for g in range(groups):
            other = c * groups + g

            @pl.when(jnp.logical_not(owner & (other == chip)))
            def _():
                ext_pass(it, other).wait_recv()

    def take_and_pass(it, c):
        take(it, c)

        @pl.when(owner & jnp.logical_not(both_cores(c)))
        def _():
            for g in range(groups):
                ext_pass(it, c * groups + g).start()

    def flow(x, w):
        return lax.dot_general(x, w, (((1,), (1,)), ((), ())), preferred_element_type=f32)

    @pl.loop(0, ITERS)
    def _(it):
        @pl.when(it > 0)
        def _():
            @pl.loop(0, chunks + LAG)
            def _(j):
                @pl.when(j < chunks)
                def _():
                    product(far_chunk(j))
                    pair_start(it, j)

                @pl.when((j == LAG) & owner)
                def _():
                    halo_ramp_start(it)
                    flow_stat_copy(it).wait_recv()
                    stats[it, chip, 3:4] = stats[it, chip, 3:4] + flow_stat[it, 0:1]
                    stat_start(it)

                @pl.when(j >= LAG)
                def _():
                    forward(it, j - LAG)

        pull_sent(it)

        @pl.when(owner)
        def _():
            primal(it)

        take(it, my_chunk)
        flow_acc[...] = flow(ext_half[it, my_chunk], masked[my_chunk])
        near = my_pair * 2 + 1 - my_side
        first = near_pair(1) * 2
        take_and_pass(it, first)
        take_and_pass(it, first + 1)
        take(it, near)
        flow_acc[...] += flow(ext_half[it, near], masked[near])

        @pl.loop(1, pairs)
        def _(j):
            @pl.when(j + 1 < pairs)
            def _():
                following = near_pair(j + 1) * 2
                take_and_pass(it, following)
                take_and_pass(it, following + 1)

            c = near_pair(j) * 2
            x = jnp.concatenate([ext_half[it, c], ext_half[it, c + 1]], axis=1)
            w = jnp.concatenate([masked[c], masked[c + 1]], axis=1)
            flow_acc[...] += flow(x, w)

        @pl.when(owner)
        def _():
            @pl.loop(0, chunks)
            def _(c):
                for g in range(groups):
                    other = c * groups + g

                    @pl.when(other != chip)
                    def _():
                        ext_out(it, other * 2 + 1).wait_send()

                    @pl.when(both_cores(c))
                    def _():
                        ext_out(it, other * 2).wait_send()

                    @pl.when(jnp.logical_not(both_cores(c)))
                    def _():
                        ext_pass(it, other).wait_send()

            @pl.when(it > 0)
            def _():
                omega_copy().wait_send()

        @pl.when((it > 0) & jnp.logical_not(owner))
        def _():
            omega_copy().wait_recv()

        sigma = step_size * omega[0:1, 0:1]
        old_dual = dual[...]
        trial = old_dual + sigma * flow_acc[...]
        bound = limit[...]
        dual_new = trial - sigma * jnp.clip(trial / sigma, base[...] - bound, base[...] + bound)
        dual[...] = dual_new
        dual_half[...] = dual_new.astype(bf16)

        @pl.when(it < ITERS - 1)
        def _():
            flow_sq = fold((dual_new - old_dual) ** 2)

            @pl.when(owner)
            def _():
                stats[it + 1, chip, 3:4] = flow_sq

            @pl.when(jnp.logical_not(owner))
            def _():
                @pl.when(it > 0)
                def _():
                    flow_stat_copy(it).wait_send()

                flow_stat[0] = jnp.broadcast_to(flow_sq, (8, 128))
                flow_stat_copy(it + 1).start()

    dual_out = pltpu.make_async_copy(dual, out_dual, out_sem.at[0])
    dual_out.start()

    @pl.when(owner)
    def _():
        stat_wait(ITERS)
        absorb(ITERS, step_size * omega[0:1, 0:1])
        price_copy().start()

    for c in range(chunks):
        peer = (c * groups + home_group) * 2 + 1

        @pl.when(peer != me)
        def _():
            fin_copy(0, c, peer).wait_recv()

    def level_out(c, which, out):
        return pltpu.make_async_copy(
            frag_in.at[c, which], out.at[:, pl.ds(c * width, width)], out_sem.at[2 + 2 * c + which]
        )

    for c in range(chunks):
        level_out(c, 0, out_levels).start()
        level_out(c, 1, out_ramp).start()

    @pl.when(owner)
    def _():
        for r in range(members):
            target = my_group * members + r

            @pl.when(target != me)
            def _():
                fin_copy(r, my_chunk, target).wait_send()

        price_copy().wait_send()

    @pl.when(jnp.logical_not(owner))
    def _():
        flow_stat_copy(0).wait_send()
        price_copy().wait_recv()

    price_out = pltpu.make_async_copy(price, out_price, out_sem.at[1])
    price_out.start()
    for c in range(chunks):
        level_out(c, 0, out_levels).wait()
        level_out(c, 1, out_ramp).wait()
    price_out.wait()
    dual_out.wait()


def finish(levels, dual, ramp, price, out_levels, out_dual, out_ramp, out_price):
    lines = out_dual.shape[2]
    out_levels[...] = levels[...]
    out_ramp[...] = ramp[...]
    for k in range(out_dual.shape[1]):
        out_dual[:, k, :] = dual[:, k * lines:(k + 1) * lines]
    hour_rows = out_price.shape[0]
    lane = lax.broadcasted_iota(jnp.int32, (1, 128), 1) - lax.axis_index("ctg") * hour_rows
    for r in range(hour_rows):
        out_price[r] = jnp.sum(jnp.where(lane == r, price[0:1], 0.0))


def body(
    flow_tiles,
    tile_pattern,
    monitored,
    ratings,
    base_flow,
    unit_cost,
    unit_floor,
    unit_span,
    ramp_limit,
    ramp_mask,
    demand,
    start_output,
    start_flow_dual,
    start_ramp_dual,
):
    f32, bf16 = jnp.float32, jnp.bfloat16
    ctgs, lines, unit_count = flow_tiles.shape
    n = lax.axis_size("ctg")
    hour_rows = start_output.shape[0]
    hours = hour_rows * n
    groups = hours // ROWS
    chips = n // 2
    chunks = chips // groups
    members = ROWS // hour_rows
    width = unit_count // chunks
    flat = ctgs * lines
    step_size = 0.5 / (2.0 + math.sqrt(ctgs * n * lines / unit_count))
    balance = 1.0 / math.sqrt(unit_count)

    gate_rows = ctgs * tile_pattern.shape[1]

    vmem = pl.BlockSpec(memory_space=pltpu.VMEM)
    hbm = pl.BlockSpec(memory_space=pl.ANY)
    sem = pltpu.SemaphoreType.DMA
    out = pl.pallas_call(
        functools.partial(kernel, n, hour_rows, step_size, balance),
        out_shape=(
            jax.ShapeDtypeStruct((hour_rows, unit_count), f32),
            jax.ShapeDtypeStruct((hours, flat), f32),
            jax.ShapeDtypeStruct((hour_rows, unit_count), f32),
            jax.ShapeDtypeStruct((8, 128), f32),
        ),
        in_specs=[hbm] * 14,
        out_specs=(hbm,) * 4,
        scratch_shapes=[
            pltpu.VMEM((chunks, flat, width), bf16),
            pltpu.VMEM((chunks, gate_rows, width), f32),
            pltpu.VMEM(tile_pattern.shape, jnp.int32),
            pltpu.VMEM((gate_rows, tile_pattern.shape[2]), f32),
            pltpu.VMEM(monitored.shape, jnp.int32),
            pltpu.VMEM((ratings.shape[0] // 128, 128), f32),
            pltpu.VMEM(base_flow.shape, f32),
            pltpu.VMEM(start_flow_dual.shape, f32),
            pltpu.VMEM((3, 1, width), f32),
            pltpu.VMEM((1, width), jnp.int32),
            pltpu.VMEM((1, hour_rows), f32),
            pltpu.VMEM((hours, flat), f32),
            pltpu.VMEM((hours, flat), f32),
            pltpu.VMEM((4, hour_rows, unit_count), f32),
            pltpu.VMEM((1, flat), f32),
            pltpu.VMEM((hours, flat), bf16),
            pltpu.VMEM((hours, flat), f32),
            pltpu.VMEM((members, 4, hour_rows, width), f32),
            pltpu.VMEM((chunks, 2, hour_rows, width), f32),
            pltpu.VMEM((members, 2, hour_rows, width), f32),
            pltpu.VMEM((ROWS, width), f32),
            pltpu.VMEM((ROWS, width), f32),
            pltpu.VMEM((ROWS, width), f32),
            pltpu.VMEM((ROWS, width), f32),
            pltpu.VMEM((ITERS, 8, width), f32),
            pltpu.VMEM((ITERS, 8, width), f32),
            pltpu.VMEM((chunks, hours, width), bf16),
            pltpu.VMEM((ITERS, chunks, hours, width), bf16),
            pltpu.VMEM((chunks, hours, width), bf16),
            pltpu.VMEM((ITERS, chips, ROWS, width), bf16),
            pltpu.VMEM((ITERS, chunks, hours, width), bf16),
            pltpu.VMEM((ITERS + 1, chips, 4, 128), f32),
            pltpu.VMEM((ITERS, 8, 128), f32),
            pltpu.VMEM((8, 128), f32),
            pltpu.VMEM((8, 128), f32),
            sem((chunks,)), sem((13,)), sem((2 + 2 * chunks,)),
            sem((chunks,)), sem((members,)), sem((members,)), sem((chunks,)),
            sem((chunks,)), sem((chunks,)), sem((chips,)), sem((chips,)),
            sem((n,)), sem((chips,)), sem((chips,)),
            sem((2, chips)), sem((2, chips)),
            sem((6,)), sem((4,)),
        ],
        compiler_params=pltpu.CompilerParams(collective_id=0, has_side_effects=True),
    )(
        flow_tiles.reshape(flat, unit_count),
        tile_pattern,
        monitored,
        ratings.reshape(-1, 128),
        base_flow,
        start_flow_dual,
        start_output,
        unit_cost,
        start_ramp_dual,
        demand[None],
        unit_floor[None],
        unit_span[None],
        ramp_limit[None],
        ramp_mask[None],
    )
    return pl.pallas_call(
        finish,
        out_shape=(
            jax.ShapeDtypeStruct((hour_rows, unit_count), f32),
            jax.ShapeDtypeStruct((hours, ctgs, lines), f32),
            jax.ShapeDtypeStruct((hour_rows, unit_count), f32),
            jax.ShapeDtypeStruct((hour_rows,), f32),
        ),
        in_specs=[vmem] * 4,
        out_specs=(vmem,) * 3 + (pl.BlockSpec(memory_space=pltpu.SMEM),),
    )(*out)


def solution(mesh):
    return jax.shard_map(
        body,
        mesh=mesh,
        in_specs=(
            P("ctg", None, None),
            P("ctg", None, None),
            P("ctg", None),
            P(),
            P("grp", "ctg", None),
            P(("grp", "ctg"), None),
            P(),
            P(),
            P(),
            P(),
            P(("grp", "ctg")),
            P(("grp", "ctg"), None),
            P("grp", "ctg", None),
            P(("grp", "ctg"), None),
        ),
        out_specs=(
            P(("grp", "ctg"), None),
            P("grp", "ctg", None),
            P(("grp", "ctg"), None),
            P(("grp", "ctg")),
        ),
        check_vma=False,
    )
```

```python
import functools
import math

import jax
import jax.numpy as jnp
from jax import lax
from jax.experimental import pallas as pl
from jax.experimental.pallas import tpu as pltpu
from jax.sharding import PartitionSpec as P

ITERS = 4
ROWS = 32
STAT = 3
LAG = 0
AHEAD = 1
IN_FLIGHT = 3


def send(src, dst, send_sem, recv_sem, target):
    return pltpu.make_async_remote_copy(
        src_ref=src,
        dst_ref=dst,
        send_sem=send_sem,
        recv_sem=recv_sem,
        device_id={"ctg": target},
        device_id_type=pl.DeviceIdType.MESH,
    )


def kernel(
    n, hour_rows, step_size, balance,
    tiles, pattern_hbm, index_hbm, table_hbm, base_hbm, dual_hbm, level_hbm, cost_hbm, ramp_hbm, demand_hbm,
    floor_hbm, span_hbm, ramp_limit_hbm, ramp_mask_hbm,
    out_levels, out_dual, out_ramp, out_price,
    masked, turned, gates, pattern, pattern_rows, index, table, base_in, dual_in, unit_rows, mask_row, demand,
    dual, base, starts, limit, dual_half, flow_acc,
    start_stage, frag_in, frag_out,
    cost, levels, ramp, extended, halo_ext, halo_ramp,
    pull_out, pair_in, pull_sum, pull_in, ext_half, stats, flow_stat, price, omega,
    frag_send, frag_recv, pair_recv, pull_send, pull_recv, ext_send, ext_recv, stat_send, stat_recv,
    core_sems, halo_sems,
):
    f32 = jnp.float32
    bf16 = jnp.bfloat16
    chips = n // 2
    members = ROWS // hour_rows
    groups = n // members
    chunks = chips // groups
    unit_count = tiles.shape[1]
    width = unit_count // chunks
    ctgs, lines = base_in.shape[1], base_in.shape[2]
    hours = groups * ROWS
    pairs = chunks // 2
    halves = lines // 128

    me = lax.axis_index("ctg")
    core = lax.rem(me, 2)
    chip = lax.div(me, 2)
    owner = core == 1
    partner = me + 1 - 2 * core
    my_chunk = lax.div(chip, groups)
    my_group = lax.rem(chip, groups)
    home_group = lax.div(me, members)
    home_row = lax.rem(me, members)
    my_pair = lax.div(my_chunk, 2)
    my_side = lax.rem(my_chunk, 2)
    my_rows = pl.ds(pl.multiple_of(my_group * ROWS, ROWS), ROWS)
    my_lanes = pl.ds(pl.multiple_of(my_chunk * width, 128), width)

    ahead = 1 - lax.div(my_pair, pairs // 2)

    def flip(place, length):
        return ahead * (length - 1 - place) + (1 - ahead) * place

    def skip(place, own, length):
        return place + lax.div(place + length - own, length)

    def far_pair(j):
        last = lax.div(j + 1, pairs)
        place = flip(skip(j, flip(my_pair, pairs), pairs), pairs)
        return last * my_pair + (1 - last) * place

    def near_pair(j):
        return far_pair(pairs - 1 - j)

    def far_chunk(j):
        second = lax.rem(j, 2)
        side = second * my_side + (1 - second) * (1 - my_side)
        return far_pair(lax.div(j, 2)) * 2 + side

    def sums_here(j):
        return (j >= EARLY) == owner

    def both_cores(c):
        return lax.div(c, 2) == my_pair

    def block_rows(g):
        return pl.ds(pl.multiple_of(g * ROWS, ROWS), ROWS)

    def tile_copy(j):
        c = far_chunk(j)
        return pltpu.make_async_copy(
            tiles.at[:, pl.ds(pl.multiple_of(c * width, 128), width)], masked.at[c], stat_send.at[j]
        )

    def staged(i):
        src, dst = (
            (pattern_hbm, pattern),
            (dual_hbm, dual_in),
            (demand_hbm, demand),
            (level_hbm, starts.at[0]),
            (cost_hbm, starts.at[1]),
            (ramp_hbm, starts.at[2]),
            (index_hbm, index),
            (table_hbm, table),
            (base_hbm, base_in),
            (floor_hbm.at[:, my_lanes], unit_rows.at[0]),
            (span_hbm.at[:, my_lanes], unit_rows.at[1]),
            (ramp_limit_hbm.at[:, my_lanes], unit_rows.at[2]),
            (ramp_mask_hbm.at[:, my_lanes], mask_row),
        )[i]
        return pltpu.make_async_copy(src, dst, core_sems.at[i - 3] if i in (6, 7, 8) else ext_send.at[i])

    for i in range(2):
        staged(i).start()
    tile_copy(0).start()

    barrier = pltpu.get_barrier_semaphore()

    @pl.loop(1, n)
    def _(d):
        pl.semaphore_signal(
            barrier, inc=1, device_id={"ctg": lax.rem(me + d, n)}, device_id_type=pl.DeviceIdType.MESH
        )

    for j in range(1, IN_FLIGHT):
        tile_copy(j).start()
    for i in range(2, 13):
        staged(i).start()

    omega[...] = jnp.ones_like(omega)
    price[...] = jnp.zeros_like(price)

    staged(0).wait()
    for k in range(ctgs):
        pattern_rows[k * halves:(k + 1) * halves, :] = pattern[k].astype(f32)
    for b in range(unit_count // 128):
        place = b * 128 % width
        gates[b * 128 // width, :, place:place + 128] = jnp.broadcast_to(
            pattern_rows[:, b:b + 1], (ctgs * halves, 128)
        )

    def frag_copy(c, target):
        return send(
            starts.at[:, :, pl.ds(pl.multiple_of(c * width, 128), width)],
            start_stage.at[home_row], frag_send.at[c], frag_recv.at[home_row], target,
        )

    def fin_copy(r, source_chunk, target):
        return send(
            frag_out.at[r], frag_in.at[source_chunk], frag_recv.at[r], frag_send.at[source_chunk], target
        )

    def stat_copy(slot, target_chip, sender_chip):
        return send(
            stats.at[slot, sender_chip], stats.at[slot, sender_chip],
            stat_send.at[target_chip], stat_recv.at[slot % 2, sender_chip], target_chip * 2 + 1,
        )

    def stat_start(slot):
        @pl.loop(1, chips)
        def _(d):
            stat_copy(slot, lax.rem(chip + d, chips), chip).start()

    def stat_wait(slot):
        @pl.loop(1, chips)
        def _(d):
            peer = lax.rem(chip + d, chips)
            stat_copy(slot, peer, chip).wait_send()
            stat_copy(slot, peer, peer).wait_recv()

    def flow_stat_copy(slot):
        return send(flow_stat.at[0], flow_stat.at[slot], core_sems.at[0], core_sems.at[1], partner)

    def omega_copy():
        return send(omega, omega, core_sems.at[2], core_sems.at[3], partner)

    def price_copy():
        return send(price, price, core_sems.at[4], core_sems.at[5], partner)

    def pair_copy(it, c):
        return send(pull_out.at[c], pair_in.at[it, c], pull_send.at[c * groups], pair_recv.at[c], partner)

    def pull_copy(it, src, target_chip, sender):
        c, g = lax.div(target_chip, groups), lax.rem(target_chip, groups)
        return send(
            src.at[c, block_rows(g)], pull_in.at[it, sender],
            pull_send.at[target_chip], pull_recv.at[sender], target_chip * 2 + 1,
        )

    def ext_copy(it, origin_chip, send_sem, target):
        c, g = lax.div(origin_chip, groups), lax.rem(origin_chip, groups)
        spot = ext_half.at[it, c, block_rows(g)]
        return send(spot, spot, send_sem, ext_recv.at[origin_chip], target)

    def ext_out(it, target):
        return ext_copy(it, chip, ext_send.at[target], target)

    def ext_pass(it, origin_chip):
        return ext_copy(it, origin_chip, ext_send.at[origin_chip * 2], partner)

    def halo_ext_copy(it, target):
        return send(extended.at[pl.ds(0, 8)], halo_ext.at[it], halo_sems.at[0], halo_sems.at[1], target)

    def halo_ramp_copy(it, target):
        return send(ramp.at[pl.ds(ROWS - 8, 8)], halo_ramp.at[it], halo_sems.at[2], halo_sems.at[3], target)

    def product(c):
        pull_out[c] = jnp.dot(dual_half[...], masked[c], preferred_element_type=f32).astype(bf16)

    def deliver(it, j):
        c = far_chunk(j)

        @pl.when((j < chunks // 2) & owner)
        def _():
            pair_copy(it, c).start()

        @pl.when(j >= chunks // 2)
        def _():
            for g in range(groups):
                target_chip = c * groups + g
                here = owner & (target_chip == chip)

                @pl.when(here)
                def _():
                    pull_in[it, me] = pull_out[c, g * ROWS:(g + 1) * ROWS, :]

                @pl.when(jnp.logical_not(here))
                def _():
                    pull_copy(it, pull_out, target_chip, me).start()

    def forward(it, j):
        @pl.when((j >= 0) & (j < chunks // 2) & jnp.logical_not(owner))
        def _():
            c = far_chunk(j)
            pair_copy(it, c).wait_recv()
            pull_sum[c] = (pull_out[c].astype(f32) + pair_in[it, c].astype(f32)).astype(bf16)
            for g in range(groups):
                pull_copy(it, pull_sum, c * groups + g, me).start()

    def pull_sent(it):
        @pl.loop(0, chunks)
        def _(j):
            c = far_chunk(j)
            paired = (j < chunks // 2) & owner

            @pl.when(paired)
            def _():
                pair_copy(it, c).wait_send()

            for g in range(groups):
                target_chip = c * groups + g
                here = owner & (target_chip == chip)

                @pl.when(jnp.logical_not(paired | here))
                def _():
                    pull_copy(it, pull_out, target_chip, me).wait_send()

    def mask(j):
        c = far_chunk(j)
        tile_copy(j).wait()

        @pl.when(j + IN_FLIGHT < chunks)
        def _():
            tile_copy(j + IN_FLIGHT).start()

        for r in range(ctgs * halves):
            gate = jnp.broadcast_to(gates[c, r:r + 1, :], (16, width)).astype(bf16)
            for q in range(8):
                where = slice(r * 128 + q * 16, r * 128 + q * 16 + 16)
                masked[c, where, :] = masked[c, where, :] * gate

    first_lag = 2

    @pl.loop(0, chunks + first_lag)
    def _(j):
        @pl.when(j < chunks)
        def _():
            mask(j)

        @pl.when(j == 0)
        def _():
            staged(1).wait()
            for k in range(ctgs):
                lanes = slice(k * lines, (k + 1) * lines)
                start_dual = dual_in[:, k, :]
                dual[:, lanes] = start_dual
                dual_half[:, lanes] = start_dual.astype(bf16)

        @pl.when(j < chunks)
        def _():
            product(far_chunk(j))

        @pl.when(j == 0)
        def _():
            for i in range(2, 6):
                staged(i).wait()
            for r in range(hour_rows):
                starts[3, r:r + 1] = jnp.broadcast_to(demand[0:1, r:r + 1], (1, unit_count))
            pl.semaphore_wait(barrier, n - 1)
            for c in range(chunks):
                target = (c * groups + home_group) * 2 + 1

                @pl.when(target != me)
                def _():
                    frag_copy(c, target).start()

                @pl.when(target == me)
                def _():
                    start_stage[home_row] = starts[:, :, c * width:(c + 1) * width]

        @pl.when(j < chunks)
        def _():
            deliver(0, j)

        forward(0, j - first_lag)

    for i in range(9, 13):
        staged(i).wait()

    block_row = lax.broadcasted_iota(jnp.int32, (ROWS, width), 0)
    lane_here = lax.broadcasted_iota(jnp.int32, (ROWS, 128), 1)
    row_here = lax.broadcasted_iota(jnp.int32, (ROWS, 128), 0) + my_group * ROWS
    diagonal = lane_here == row_here
    hour_lanes = lax.broadcasted_iota(jnp.int32, (1, 128), 1) < hours
    stat_row = lax.broadcasted_iota(jnp.int32, (4, 128), 0)

    def to_lanes(column):
        return jnp.sum(
            jnp.where(diagonal, jnp.broadcast_to(column, (ROWS, 128)), 0.0), axis=0, keepdims=True
        )

    def fold(x):
        rows, cols = x.shape
        out = None
        for r in range(0, rows, 8):
            for b in range(0, cols, 128):
                piece = x[r:r + 8, b:b + 128]
                out = piece if out is None else out + piece
        return jnp.sum(out, axis=0, keepdims=True)

    def halo_ramp_start(it):
        if groups > 1:
            @pl.when(my_group < groups - 1)
            def _():
                halo_ramp_copy(it, me + 2).start()

    @pl.when(owner)
    def _():
        for r in range(members):
            peer = my_group * members + r

            @pl.when(peer != me)
            def _():
                send(
                    starts.at[:, :, pl.ds(0, width)], start_stage.at[r],
                    frag_send.at[0], frag_recv.at[r], peer,
                ).wait_recv()

        demand_rows = []
        for r in range(members):
            rows = slice(r * hour_rows, (r + 1) * hour_rows)
            levels[rows, :] = start_stage[r, 0]
            cost[rows, :] = start_stage[r, 1]
            ramp[rows, :] = start_stage[r, 2]
            extended[rows, 0:128] = start_stage[r, 3, :, 0:128]
        lanes = to_lanes(extended[:, 0:1])
        mine = (stat_row == 0) & (jnp.full((4, 128), my_chunk) == 0)
        stats[0, chip] = jnp.where(mine, lanes, 0.0)
        stat_start(0)
        halo_ramp_start(0)

    for c in range(chunks):
        target = (c * groups + home_group) * 2 + 1

        @pl.when(target != me)
        def _():
            frag_copy(c, target).wait_send()

    def absorb(slot, sigma):
        total = stats[slot, 0]
        for q in range(1, chips):
            total = total + stats[slot, q]
        move = sigma * (balance * (total[0:1] - price[1:2]))
        move = jnp.where(hour_lanes, move, 0.0)
        price[0:1] = price[0:1] + move
        return total, jnp.sum(move * move, axis=1, keepdims=True)

    def primal(it):
        @pl.when(it > 0)
        def _():
            stat_wait(it)

        @pl.when(it > 0)
        def _():
            old = omega[0:1, 0:1]
            total, price_sq = absorb(it, step_size * old)
            sums = jnp.sum(total, axis=1, keepdims=True)
            dual_sq = sums[3:4] + sums[2:3] + price_sq
            ratio = (dual_sq + 1e-06) / (sums[1:2] + 1e-06)
            omega[...] = jnp.broadcast_to(jnp.sqrt(old) * jnp.sqrt(jnp.sqrt(ratio)), omega.shape)
            omega_copy().start()

        weight = omega[0:1, 0:1]
        tau = step_size / weight
        sigma = step_size * weight

        if groups > 1:
            @pl.when(my_group < groups - 1)
            def _():
                halo_ramp_copy(it, me + 2).wait_send()

            @pl.when(my_group > 0)
            def _():
                halo_ramp_copy(it, me - 2).wait_recv()

            @pl.when(my_group == 0)
            def _():
                halo_ramp[it] = jnp.zeros_like(halo_ramp[it])

            edge_ramp = halo_ramp[it][7:8]
        else:
            edge_ramp = jnp.zeros((1, width), f32)

        floor = unit_rows[0]
        ceiling = floor + unit_rows[1]
        ramp_limit = unit_rows[2]
        ramp_on = mask_row[...].astype(f32)
        ramp_now = ramp[...]
        before = jnp.where(block_row == 0, edge_ramp, pltpu.roll(ramp_now, 1, 0))
        price_here = jnp.sum(
            jnp.where(diagonal, jnp.broadcast_to(price[0:1], (ROWS, 128)), 0.0), axis=1, keepdims=True
        )
        known = cost[...] + ramp_on * (before - ramp_now) + balance * price_here

        first_near = lax.div(my_pair, pairs // 2) * (chips // 2)

        @pl.loop(0, chips)
        def _(q):
            pull_copy(it, pull_out, q, q * 2).wait_recv()

        @pl.loop(0, chips // 2)
        def _(q):
            @pl.when(first_near + q != chip)
            def _():
                pull_copy(it, pull_out, q, (first_near + q) * 2 + 1).wait_recv()

        pulled = pull_in[it, 0].astype(f32)
        for q in range(1, chips):
            pulled = pulled + pull_in[it, q * 2].astype(f32)
        for q in range(chips // 2):
            pulled = pulled + pull_in[it, (first_near + q) * 2 + 1].astype(f32)

        gradient = known + pulled
        old_levels = levels[...]
        moved = jnp.clip(old_levels - tau * gradient, floor, ceiling)
        ext = 2.0 * moved - old_levels
        levels[...] = moved
        ext_half[it, my_chunk, my_rows, :] = ext.astype(bf16)
        extended[...] = ext

        @pl.loop(0, chunks)
        def _(j):
            c = far_chunk(j)
            for g in range(groups):
                other = c * groups + g

                @pl.when(other != chip)
                def _():
                    ext_out(it, other * 2 + 1).start()

                @pl.when(both_cores(c))
                def _():
                    ext_out(it, other * 2).start()

        if groups > 1:
            @pl.when(my_group > 0)
            def _():
                halo_ext_copy(it, me - 2).start()
                halo_ext_copy(it, me - 2).wait_send()

            @pl.when(my_group < groups - 1)
            def _():
                halo_ext_copy(it, me + 2).wait_recv()

            @pl.when(my_group == groups - 1)
            def _():
                halo_ext[it] = jnp.zeros_like(halo_ext[it])

            edge_ext = halo_ext[it][0:1]
        else:
            edge_ext = jnp.zeros((1, width), f32)

        after = jnp.where(block_row == ROWS - 1, edge_ext, pltpu.roll(ext, ROWS - 1, 0))
        change = ramp_on * (after - ext)
        last_hour = block_row + my_group * ROWS == hours - 1
        change = jnp.where(last_hour, 0.0, change)
        trial = ramp_now + sigma * change
        ramp_new = trial - jnp.clip(trial, -sigma * ramp_limit, sigma * ramp_limit)
        ramp[...] = ramp_new

        row_sums = to_lanes(jnp.sum(ext, axis=1, keepdims=True))
        primal_sq = fold((moved - old_levels) ** 2)
        ramp_sq = fold((ramp_new - ramp_now) ** 2)
        stats[it + 1, chip] = jnp.where(
            stat_row == 0, row_sums,
            jnp.where(stat_row == 1, primal_sq, jnp.where(stat_row == 2, ramp_sq, 0.0)),
        )

        @pl.when(it == ITERS - 1)
        def _():
            stat_start(it + 1)
            for r in range(members):
                rows = slice(r * hour_rows, (r + 1) * hour_rows)
                frag_out[r, 0] = moved[rows, :]
                frag_out[r, 1] = ramp_new[rows, :]
            for r in range(members):
                target = my_group * members + r

                @pl.when(target != me)
                def _():
                    fin_copy(r, my_chunk, target).start()

                @pl.when(target == me)
                def _():
                    frag_in[my_chunk] = frag_out[r]

    def line_limits():
        for i in range(6, 9):
            staged(i).wait()

        row_iota = lax.broadcasted_iota(jnp.int32, (128, lines), 0)
        values = table[...].T
        part_a = values.astype(bf16)
        rest = values - part_a.astype(f32)
        part_b = rest.astype(bf16)
        part_c = (rest - part_b.astype(f32)).astype(bf16)
        for k in range(ctgs):
            which = index[k:k + 1, :]
            high = lax.shift_right_logical(which, 7)
            low = lax.bitwise_and(which, 127)
            blocks = table.shape[0] // 128
            got = jnp.zeros((128, lines), f32)
            for b in range(blocks):
                pick = jnp.where(row_iota + b * 128 == high, 1.0, 0.0).astype(bf16)
                for part in (part_a, part_b, part_c):
                    got = got + jnp.dot(part[:, b * 128:(b + 1) * 128], pick, preferred_element_type=f32)
            limit[:, k * lines:(k + 1) * lines] = jnp.sum(
                jnp.where(row_iota == low, got, 0.0), axis=0, keepdims=True
            )
            base[:, k * lines:(k + 1) * lines] = base_in[:, k, :]

    def take(it, c):
        for g in range(groups):
            other = c * groups + g

            @pl.when(jnp.logical_not(owner & (other == chip)))
            def _():
                ext_pass(it, other).wait_recv()

    def take_and_pass(it, c):
        take(it, c)

        @pl.when(owner & jnp.logical_not(both_cores(c)))
        def _():
            for g in range(groups):
                ext_pass(it, c * groups + g).start()

    def flow(x, w):
        return lax.dot_general(x, w, (((1,), (1,)), ((), ())), preferred_element_type=f32)

    def small_out(i):
        src, dst = ((price, out_price), (starts.at[0], out_levels), (starts.at[1], out_ramp))[i]
        return pltpu.make_async_copy(src, dst, pull_recv.at[i])

    def write_small():
        @pl.when(owner)
        def _():
            stat_wait(ITERS)
            absorb(ITERS, step_size * omega[0:1, 0:1])
            price_copy().start()

        for c in range(chunks):
            peer = (c * groups + home_group) * 2 + 1

            @pl.when(peer != me)
            def _():
                fin_copy(0, c, peer).wait_recv()

        for c in range(chunks):
            for which in range(2):
                starts[which, :, c * width:(c + 1) * width] = frag_in[c, which]
        small_out(1).start()
        small_out(2).start()

    @pl.loop(0, ITERS)
    def _(it):
        @pl.when(it > 0)
        def _():
            @pl.loop(0, chunks)
            def _(j):
                product(far_chunk(j))
                deliver(it, j)

                @pl.when((j == STAT) & owner)
                def _():
                    halo_ramp_start(it)
                    flow_stat_copy(it).wait_recv()
                    stats[it, chip, 3:4] = stats[it, chip, 3:4] + flow_stat[it, 0:1]
                    stat_start(it)

                forward(it, j - LAG)

            turn = (chunks - 1) // 2

            @pl.when(it < 3)
            def _():
                @pl.loop(0, turn * (ctgs * lines // 256))
                def _(i):
                    j = (it - 1) * turn + lax.div(i, ctgs * lines // 256)
                    block = pl.ds(pl.multiple_of(lax.rem(i, ctgs * lines // 256) * 256, 256), 256)
                    turned[j, :, block] = masked[far_chunk(j), block, :].T

        pull_sent(it)

        @pl.when(owner)
        def _():
            primal(it)

        take(it, my_chunk)
        flow_acc[...] = flow(ext_half[it, my_chunk], masked[my_chunk])

        @pl.when(it == 0)
        def _():
            line_limits()

        near = my_pair * 2 + 1 - my_side
        take(it, near)
        flow_acc[...] += flow(ext_half[it, near], masked[near])

        @pl.loop(1, pairs + AHEAD)
        def _(j):
            @pl.when(j < pairs)
            def _():
                c = near_pair(j) * 2
                take_and_pass(it, c)
                take_and_pass(it, c + 1)

            @pl.when((it == ITERS - 1) & (j == pairs))
            def _():
                write_small()

            @pl.when(j > AHEAD)
            def _():
                place = (pairs - 1 - j + AHEAD) * 2
                c, d = far_chunk(place), far_chunk(place + 1)
                x = jnp.concatenate([ext_half[it, c], ext_half[it, d]], axis=1)
                ready = (it > 1) | ((it == 1) & (place + 1 < (chunks - 1) // 2))

                @pl.when(ready)
                def _():
                    w = jnp.concatenate([turned[place], turned[place + 1]], axis=0)
                    flow_acc[...] += jnp.dot(x, w, preferred_element_type=f32)

                @pl.when(jnp.logical_not(ready))
                def _():
                    w = jnp.concatenate([masked[c], masked[d]], axis=1)
                    flow_acc[...] += flow(x, w)

        @pl.when(owner)
        def _():
            @pl.loop(0, chunks)
            def _(c):
                for g in range(groups):
                    other = c * groups + g

                    @pl.when(other != chip)
                    def _():
                        ext_out(it, other * 2 + 1).wait_send()

                    @pl.when(both_cores(c))
                    def _():
                        ext_out(it, other * 2).wait_send()

                    @pl.when(jnp.logical_not(both_cores(c)))
                    def _():
                        ext_pass(it, other).wait_send()

            @pl.when(it > 0)
            def _():
                omega_copy().wait_send()

        @pl.when((it == 0) & owner)
        def _():
            stat_wait(0)
            first = stats[0, 0]
            for q in range(1, chips):
                first = first + stats[0, q]
            price[1:2] = first[0:1]

        @pl.when((it > 0) & jnp.logical_not(owner))
        def _():
            omega_copy().wait_recv()

        @pl.when(it == ITERS - 1)
        def _():
            @pl.when(jnp.logical_not(owner))
            def _():
                price_copy().wait_recv()

            small_out(0).start()

        sigma = step_size * omega[0:1, 0:1]
        old_dual = dual[...]
        trial = old_dual + sigma * flow_acc[...]
        bound = limit[...]
        dual_new = trial - jnp.clip(trial, sigma * (base[...] - bound), sigma * (base[...] + bound))
        dual[...] = dual_new
        dual_half[...] = dual_new.astype(bf16)

        @pl.when(it < ITERS - 1)
        def _():
            flow_sq = fold((dual_new - old_dual) ** 2)

            @pl.when(owner)
            def _():
                stats[it + 1, chip, 3:4] = flow_sq

            @pl.when(jnp.logical_not(owner))
            def _():
                @pl.when(it > 0)
                def _():
                    flow_stat_copy(it).wait_send()

                flow_stat[0] = jnp.broadcast_to(flow_sq, (8, 128))
                flow_stat_copy(it + 1).start()

    dual_out = pltpu.make_async_copy(dual, out_dual, ext_send.at[0])
    dual_out.start()

    @pl.when(owner)
    def _():
        for r in range(members):
            target = my_group * members + r

            @pl.when(target != me)
            def _():
                fin_copy(r, my_chunk, target).wait_send()

        price_copy().wait_send()

    @pl.when(jnp.logical_not(owner))
    def _():
        flow_stat_copy(0).wait_send()

    for i in range(3):
        small_out(i).wait()
    dual_out.wait()


def finish(
    levels, dual, ramp, price, out_levels, out_dual, out_ramp, out_price,
    level_box, dual_box, tile_box, ramp_box, price_box, own_price, in_sem, out_sem,
):
    hours, ctgs, lines = out_dual.shape
    hour_rows = own_price.shape[1]
    pieces = hours // 8

    def dual_in(p):
        return pltpu.make_async_copy(dual.at[p * 8:p * 8 + 8], dual_box.at[p], in_sem.at[3 + p])

    def dual_out(p):
        return pltpu.make_async_copy(tile_box.at[p], out_dual.at[p * 8:p * 8 + 8], out_sem.at[3 + p])

    small_in = (
        pltpu.make_async_copy(price, price_box, in_sem.at[0]),
        pltpu.make_async_copy(levels, level_box, in_sem.at[1]),
        pltpu.make_async_copy(ramp, ramp_box, in_sem.at[2]),
    )
    small_out = (
        pltpu.make_async_copy(own_price, out_price, out_sem.at[0]),
        pltpu.make_async_copy(level_box, out_levels, out_sem.at[1]),
        pltpu.make_async_copy(ramp_box, out_ramp, out_sem.at[2]),
    )
    for p in range(pieces):
        dual_in(p).start()
    for copy in small_in:
        copy.start()
    for p in range(pieces):
        dual_in(p).wait()
        for k in range(ctgs):
            tile_box[p, :, k, :] = dual_box[p, :, k * lines:(k + 1) * lines]
        dual_out(p).start()
    small_in[0].wait()
    lane = lax.broadcasted_iota(jnp.int32, (1, 128), 1) - lax.axis_index("ctg") * hour_rows
    for r in range(hour_rows):
        own_price[0:1, r:r + 1] = jnp.sum(
            jnp.where(lane == r, price_box[0:1], 0.0), axis=1, keepdims=True
        )
    small_out[0].start()
    for i in (1, 2):
        small_in[i].wait()
        small_out[i].start()
    for p in range(pieces):
        dual_out(p).wait()
    for copy in small_out:
        copy.wait()


def body(
    flow_tiles,
    tile_pattern,
    monitored,
    ratings,
    base_flow,
    unit_cost,
    unit_floor,
    unit_span,
    ramp_limit,
    ramp_mask,
    demand,
    start_output,
    start_flow_dual,
    start_ramp_dual,
):
    f32, bf16 = jnp.float32, jnp.bfloat16
    ctgs, lines, unit_count = flow_tiles.shape
    n = lax.axis_size("ctg")
    hour_rows = start_output.shape[0]
    hours = hour_rows * n
    groups = hours // ROWS
    chips = n // 2
    chunks = chips // groups
    members = ROWS // hour_rows
    width = unit_count // chunks
    flat = ctgs * lines
    step_size = 0.5 / (2.0 + math.sqrt(ctgs * n * lines / unit_count))
    balance = 1.0 / math.sqrt(unit_count)

    gate_rows = ctgs * tile_pattern.shape[1]

    vmem = pl.BlockSpec(memory_space=pltpu.VMEM)
    hbm = pl.BlockSpec(memory_space=pl.ANY)
    sem = pltpu.SemaphoreType.DMA
    out = pl.pallas_call(
        functools.partial(kernel, n, hour_rows, step_size, balance),
        out_shape=(
            jax.ShapeDtypeStruct((hour_rows, unit_count), f32),
            jax.ShapeDtypeStruct((hours, flat), f32),
            jax.ShapeDtypeStruct((hour_rows, unit_count), f32),
            jax.ShapeDtypeStruct((8, 128), f32),
        ),
        in_specs=[hbm] * 14,
        out_specs=(hbm,) * 4,
        scratch_shapes=[
            pltpu.VMEM((chunks, flat, width), bf16),
            pltpu.VMEM((chunks - 2, width, flat), bf16),
            pltpu.VMEM((chunks, gate_rows, width), f32),
            pltpu.VMEM(tile_pattern.shape, jnp.int32),
            pltpu.VMEM((gate_rows, tile_pattern.shape[2]), f32),
            pltpu.VMEM(monitored.shape, jnp.int32),
            pltpu.VMEM((ratings.shape[0] // 128, 128), f32),
            pltpu.VMEM(base_flow.shape, f32),
            pltpu.VMEM(start_flow_dual.shape, f32),
            pltpu.VMEM((3, 1, width), f32),
            pltpu.VMEM((1, width), jnp.int32),
            pltpu.VMEM((1, hour_rows), f32),
            pltpu.VMEM((hours, flat), f32),
            pltpu.VMEM((hours, flat), f32),
            pltpu.VMEM((4, hour_rows, unit_count), f32),
            pltpu.VMEM((1, flat), f32),
            pltpu.VMEM((hours, flat), bf16),
            pltpu.VMEM((hours, flat), f32),
            pltpu.VMEM((members, 4, hour_rows, width), f32),
            pltpu.VMEM((chunks, 2, hour_rows, width), f32),
            pltpu.VMEM((members, 2, hour_rows, width), f32),
            pltpu.VMEM((ROWS, width), f32),
            pltpu.VMEM((ROWS, width), f32),
            pltpu.VMEM((ROWS, width), f32),
            pltpu.VMEM((ROWS, width), f32),
            pltpu.VMEM((ITERS, 8, width), f32),
            pltpu.VMEM((ITERS, 8, width), f32),
            pltpu.VMEM((chunks, hours, width), bf16),
            pltpu.VMEM((ITERS, chunks, hours, width), bf16),
            pltpu.VMEM((chunks, hours, width), bf16),
            pltpu.VMEM((ITERS, n, ROWS, width), bf16),
            pltpu.VMEM((ITERS, chunks, hours, width), bf16),
            pltpu.VMEM((ITERS + 1, chips, 4, 128), f32),
            pltpu.VMEM((ITERS, 8, 128), f32),
            pltpu.VMEM((8, 128), f32),
            pltpu.VMEM((8, 128), f32),
            sem((chunks,)), sem((members,)), sem((chunks,)), sem((chips,)), sem((n,)),
            sem((n,)), sem((chips,)), sem((max(chips, chunks),)), sem((2, chips)),
            sem((6,)), sem((4,)),
        ],
        compiler_params=pltpu.CompilerParams(collective_id=0, has_side_effects=True),
    )(
        flow_tiles.reshape(flat, unit_count),
        tile_pattern,
        monitored,
        ratings.reshape(-1, 128),
        base_flow,
        start_flow_dual,
        start_output,
        unit_cost,
        start_ramp_dual,
        demand[None],
        unit_floor[None],
        unit_span[None],
        ramp_limit[None],
        ramp_mask[None],
    )
    levels, dual, ramp, price = pl.pallas_call(
        finish,
        out_shape=(
            jax.ShapeDtypeStruct((hour_rows, unit_count), f32),
            jax.ShapeDtypeStruct((hours, ctgs, lines), f32),
            jax.ShapeDtypeStruct((hour_rows, unit_count), f32),
            jax.ShapeDtypeStruct((1, hour_rows), f32),
        ),
        in_specs=[hbm] * 4,
        out_specs=(hbm,) * 4,
        scratch_shapes=[
            pltpu.VMEM((hour_rows, unit_count), f32),
            pltpu.VMEM((hours // 8, 8, flat), f32),
            pltpu.VMEM((hours // 8, 8, ctgs, lines), f32),
            pltpu.VMEM((hour_rows, unit_count), f32),
            pltpu.VMEM((8, 128), f32),
            pltpu.VMEM((1, hour_rows), f32),
            sem((3 + hours // 8,)),
            sem((3 + hours // 8,)),
        ],
    )(*out)
    return levels, dual, ramp, price.reshape(hour_rows)


def solution(mesh):
    return jax.shard_map(
        body,
        mesh=mesh,
        in_specs=(
            P("ctg", None, None),
            P("ctg", None, None),
            P("ctg", None),
            P(),
            P("grp", "ctg", None),
            P(("grp", "ctg"), None),
            P(),
            P(),
            P(),
            P(),
            P(("grp", "ctg")),
            P(("grp", "ctg"), None),
            P("grp", "ctg", None),
            P(("grp", "ctg"), None),
        ),
        out_specs=(
            P(("grp", "ctg"), None),
            P("grp", "ctg", None),
            P(("grp", "ctg"), None),
            P(("grp", "ctg")),
        ),
        check_vma=False,
    )
```

```python
import functools
import math

import jax
import jax.numpy as jnp
from jax import lax
from jax.experimental import pallas as pl
from jax.experimental.pallas import tpu as pltpu
from jax.sharding import PartitionSpec as P

ITERS = 4
ROWS = 32
STAT = 5
LAG = 0
AHEAD = 1
IN_FLIGHT = 3


def send(src, dst, send_sem, recv_sem, target):
    return pltpu.make_async_remote_copy(
        src_ref=src,
        dst_ref=dst,
        send_sem=send_sem,
        recv_sem=recv_sem,
        device_id={"ctg": target},
        device_id_type=pl.DeviceIdType.MESH,
    )


def kernel(
    n, hour_rows, step_size, balance,
    tiles, pattern_hbm, index_hbm, table_hbm, base_hbm, dual_hbm, level_hbm, cost_hbm, ramp_hbm, demand_hbm,
    floor_hbm, span_hbm, ramp_limit_hbm, ramp_mask_hbm,
    out_levels, out_dual, out_ramp, out_price,
    masked, turned, gates, pattern, pattern_rows, index, table, base_in, dual_in, unit_rows, mask_row, demand,
    dual, base, starts, limit, dual_half, flow_acc,
    start_stage, frag_in, frag_out,
    cost, levels, ramp, extended, halo_ext, halo_ramp,
    pull_out, pair_in, pull_sum, pull_in, ext_half, stats, flow_stat, price, omega,
    frag_send, frag_recv, pull_send, pull_recv, ext_send, ext_recv, stat_send, stat_recv,
    core_sems, halo_sems,
):
    f32 = jnp.float32
    bf16 = jnp.bfloat16
    chips = n // 2
    members = ROWS // hour_rows
    groups = n // members
    chunks = chips // groups
    unit_count = tiles.shape[1]
    width = unit_count // chunks
    ctgs, lines = base_in.shape[1], base_in.shape[2]
    hours = groups * ROWS
    pairs = chunks // 2
    halves = lines // 128

    me = lax.axis_index("ctg")
    core = lax.rem(me, 2)
    chip = lax.div(me, 2)
    owner = core == 1
    partner = me + 1 - 2 * core
    my_chunk = lax.div(chip, groups)
    my_group = lax.rem(chip, groups)
    home_group = lax.div(me, members)
    home_row = lax.rem(me, members)
    my_pair = lax.div(my_chunk, 2)
    my_side = lax.rem(my_chunk, 2)
    my_rows = pl.ds(pl.multiple_of(my_group * ROWS, ROWS), ROWS)
    my_lanes = pl.ds(pl.multiple_of(my_chunk * width, 128), width)

    ahead = 1 - lax.div(my_pair, pairs // 2)

    def flip(place, length):
        return ahead * (length - 1 - place) + (1 - ahead) * place

    def skip(place, own, length):
        return place + lax.div(place + length - own, length)

    def far_pair(j):
        last = lax.div(j + 1, pairs)
        place = flip(skip(j, flip(my_pair, pairs), pairs), pairs)
        return last * my_pair + (1 - last) * place

    def near_pair(j):
        return far_pair(pairs - 1 - j)

    def far_chunk(j):
        second = lax.rem(j, 2)
        side = second * my_side + (1 - second) * (1 - my_side)
        return far_pair(lax.div(j, 2)) * 2 + side

    def sums_here(j):
        return (j >= EARLY) == owner

    def both_cores(c):
        return c == my_chunk

    def block_rows(g):
        return pl.ds(pl.multiple_of(g * ROWS, ROWS), ROWS)

    def tile_copy(j):
        c = far_chunk(j)
        return pltpu.make_async_copy(
            tiles.at[:, pl.ds(pl.multiple_of(c * width, 128), width)], masked.at[c], stat_send.at[j]
        )

    def staged(i):
        src, dst = (
            (pattern_hbm, pattern),
            (dual_hbm, dual_in),
            (demand_hbm, demand),
            (level_hbm, starts.at[0]),
            (cost_hbm, starts.at[1]),
            (ramp_hbm, starts.at[2]),
            (index_hbm, index),
            (table_hbm, table),
            (base_hbm, base_in),
            (floor_hbm.at[:, my_lanes], unit_rows.at[0]),
            (span_hbm.at[:, my_lanes], unit_rows.at[1]),
            (ramp_limit_hbm.at[:, my_lanes], unit_rows.at[2]),
            (ramp_mask_hbm.at[:, my_lanes], mask_row),
        )[i]
        return pltpu.make_async_copy(src, dst, core_sems.at[i - 3] if i in (6, 7, 8) else ext_send.at[i])

    for i in range(2):
        staged(i).start()
    tile_copy(0).start()

    barrier = pltpu.get_barrier_semaphore()

    @pl.loop(1, n)
    def _(d):
        pl.semaphore_signal(
            barrier, inc=1, device_id={"ctg": lax.rem(me + d, n)}, device_id_type=pl.DeviceIdType.MESH
        )

    for j in range(1, IN_FLIGHT):
        tile_copy(j).start()
    for i in range(2, 13):
        staged(i).start()

    omega[...] = jnp.ones_like(omega)
    price[...] = jnp.zeros_like(price)

    staged(0).wait()
    for k in range(ctgs):
        pattern_rows[k * halves:(k + 1) * halves, :] = pattern[k].astype(f32)
    for b in range(unit_count // 128):
        place = b * 128 % width
        gates[b * 128 // width, :, place:place + 128] = jnp.broadcast_to(
            pattern_rows[:, b:b + 1], (ctgs * halves, 128)
        )

    def frag_copy(c, target):
        return send(
            starts.at[:, :, pl.ds(pl.multiple_of(c * width, 128), width)],
            start_stage.at[home_row], frag_send.at[c], frag_recv.at[home_row], target,
        )

    def fin_copy(r, source_chunk, target):
        return send(
            frag_out.at[r], frag_in.at[source_chunk], frag_recv.at[r], frag_send.at[source_chunk], target
        )

    def stat_copy(slot, target_chip, sender_chip):
        return send(
            stats.at[slot, sender_chip], stats.at[slot, sender_chip],
            stat_send.at[target_chip], stat_recv.at[slot % 2, sender_chip], target_chip * 2 + 1,
        )

    def stat_start(slot):
        @pl.loop(1, chips)
        def _(d):
            stat_copy(slot, lax.rem(chip + d, chips), chip).start()

    def stat_wait(slot):
        @pl.loop(1, chips)
        def _(d):
            peer = lax.rem(chip + d, chips)
            stat_copy(slot, peer, chip).wait_send()
            stat_copy(slot, peer, peer).wait_recv()

    def flow_stat_copy(slot):
        return send(flow_stat.at[0], flow_stat.at[slot], core_sems.at[0], core_sems.at[1], partner)

    def omega_copy():
        return send(omega, omega, core_sems.at[2], core_sems.at[3], partner)

    def price_copy():
        return send(price, price, core_sems.at[4], core_sems.at[5], partner)

    def pair_copy(it, c):
        return send(pull_out.at[c], pair_in.at[it, c], pull_send.at[c * groups], pull_recv.at[c], partner)

    def pull_copy(it, src, target_chip, sender):
        c, g = lax.div(target_chip, groups), lax.rem(target_chip, groups)
        return send(
            src.at[c, block_rows(g)], pull_in.at[it, sender],
            pull_send.at[target_chip], pull_recv.at[sender], target_chip * 2 + 1,
        )

    def ext_copy(it, origin_chip, send_sem, target):
        c, g = lax.div(origin_chip, groups), lax.rem(origin_chip, groups)
        spot = ext_half.at[it, c, block_rows(g)]
        return send(spot, spot, send_sem, ext_recv.at[origin_chip], target)

    def ext_out(it, target):
        return ext_copy(it, chip, ext_send.at[target], target)

    def ext_pass(it, origin_chip):
        return ext_copy(it, origin_chip, ext_send.at[origin_chip * 2], partner)

    def halo_ext_copy(it, target):
        return send(extended.at[pl.ds(0, 8)], halo_ext.at[it], halo_sems.at[0], halo_sems.at[1], target)

    def halo_ramp_copy(it, target):
        return send(ramp.at[pl.ds(ROWS - 8, 8)], halo_ramp.at[it], halo_sems.at[2], halo_sems.at[3], target)

    def product(c):
        pull_out[c] = jnp.dot(dual_half[...], masked[c], preferred_element_type=f32).astype(bf16)

    def deliver(it, j):
        c = far_chunk(j)

        @pl.when((j < chunks // 2) & owner)
        def _():
            pair_copy(it, c).start()

        @pl.when(j >= chunks // 2)
        def _():
            for g in range(groups):
                target_chip = c * groups + g
                here = owner & (target_chip == chip)

                @pl.when(here)
                def _():
                    pull_in[it, me] = pull_out[c, g * ROWS:(g + 1) * ROWS, :]

                @pl.when(jnp.logical_not(here))
                def _():
                    pull_copy(it, pull_out, target_chip, me).start()

    def forward(it, j):
        @pl.when((j >= 0) & (j < chunks // 2) & jnp.logical_not(owner))
        def _():
            c = far_chunk(j)
            pair_copy(it, c).wait_recv()
            pull_sum[c] = (pull_out[c].astype(f32) + pair_in[it, c].astype(f32)).astype(bf16)
            for g in range(groups):
                pull_copy(it, pull_sum, c * groups + g, me).start()

    def pull_sent(it):
        @pl.loop(0, chunks)
        def _(j):
            c = far_chunk(j)
            paired = (j < chunks // 2) & owner

            @pl.when(paired)
            def _():
                pair_copy(it, c).wait_send()

            for g in range(groups):
                target_chip = c * groups + g
                here = owner & (target_chip == chip)

                @pl.when(jnp.logical_not(paired | here))
                def _():
                    pull_copy(it, pull_out, target_chip, me).wait_send()

    def mask(j):
        c = far_chunk(j)
        tile_copy(j).wait()

        @pl.when(j + IN_FLIGHT < chunks)
        def _():
            tile_copy(j + IN_FLIGHT).start()

        for r in range(ctgs * halves):
            gate = jnp.broadcast_to(gates[c, r:r + 1, :], (16, width)).astype(bf16)
            for q in range(8):
                where = slice(r * 128 + q * 16, r * 128 + q * 16 + 16)
                masked[c, where, :] = masked[c, where, :] * gate

    first_lag = 2

    @pl.loop(0, chunks + first_lag)
    def _(j):
        @pl.when(j < chunks)
        def _():
            mask(j)

        @pl.when(j == 0)
        def _():
            staged(1).wait()
            for k in range(ctgs):
                lanes = slice(k * lines, (k + 1) * lines)
                start_dual = dual_in[:, k, :]
                dual[:, lanes] = start_dual
                dual_half[:, lanes] = start_dual.astype(bf16)

        @pl.when(j < chunks)
        def _():
            product(far_chunk(j))

        @pl.when(j == 0)
        def _():
            for i in range(2, 6):
                staged(i).wait()
            for r in range(hour_rows):
                starts[3, r:r + 1] = jnp.broadcast_to(demand[0:1, r:r + 1], (1, unit_count))
            pl.semaphore_wait(barrier, n - 1)
            for c in range(chunks):
                target = (c * groups + home_group) * 2 + 1

                @pl.when(target != me)
                def _():
                    frag_copy(c, target).start()

                @pl.when(target == me)
                def _():
                    start_stage[home_row] = starts[:, :, c * width:(c + 1) * width]

        @pl.when(j < chunks)
        def _():
            deliver(0, j)

        forward(0, j - first_lag)

    for i in range(9, 13):
        staged(i).wait()

    block_row = lax.broadcasted_iota(jnp.int32, (ROWS, width), 0)
    lane_here = lax.broadcasted_iota(jnp.int32, (ROWS, 128), 1)
    row_here = lax.broadcasted_iota(jnp.int32, (ROWS, 128), 0) + my_group * ROWS
    diagonal = lane_here == row_here
    hour_lanes = lax.broadcasted_iota(jnp.int32, (1, 128), 1) < hours
    stat_row = lax.broadcasted_iota(jnp.int32, (4, 128), 0)

    def to_lanes(column):
        return jnp.sum(
            jnp.where(diagonal, jnp.broadcast_to(column, (ROWS, 128)), 0.0), axis=0, keepdims=True
        )

    def fold(x):
        rows, cols = x.shape
        out = None
        for r in range(0, rows, 8):
            for b in range(0, cols, 128):
                piece = x[r:r + 8, b:b + 128]
                out = piece if out is None else out + piece
        return jnp.sum(out, axis=0, keepdims=True)

    def halo_ramp_start(it):
        if groups > 1:
            @pl.when(my_group < groups - 1)
            def _():
                halo_ramp_copy(it, me + 2).start()

    @pl.when(owner)
    def _():
        for r in range(members):
            peer = my_group * members + r

            @pl.when(peer != me)
            def _():
                send(
                    starts.at[:, :, pl.ds(0, width)], start_stage.at[r],
                    frag_send.at[0], frag_recv.at[r], peer,
                ).wait_recv()

        demand_rows = []
        for r in range(members):
            rows = slice(r * hour_rows, (r + 1) * hour_rows)
            levels[rows, :] = start_stage[r, 0]
            cost[rows, :] = start_stage[r, 1]
            ramp[rows, :] = start_stage[r, 2]
            extended[rows, 0:128] = start_stage[r, 3, :, 0:128]
        lanes = to_lanes(extended[:, 0:1])
        mine = (stat_row == 0) & (jnp.full((4, 128), my_chunk) == 0)
        stats[0, chip] = jnp.where(mine, lanes, 0.0)
        stat_start(0)
        halo_ramp_start(0)

    for c in range(chunks):
        target = (c * groups + home_group) * 2 + 1

        @pl.when(target != me)
        def _():
            frag_copy(c, target).wait_send()

    def absorb(slot, sigma):
        total = stats[slot, 0]
        for q in range(1, chips):
            total = total + stats[slot, q]
        move = sigma * (balance * (total[0:1] - price[1:2]))
        move = jnp.where(hour_lanes, move, 0.0)
        price[0:1] = price[0:1] + move
        return total, jnp.sum(move * move, axis=1, keepdims=True)

    def primal(it):
        @pl.when(it > 0)
        def _():
            stat_wait(it)

        @pl.when(it > 0)
        def _():
            old = omega[0:1, 0:1]
            total, price_sq = absorb(it, step_size * old)
            sums = jnp.sum(total, axis=1, keepdims=True)
            dual_sq = sums[3:4] + sums[2:3] + price_sq
            ratio = (dual_sq + 1e-06) / (sums[1:2] + 1e-06)
            omega[...] = jnp.broadcast_to(jnp.sqrt(old) * jnp.sqrt(jnp.sqrt(ratio)), omega.shape)
            omega_copy().start()

        weight = omega[0:1, 0:1]
        tau = step_size / weight
        sigma = step_size * weight

        if groups > 1:
            @pl.when(my_group < groups - 1)
            def _():
                halo_ramp_copy(it, me + 2).wait_send()

            @pl.when(my_group > 0)
            def _():
                halo_ramp_copy(it, me - 2).wait_recv()

            @pl.when(my_group == 0)
            def _():
                halo_ramp[it] = jnp.zeros_like(halo_ramp[it])

            edge_ramp = halo_ramp[it][7:8]
        else:
            edge_ramp = jnp.zeros((1, width), f32)

        floor = unit_rows[0]
        ceiling = floor + unit_rows[1]
        ramp_limit = unit_rows[2]
        ramp_on = mask_row[...].astype(f32)
        ramp_now = ramp[...]
        before = jnp.where(block_row == 0, edge_ramp, pltpu.roll(ramp_now, 1, 0))
        price_here = jnp.sum(
            jnp.where(diagonal, jnp.broadcast_to(price[0:1], (ROWS, 128)), 0.0), axis=1, keepdims=True
        )
        known = cost[...] + ramp_on * (before - ramp_now) + balance * price_here

        first_near = lax.div(my_pair, pairs // 2) * (chips // 2)

        @pl.loop(0, chips)
        def _(q):
            pull_copy(it, pull_out, q, q * 2).wait_recv()

        @pl.loop(0, chips // 2)
        def _(q):
            @pl.when(first_near + q != chip)
            def _():
                pull_copy(it, pull_out, q, (first_near + q) * 2 + 1).wait_recv()

        pulled = pull_in[it, 0].astype(f32)
        for q in range(1, chips):
            pulled = pulled + pull_in[it, q * 2].astype(f32)
        for q in range(chips // 2):
            pulled = pulled + pull_in[it, (first_near + q) * 2 + 1].astype(f32)

        gradient = known + pulled
        old_levels = levels[...]
        moved = jnp.clip(old_levels - tau * gradient, floor, ceiling)
        ext = 2.0 * moved - old_levels
        levels[...] = moved
        ext_half[it, my_chunk, my_rows, :] = ext.astype(bf16)
        extended[...] = ext

        @pl.loop(0, chunks)
        def _(j):
            c = far_chunk(j)
            for g in range(groups):
                other = c * groups + g

                @pl.when(other != chip)
                def _():
                    ext_out(it, other * 2 + 1).start()

                @pl.when(both_cores(c))
                def _():
                    ext_out(it, other * 2).start()

        if groups > 1:
            @pl.when(my_group > 0)
            def _():
                halo_ext_copy(it, me - 2).start()
                halo_ext_copy(it, me - 2).wait_send()

            @pl.when(my_group < groups - 1)
            def _():
                halo_ext_copy(it, me + 2).wait_recv()

            @pl.when(my_group == groups - 1)
            def _():
                halo_ext[it] = jnp.zeros_like(halo_ext[it])

            edge_ext = halo_ext[it][0:1]
        else:
            edge_ext = jnp.zeros((1, width), f32)

        after = jnp.where(block_row == ROWS - 1, edge_ext, pltpu.roll(ext, ROWS - 1, 0))
        change = ramp_on * (after - ext)
        last_hour = block_row + my_group * ROWS == hours - 1
        change = jnp.where(last_hour, 0.0, change)
        trial = ramp_now + sigma * change
        ramp_new = trial - jnp.clip(trial, -sigma * ramp_limit, sigma * ramp_limit)
        ramp[...] = ramp_new

        row_sums = to_lanes(jnp.sum(ext, axis=1, keepdims=True))
        primal_sq = fold((moved - old_levels) ** 2)
        ramp_sq = fold((ramp_new - ramp_now) ** 2)
        stats[it + 1, chip] = jnp.where(
            stat_row == 0, row_sums,
            jnp.where(stat_row == 1, primal_sq, jnp.where(stat_row == 2, ramp_sq, 0.0)),
        )

        @pl.when(it == ITERS - 1)
        def _():
            stat_start(it + 1)
            for r in range(members):
                rows = slice(r * hour_rows, (r + 1) * hour_rows)
                frag_out[r, 0] = moved[rows, :]
                frag_out[r, 1] = ramp_new[rows, :]
            for r in range(members):
                target = my_group * members + r

                @pl.when(target != me)
                def _():
                    fin_copy(r, my_chunk, target).start()

                @pl.when(target == me)
                def _():
                    frag_in[my_chunk] = frag_out[r]

    def line_limits():
        for i in range(6, 9):
            staged(i).wait()

        row_iota = lax.broadcasted_iota(jnp.int32, (128, lines), 0)
        values = table[...].T
        part_a = values.astype(bf16)
        rest = values - part_a.astype(f32)
        part_b = rest.astype(bf16)
        part_c = (rest - part_b.astype(f32)).astype(bf16)
        for k in range(ctgs):
            which = index[k:k + 1, :]
            high = lax.shift_right_logical(which, 7)
            low = lax.bitwise_and(which, 127)
            blocks = table.shape[0] // 128
            got = jnp.zeros((128, lines), f32)
            for b in range(blocks):
                pick = jnp.where(row_iota + b * 128 == high, 1.0, 0.0).astype(bf16)
                for part in (part_a, part_b, part_c):
                    got = got + jnp.dot(part[:, b * 128:(b + 1) * 128], pick, preferred_element_type=f32)
            limit[:, k * lines:(k + 1) * lines] = jnp.sum(
                jnp.where(row_iota == low, got, 0.0), axis=0, keepdims=True
            )
            base[:, k * lines:(k + 1) * lines] = base_in[:, k, :]

    def take(it, c):
        for g in range(groups):
            other = c * groups + g

            @pl.when(jnp.logical_not(owner & (other == chip)))
            def _():
                ext_pass(it, other).wait_recv()

    def take_and_pass(it, c):
        take(it, c)

        @pl.when(owner & jnp.logical_not(both_cores(c)))
        def _():
            for g in range(groups):
                ext_pass(it, c * groups + g).start()

    def flow(x, w):
        return lax.dot_general(x, w, (((1,), (1,)), ((), ())), preferred_element_type=f32)

    def small_out(i):
        src, dst = ((price, out_price), (starts.at[0], out_levels), (starts.at[1], out_ramp))[i]
        return pltpu.make_async_copy(src, dst, pull_recv.at[i])

    def write_small():
        @pl.when(owner)
        def _():
            stat_wait(ITERS)
            absorb(ITERS, step_size * omega[0:1, 0:1])
            price_copy().start()

        for c in range(chunks):
            peer = (c * groups + home_group) * 2 + 1

            @pl.when(peer != me)
            def _():
                fin_copy(0, c, peer).wait_recv()

        for c in range(chunks):
            for which in range(2):
                starts[which, :, c * width:(c + 1) * width] = frag_in[c, which]
        small_out(1).start()
        small_out(2).start()

    turns = (chunks - 1) // 2
    blocks = ctgs * lines // 256

    def turn(first, last):
        @pl.loop(first * blocks, last * blocks)
        def _(i):
            j = lax.div(i, blocks)
            block = pl.ds(pl.multiple_of(lax.rem(i, blocks) * 256, 256), 256)
            turned[j, :, block] = masked[far_chunk(j), block, :].T

    @pl.loop(0, ITERS)
    def _(it):
        @pl.when(it > 0)
        def _():
            @pl.loop(0, chunks)
            def _(j):
                product(far_chunk(j))
                deliver(it, j)

                @pl.when((j == STAT) & owner)
                def _():
                    halo_ramp_start(it)
                    flow_stat_copy(it).wait_recv()
                    stats[it, chip, 3:4] = stats[it, chip, 3:4] + flow_stat[it, 0:1]
                    stat_start(it)

                forward(it, j - LAG)

            @pl.when(it < 3)
            def _():
                turn((it - 1) * turns, (it - 1) * turns + turns - 1)

        pull_sent(it)

        @pl.when(owner)
        def _():
            primal(it)

        take(it, my_chunk)
        flow_acc[...] = flow(ext_half[it, my_chunk], masked[my_chunk])

        @pl.when(it == 0)
        def _():
            line_limits()

        @pl.when((it > 0) & (it < 3))
        def _():
            turn(it * turns - 1, it * turns)

        near = my_pair * 2 + 1 - my_side
        take_and_pass(it, near)
        flow_acc[...] += flow(ext_half[it, near], masked[near])

        @pl.loop(1, pairs + AHEAD)
        def _(j):
            @pl.when(j < pairs)
            def _():
                c = near_pair(j) * 2
                take_and_pass(it, c)
                take_and_pass(it, c + 1)

            @pl.when((it == ITERS - 1) & (j == pairs))
            def _():
                write_small()

            @pl.when(j > AHEAD)
            def _():
                place = (pairs - 1 - j + AHEAD) * 2
                c, d = far_chunk(place), far_chunk(place + 1)
                x = jnp.concatenate([ext_half[it, c], ext_half[it, d]], axis=1)
                ready = (it > 1) | ((it == 1) & (place + 1 < (chunks - 1) // 2))

                @pl.when(ready)
                def _():
                    w = jnp.concatenate([turned[place], turned[place + 1]], axis=0)
                    flow_acc[...] += jnp.dot(x, w, preferred_element_type=f32)

                @pl.when(jnp.logical_not(ready))
                def _():
                    w = jnp.concatenate([masked[c], masked[d]], axis=1)
                    flow_acc[...] += flow(x, w)

        @pl.when(owner)
        def _():
            @pl.loop(0, chunks)
            def _(c):
                for g in range(groups):
                    other = c * groups + g

                    @pl.when(other != chip)
                    def _():
                        ext_out(it, other * 2 + 1).wait_send()

                    @pl.when(both_cores(c))
                    def _():
                        ext_out(it, other * 2).wait_send()

                    @pl.when(jnp.logical_not(both_cores(c)))
                    def _():
                        ext_pass(it, other).wait_send()

            @pl.when(it > 0)
            def _():
                omega_copy().wait_send()

        @pl.when((it == 0) & owner)
        def _():
            stat_wait(0)
            first = stats[0, 0]
            for q in range(1, chips):
                first = first + stats[0, q]
            price[1:2] = first[0:1]

        @pl.when((it > 0) & jnp.logical_not(owner))
        def _():
            omega_copy().wait_recv()

        @pl.when(it == ITERS - 1)
        def _():
            @pl.when(jnp.logical_not(owner))
            def _():
                price_copy().wait_recv()

            small_out(0).start()

        sigma = step_size * omega[0:1, 0:1]
        old_dual = dual[...]
        trial = old_dual + sigma * flow_acc[...]
        bound = limit[...]
        dual_new = trial - jnp.clip(trial, sigma * (base[...] - bound), sigma * (base[...] + bound))
        dual[...] = dual_new
        dual_half[...] = dual_new.astype(bf16)

        @pl.when(it < ITERS - 1)
        def _():
            flow_sq = fold((dual_new - old_dual) ** 2)

            @pl.when(owner)
            def _():
                stats[it + 1, chip, 3:4] = flow_sq

            @pl.when(jnp.logical_not(owner))
            def _():
                @pl.when(it > 0)
                def _():
                    flow_stat_copy(it).wait_send()

                flow_stat[0] = jnp.broadcast_to(flow_sq, (8, 128))
                flow_stat_copy(it + 1).start()

    dual_out = pltpu.make_async_copy(dual, out_dual, ext_send.at[0])
    dual_out.start()

    @pl.when(owner)
    def _():
        for r in range(members):
            target = my_group * members + r

            @pl.when(target != me)
            def _():
                fin_copy(r, my_chunk, target).wait_send()

        price_copy().wait_send()

    @pl.when(jnp.logical_not(owner))
    def _():
        flow_stat_copy(0).wait_send()

    for i in range(3):
        small_out(i).wait()
    dual_out.wait()


def finish(
    levels, dual, ramp, price, out_levels, out_dual, out_ramp, out_price,
    level_box, dual_box, tile_box, ramp_box, price_box, own_price, in_sem, out_sem,
):
    hours, ctgs, lines = out_dual.shape
    hour_rows = own_price.shape[1]
    pieces = hours // 8

    def dual_in(p):
        return pltpu.make_async_copy(dual.at[p * 8:p * 8 + 8], dual_box.at[p], in_sem.at[3 + p])

    def dual_out(p):
        return pltpu.make_async_copy(tile_box.at[p], out_dual.at[p * 8:p * 8 + 8], out_sem.at[3 + p])

    small_in = (
        pltpu.make_async_copy(price, price_box, in_sem.at[0]),
        pltpu.make_async_copy(levels, level_box, in_sem.at[1]),
        pltpu.make_async_copy(ramp, ramp_box, in_sem.at[2]),
    )
    small_out = (
        pltpu.make_async_copy(own_price, out_price, out_sem.at[0]),
        pltpu.make_async_copy(level_box, out_levels, out_sem.at[1]),
        pltpu.make_async_copy(ramp_box, out_ramp, out_sem.at[2]),
    )
    for p in range(pieces):
        dual_in(p).start()
    for copy in small_in:
        copy.start()
    for p in range(pieces):
        dual_in(p).wait()
        for k in range(ctgs):
            tile_box[p, :, k, :] = dual_box[p, :, k * lines:(k + 1) * lines]
        dual_out(p).start()
    small_in[0].wait()
    lane = lax.broadcasted_iota(jnp.int32, (1, 128), 1) - lax.axis_index("ctg") * hour_rows
    for r in range(hour_rows):
        own_price[0:1, r:r + 1] = jnp.sum(
            jnp.where(lane == r, price_box[0:1], 0.0), axis=1, keepdims=True
        )
    small_out[0].start()
    for i in (1, 2):
        small_in[i].wait()
        small_out[i].start()
    for p in range(pieces):
        dual_out(p).wait()
    for copy in small_out:
        copy.wait()


def body(
    flow_tiles,
    tile_pattern,
    monitored,
    ratings,
    base_flow,
    unit_cost,
    unit_floor,
    unit_span,
    ramp_limit,
    ramp_mask,
    demand,
    start_output,
    start_flow_dual,
    start_ramp_dual,
):
    f32, bf16 = jnp.float32, jnp.bfloat16
    ctgs, lines, unit_count = flow_tiles.shape
    n = lax.axis_size("ctg")
    hour_rows = start_output.shape[0]
    hours = hour_rows * n
    groups = hours // ROWS
    chips = n // 2
    chunks = chips // groups
    members = ROWS // hour_rows
    width = unit_count // chunks
    flat = ctgs * lines
    step_size = 0.5 / (2.0 + math.sqrt(ctgs * n * lines / unit_count))
    balance = 1.0 / math.sqrt(unit_count)

    gate_rows = ctgs * tile_pattern.shape[1]

    vmem = pl.BlockSpec(memory_space=pltpu.VMEM)
    hbm = pl.BlockSpec(memory_space=pl.ANY)
    sem = pltpu.SemaphoreType.DMA
    out = pl.pallas_call(
        functools.partial(kernel, n, hour_rows, step_size, balance),
        out_shape=(
            jax.ShapeDtypeStruct((hour_rows, unit_count), f32),
            jax.ShapeDtypeStruct((hours, flat), f32),
            jax.ShapeDtypeStruct((hour_rows, unit_count), f32),
            jax.ShapeDtypeStruct((8, 128), f32),
        ),
        in_specs=[hbm] * 14,
        out_specs=(hbm,) * 4,
        scratch_shapes=[
            pltpu.VMEM((chunks, flat, width), bf16),
            pltpu.VMEM((chunks - 2, width, flat), bf16),
            pltpu.VMEM((chunks, gate_rows, width), f32),
            pltpu.VMEM(tile_pattern.shape, jnp.int32),
            pltpu.VMEM((gate_rows, tile_pattern.shape[2]), f32),
            pltpu.VMEM(monitored.shape, jnp.int32),
            pltpu.VMEM((ratings.shape[0] // 128, 128), f32),
            pltpu.VMEM(base_flow.shape, f32),
            pltpu.VMEM(start_flow_dual.shape, f32),
            pltpu.VMEM((3, 1, width), f32),
            pltpu.VMEM((1, width), jnp.int32),
            pltpu.VMEM((1, hour_rows), f32),
            pltpu.VMEM((hours, flat), f32),
            pltpu.VMEM((hours, flat), f32),
            pltpu.VMEM((4, hour_rows, unit_count), f32),
            pltpu.VMEM((1, flat), f32),
            pltpu.VMEM((hours, flat), bf16),
            pltpu.VMEM((hours, flat), f32),
            pltpu.VMEM((members, 4, hour_rows, width), f32),
            pltpu.VMEM((chunks, 2, hour_rows, width), f32),
            pltpu.VMEM((members, 2, hour_rows, width), f32),
            pltpu.VMEM((ROWS, width), f32),
            pltpu.VMEM((ROWS, width), f32),
            pltpu.VMEM((ROWS, width), f32),
            pltpu.VMEM((ROWS, width), f32),
            pltpu.VMEM((ITERS, 8, width), f32),
            pltpu.VMEM((ITERS, 8, width), f32),
            pltpu.VMEM((chunks, hours, width), bf16),
            pltpu.VMEM((ITERS, chunks, hours, width), bf16),
            pltpu.VMEM((chunks, hours, width), bf16),
            pltpu.VMEM((ITERS, n, ROWS, width), bf16),
            pltpu.VMEM((ITERS, chunks, hours, width), bf16),
            pltpu.VMEM((ITERS + 1, chips, 4, 128), f32),
            pltpu.VMEM((ITERS, 8, 128), f32),
            pltpu.VMEM((8, 128), f32),
            pltpu.VMEM((8, 128), f32),
            sem((chunks,)), sem((members,)), sem((chips,)), sem((n,)),
            sem((n,)), sem((chips,)), sem((max(chips, chunks),)), sem((2, chips)),
            sem((6,)), sem((4,)),
        ],
        compiler_params=pltpu.CompilerParams(collective_id=0, has_side_effects=True),
    )(
        flow_tiles.reshape(flat, unit_count),
        tile_pattern,
        monitored,
        ratings.reshape(-1, 128),
        base_flow,
        start_flow_dual,
        start_output,
        unit_cost,
        start_ramp_dual,
        demand[None],
        unit_floor[None],
        unit_span[None],
        ramp_limit[None],
        ramp_mask[None],
    )
    levels, dual, ramp, price = pl.pallas_call(
        finish,
        out_shape=(
            jax.ShapeDtypeStruct((hour_rows, unit_count), f32),
            jax.ShapeDtypeStruct((hours, ctgs, lines), f32),
            jax.ShapeDtypeStruct((hour_rows, unit_count), f32),
            jax.ShapeDtypeStruct((1, hour_rows), f32),
        ),
        in_specs=[hbm] * 4,
        out_specs=(hbm,) * 4,
        scratch_shapes=[
            pltpu.VMEM((hour_rows, unit_count), f32),
            pltpu.VMEM((hours // 8, 8, flat), f32),
            pltpu.VMEM((hours // 8, 8, ctgs, lines), f32),
            pltpu.VMEM((hour_rows, unit_count), f32),
            pltpu.VMEM((8, 128), f32),
            pltpu.VMEM((1, hour_rows), f32),
            sem((3 + hours // 8,)),
            sem((3 + hours // 8,)),
        ],
    )(*out)
    return levels, dual, ramp, price.reshape(hour_rows)


def solution(mesh):
    return jax.shard_map(
        body,
        mesh=mesh,
        in_specs=(
            P("ctg", None, None),
            P("ctg", None, None),
            P("ctg", None),
            P(),
            P("grp", "ctg", None),
            P(("grp", "ctg"), None),
            P(),
            P(),
            P(),
            P(),
            P(("grp", "ctg")),
            P(("grp", "ctg"), None),
            P("grp", "ctg", None),
            P(("grp", "ctg"), None),
        ),
        out_specs=(
            P(("grp", "ctg"), None),
            P("grp", "ctg", None),
            P(("grp", "ctg"), None),
            P(("grp", "ctg")),
        ),
        check_vma=False,
    )
```

```python
import functools
import math

import jax
import jax.numpy as jnp
from jax import lax
from jax.experimental import pallas as pl
from jax.experimental.pallas import tpu as pltpu
from jax.sharding import PartitionSpec as P

ITERS = 4
ROWS = 32
STAT = 5
LAG = 0
AHEAD = 1
IN_FLIGHT = 3


def send(src, dst, send_sem, recv_sem, target):
    return pltpu.make_async_remote_copy(
        src_ref=src,
        dst_ref=dst,
        send_sem=send_sem,
        recv_sem=recv_sem,
        device_id={"ctg": target},
        device_id_type=pl.DeviceIdType.MESH,
    )


def kernel(
    n, hour_rows, step_size, balance,
    tiles, pattern_hbm, index_hbm, table_hbm, base_hbm, dual_hbm, level_hbm, cost_hbm, ramp_hbm, demand_hbm,
    floor_hbm, span_hbm, ramp_limit_hbm, ramp_mask_hbm,
    out_levels, out_dual, out_ramp, out_price,
    masked, turned, gates, pattern, pattern_rows, index, table, base_in, dual_in, unit_rows, mask_row, demand,
    dual, base, starts, limit, dual_half, flow_acc,
    start_stage, frag_in, frag_out,
    cost, levels, ramp, extended, halo_ext, halo_ramp,
    pull_out, pair_in, pull_sum, pull_in, ext_half, stats, flow_stat, price, omega,
    frag_send, frag_recv, pull_send, pull_recv, ext_send, ext_recv, stat_send, stat_recv,
    core_sems, halo_sems,
):
    f32 = jnp.float32
    bf16 = jnp.bfloat16
    chips = n // 2
    members = ROWS // hour_rows
    groups = n // members
    chunks = chips // groups
    unit_count = tiles.shape[1]
    width = unit_count // chunks
    ctgs, lines = base_in.shape[1], base_in.shape[2]
    hours = groups * ROWS
    pairs = chunks // 2
    halves = lines // 128

    me = lax.axis_index("ctg")
    core = lax.rem(me, 2)
    chip = lax.div(me, 2)
    owner = core == 1
    partner = me + 1 - 2 * core
    my_chunk = lax.div(chip, groups)
    my_group = lax.rem(chip, groups)
    home_group = lax.div(me, members)
    home_row = lax.rem(me, members)
    my_pair = lax.div(my_chunk, 2)
    my_side = lax.rem(my_chunk, 2)
    my_rows = pl.ds(pl.multiple_of(my_group * ROWS, ROWS), ROWS)
    my_lanes = pl.ds(pl.multiple_of(my_chunk * width, 128), width)

    ahead = 1 - lax.div(my_pair, pairs // 2)

    def flip(place, length):
        return ahead * (length - 1 - place) + (1 - ahead) * place

    def skip(place, own, length):
        return place + lax.div(place + length - own, length)

    def far_pair(j):
        last = lax.div(j + 1, pairs)
        place = flip(skip(j, flip(my_pair, pairs), pairs), pairs)
        return last * my_pair + (1 - last) * place

    def near_pair(j):
        return far_pair(pairs - 1 - j)

    def far_chunk(j):
        second = lax.rem(j, 2)
        side = second * my_side + (1 - second) * (1 - my_side)
        return far_pair(lax.div(j, 2)) * 2 + side

    def sums_here(j):
        return (j >= EARLY) == owner

    def both_cores(c):
        return c == my_chunk

    def block_rows(g):
        return pl.ds(pl.multiple_of(g * ROWS, ROWS), ROWS)

    def tile_copy(j):
        c = far_chunk(j)
        return pltpu.make_async_copy(
            tiles.at[:, pl.ds(pl.multiple_of(c * width, 128), width)], masked.at[c], stat_send.at[j]
        )

    def staged(i):
        src, dst = (
            (pattern_hbm, pattern),
            (dual_hbm, dual_in),
            (demand_hbm, demand),
            (level_hbm, starts.at[0]),
            (cost_hbm, starts.at[1]),
            (ramp_hbm, starts.at[2]),
            (index_hbm, index),
            (table_hbm, table),
            (base_hbm, base_in),
            (floor_hbm.at[:, my_lanes], unit_rows.at[0]),
            (span_hbm.at[:, my_lanes], unit_rows.at[1]),
            (ramp_limit_hbm.at[:, my_lanes], unit_rows.at[2]),
            (ramp_mask_hbm.at[:, my_lanes], mask_row),
        )[i]
        return pltpu.make_async_copy(src, dst, core_sems.at[i - 3] if i in (6, 7, 8) else ext_send.at[i])

    for i in range(2):
        staged(i).start()
    tile_copy(0).start()

    barrier = pltpu.get_barrier_semaphore()

    @pl.loop(1, n)
    def _(d):
        pl.semaphore_signal(
            barrier, inc=1, device_id={"ctg": lax.rem(me + d, n)}, device_id_type=pl.DeviceIdType.MESH
        )

    for j in range(1, IN_FLIGHT):
        tile_copy(j).start()
    for i in range(2, 13):
        staged(i).start()

    omega[...] = jnp.ones_like(omega)
    price[...] = jnp.zeros_like(price)

    staged(0).wait()
    for k in range(ctgs):
        pattern_rows[k * halves:(k + 1) * halves, :] = pattern[k].astype(f32)
    for b in range(unit_count // 128):
        place = b * 128 % width
        gates[b * 128 // width, :, place:place + 128] = jnp.broadcast_to(
            pattern_rows[:, b:b + 1], (ctgs * halves, 128)
        )

    def frag_copy(c, target):
        return send(
            starts.at[:, :, pl.ds(pl.multiple_of(c * width, 128), width)],
            start_stage.at[home_row], frag_send.at[c], frag_recv.at[home_row], target,
        )

    def fin_copy(r, source_chunk, target):
        return send(
            frag_out.at[r], frag_in.at[source_chunk], frag_recv.at[r], frag_send.at[source_chunk], target
        )

    def stat_copy(slot, target_chip, sender_chip):
        return send(
            stats.at[slot, sender_chip], stats.at[slot, sender_chip],
            stat_send.at[target_chip], stat_recv.at[slot % 2, sender_chip], target_chip * 2 + 1,
        )

    def stat_start(slot):
        @pl.loop(1, chips)
        def _(d):
            stat_copy(slot, lax.rem(chip + d, chips), chip).start()

    def stat_wait(slot):
        @pl.loop(1, chips)
        def _(d):
            peer = lax.rem(chip + d, chips)
            stat_copy(slot, peer, chip).wait_send()
            stat_copy(slot, peer, peer).wait_recv()

    def flow_stat_copy(slot):
        return send(flow_stat.at[0], flow_stat.at[slot], core_sems.at[0], core_sems.at[1], partner)

    def omega_copy():
        return send(omega, omega, core_sems.at[2], core_sems.at[3], partner)

    def price_copy():
        return send(price, price, core_sems.at[4], core_sems.at[5], partner)

    def pair_copy(it, c):
        return send(pull_out.at[c], pair_in.at[it, c], pull_send.at[c * groups], pull_recv.at[c], partner)

    def pull_copy(it, src, target_chip, sender):
        c, g = lax.div(target_chip, groups), lax.rem(target_chip, groups)
        return send(
            src.at[c, block_rows(g)], pull_in.at[it, sender],
            pull_send.at[target_chip], pull_recv.at[sender], target_chip * 2 + 1,
        )

    def ext_copy(it, origin_chip, send_sem, target):
        c, g = lax.div(origin_chip, groups), lax.rem(origin_chip, groups)
        spot = ext_half.at[it, c, block_rows(g)]
        return send(spot, spot, send_sem, ext_recv.at[origin_chip], target)

    def ext_out(it, target):
        return ext_copy(it, chip, ext_send.at[target], target)

    def ext_pass(it, origin_chip):
        return ext_copy(it, origin_chip, ext_send.at[origin_chip * 2], partner)

    def halo_ext_copy(it, target):
        return send(extended.at[pl.ds(0, 8)], halo_ext.at[it], halo_sems.at[0], halo_sems.at[1], target)

    def halo_ramp_copy(it, target):
        return send(ramp.at[pl.ds(ROWS - 8, 8)], halo_ramp.at[it], halo_sems.at[2], halo_sems.at[3], target)

    def product(c):
        pull_out[c] = jnp.dot(dual_half[...], masked[c], preferred_element_type=f32).astype(bf16)

    def deliver(it, j):
        c = far_chunk(j)

        @pl.when((j < chunks // 2) & owner)
        def _():
            pair_copy(it, c).start()

        @pl.when(j >= chunks // 2)
        def _():
            for g in range(groups):
                target_chip = c * groups + g
                here = owner & (target_chip == chip)

                @pl.when(here)
                def _():
                    pull_in[it, me] = pull_out[c, g * ROWS:(g + 1) * ROWS, :]

                @pl.when(jnp.logical_not(here))
                def _():
                    pull_copy(it, pull_out, target_chip, me).start()

    def forward(it, j):
        @pl.when((j >= 0) & (j < chunks // 2) & jnp.logical_not(owner))
        def _():
            c = far_chunk(j)
            pair_copy(it, c).wait_recv()
            pull_sum[c] = (pull_out[c].astype(f32) + pair_in[it, c].astype(f32)).astype(bf16)
            for g in range(groups):
                pull_copy(it, pull_sum, c * groups + g, me).start()

    def pull_sent(it):
        @pl.loop(0, chunks)
        def _(j):
            c = far_chunk(j)
            paired = (j < chunks // 2) & owner

            @pl.when(paired)
            def _():
                pair_copy(it, c).wait_send()

            for g in range(groups):
                target_chip = c * groups + g
                here = owner & (target_chip == chip)

                @pl.when(jnp.logical_not(paired | here))
                def _():
                    pull_copy(it, pull_out, target_chip, me).wait_send()

    def mask(j):
        c = far_chunk(j)
        tile_copy(j).wait()

        @pl.when(j + IN_FLIGHT < chunks)
        def _():
            tile_copy(j + IN_FLIGHT).start()

        for r in range(ctgs * halves):
            gate = jnp.broadcast_to(gates[c, r:r + 1, :], (16, width)).astype(bf16)
            for q in range(8):
                where = slice(r * 128 + q * 16, r * 128 + q * 16 + 16)
                masked[c, where, :] = masked[c, where, :] * gate

    first_lag = 2

    @pl.loop(0, chunks + first_lag)
    def _(j):
        @pl.when(j < chunks)
        def _():
            mask(j)

        @pl.when(j == 0)
        def _():
            staged(1).wait()
            for k in range(ctgs):
                lanes = slice(k * lines, (k + 1) * lines)
                start_dual = dual_in[:, k, :]
                dual[:, lanes] = start_dual
                dual_half[:, lanes] = start_dual.astype(bf16)

        @pl.when(j < chunks)
        def _():
            product(far_chunk(j))

        @pl.when(j == 0)
        def _():
            for i in range(2, 6):
                staged(i).wait()
            for r in range(hour_rows):
                starts[3, r:r + 1] = jnp.broadcast_to(demand[0:1, r:r + 1], (1, unit_count))
            pl.semaphore_wait(barrier, n - 1)
            for c in range(chunks):
                target = (c * groups + home_group) * 2 + 1

                @pl.when(target != me)
                def _():
                    frag_copy(c, target).start()

                @pl.when(target == me)
                def _():
                    start_stage[home_row] = starts[:, :, c * width:(c + 1) * width]

        @pl.when(j < chunks)
        def _():
            deliver(0, j)

        forward(0, j - first_lag)

    for i in range(9, 13):
        staged(i).wait()

    block_row = lax.broadcasted_iota(jnp.int32, (ROWS, width), 0)
    lane_here = lax.broadcasted_iota(jnp.int32, (ROWS, 128), 1)
    row_here = lax.broadcasted_iota(jnp.int32, (ROWS, 128), 0) + my_group * ROWS
    diagonal = lane_here == row_here
    hour_lanes = lax.broadcasted_iota(jnp.int32, (1, 128), 1) < hours
    stat_row = lax.broadcasted_iota(jnp.int32, (4, 128), 0)

    def to_lanes(column):
        return jnp.sum(
            jnp.where(diagonal, jnp.broadcast_to(column, (ROWS, 128)), 0.0), axis=0, keepdims=True
        )

    def fold(x):
        rows, cols = x.shape
        out = None
        for r in range(0, rows, 8):
            for b in range(0, cols, 128):
                piece = x[r:r + 8, b:b + 128]
                out = piece if out is None else out + piece
        return jnp.sum(out, axis=0, keepdims=True)

    def halo_ramp_start(it):
        if groups > 1:
            @pl.when(my_group < groups - 1)
            def _():
                halo_ramp_copy(it, me + 2).start()

    @pl.when(owner)
    def _():
        for r in range(members):
            peer = my_group * members + r

            @pl.when(peer != me)
            def _():
                send(
                    starts.at[:, :, pl.ds(0, width)], start_stage.at[r],
                    frag_send.at[0], frag_recv.at[r], peer,
                ).wait_recv()

        demand_rows = []
        for r in range(members):
            rows = slice(r * hour_rows, (r + 1) * hour_rows)
            levels[rows, :] = start_stage[r, 0]
            cost[rows, :] = start_stage[r, 1]
            ramp[rows, :] = start_stage[r, 2]
            extended[rows, 0:128] = start_stage[r, 3, :, 0:128]
        lanes = to_lanes(extended[:, 0:1])
        mine = (stat_row == 0) & (jnp.full((4, 128), my_chunk) == 0)
        stats[0, chip] = jnp.where(mine, lanes, 0.0)
        stat_start(0)
        halo_ramp_start(0)

    for c in range(chunks):
        target = (c * groups + home_group) * 2 + 1

        @pl.when(target != me)
        def _():
            frag_copy(c, target).wait_send()

    def absorb(slot, sigma):
        total = stats[slot, 0]
        for q in range(1, chips):
            total = total + stats[slot, q]
        move = sigma * (balance * (total[0:1] - price[1:2]))
        move = jnp.where(hour_lanes, move, 0.0)
        price[0:1] = price[0:1] + move
        return total, jnp.sum(move * move, axis=1, keepdims=True)

    def primal(it):
        @pl.when(it > 0)
        def _():
            stat_wait(it)

        @pl.when(it > 0)
        def _():
            old = omega[0:1, 0:1]
            total, price_sq = absorb(it, step_size * old)
            sums = jnp.sum(total, axis=1, keepdims=True)
            dual_sq = sums[3:4] + sums[2:3] + price_sq
            ratio = (dual_sq + 1e-06) / (sums[1:2] + 1e-06)
            omega[...] = jnp.broadcast_to(jnp.sqrt(old) * jnp.sqrt(jnp.sqrt(ratio)), omega.shape)
            omega_copy().start()

        weight = omega[0:1, 0:1]
        tau = step_size / weight
        sigma = step_size * weight

        if groups > 1:
            @pl.when(my_group < groups - 1)
            def _():
                halo_ramp_copy(it, me + 2).wait_send()

            @pl.when(my_group > 0)
            def _():
                halo_ramp_copy(it, me - 2).wait_recv()

            @pl.when(my_group == 0)
            def _():
                halo_ramp[it] = jnp.zeros_like(halo_ramp[it])

            edge_ramp = halo_ramp[it][7:8]
        else:
            edge_ramp = jnp.zeros((1, width), f32)

        floor = unit_rows[0]
        ceiling = floor + unit_rows[1]
        ramp_limit = unit_rows[2]
        ramp_on = mask_row[...].astype(f32)
        ramp_now = ramp[...]
        before = jnp.where(block_row == 0, edge_ramp, pltpu.roll(ramp_now, 1, 0))
        price_here = jnp.sum(
            jnp.where(diagonal, jnp.broadcast_to(price[0:1], (ROWS, 128)), 0.0), axis=1, keepdims=True
        )
        known = cost[...] + ramp_on * (before - ramp_now) + balance * price_here

        first_near = lax.div(my_pair, pairs // 2) * (chips // 2)

        @pl.loop(0, chips)
        def _(q):
            pull_copy(it, pull_out, q, q * 2).wait_recv()

        @pl.loop(0, chips // 2)
        def _(q):
            @pl.when(first_near + q != chip)
            def _():
                pull_copy(it, pull_out, q, (first_near + q) * 2 + 1).wait_recv()

        pulled = pull_in[it, 0].astype(f32)
        for q in range(1, chips):
            pulled = pulled + pull_in[it, q * 2].astype(f32)
        for q in range(chips // 2):
            pulled = pulled + pull_in[it, (first_near + q) * 2 + 1].astype(f32)

        gradient = known + pulled
        old_levels = levels[...]
        moved = jnp.clip(old_levels - tau * gradient, floor, ceiling)
        ext = 2.0 * moved - old_levels
        levels[...] = moved
        ext_half[it, my_chunk, my_rows, :] = ext.astype(bf16)
        extended[...] = ext

        @pl.loop(0, chunks)
        def _(j):
            c = far_chunk(j)
            for g in range(groups):
                other = c * groups + g

                @pl.when(other != chip)
                def _():
                    ext_out(it, other * 2 + 1).start()

                @pl.when(both_cores(c))
                def _():
                    ext_out(it, other * 2).start()

        if groups > 1:
            @pl.when(my_group > 0)
            def _():
                halo_ext_copy(it, me - 2).start()
                halo_ext_copy(it, me - 2).wait_send()

            @pl.when(my_group < groups - 1)
            def _():
                halo_ext_copy(it, me + 2).wait_recv()

            @pl.when(my_group == groups - 1)
            def _():
                halo_ext[it] = jnp.zeros_like(halo_ext[it])

            edge_ext = halo_ext[it][0:1]
        else:
            edge_ext = jnp.zeros((1, width), f32)

        after = jnp.where(block_row == ROWS - 1, edge_ext, pltpu.roll(ext, ROWS - 1, 0))
        change = ramp_on * (after - ext)
        last_hour = block_row + my_group * ROWS == hours - 1
        change = jnp.where(last_hour, 0.0, change)
        trial = ramp_now + sigma * change
        ramp_new = trial - jnp.clip(trial, -sigma * ramp_limit, sigma * ramp_limit)
        ramp[...] = ramp_new

        row_sums = to_lanes(jnp.sum(ext, axis=1, keepdims=True))
        primal_sq = fold((moved - old_levels) ** 2)
        ramp_sq = fold((ramp_new - ramp_now) ** 2)
        stats[it + 1, chip] = jnp.where(
            stat_row == 0, row_sums,
            jnp.where(stat_row == 1, primal_sq, jnp.where(stat_row == 2, ramp_sq, 0.0)),
        )

        @pl.when(it == ITERS - 1)
        def _():
            stat_start(it + 1)
            for r in range(members):
                rows = slice(r * hour_rows, (r + 1) * hour_rows)
                frag_out[r, 0] = moved[rows, :]
                frag_out[r, 1] = ramp_new[rows, :]
            for r in range(members):
                target = my_group * members + r

                @pl.when(target != me)
                def _():
                    fin_copy(r, my_chunk, target).start()

                @pl.when(target == me)
                def _():
                    frag_in[my_chunk] = frag_out[r]

    def line_limits():
        for i in range(6, 9):
            staged(i).wait()

        row_iota = lax.broadcasted_iota(jnp.int32, (128, lines), 0)
        values = table[...].T
        part_a = values.astype(bf16)
        rest = values - part_a.astype(f32)
        part_b = rest.astype(bf16)
        part_c = (rest - part_b.astype(f32)).astype(bf16)
        for k in range(ctgs):
            which = index[k:k + 1, :]
            high = lax.shift_right_logical(which, 7)
            low = lax.bitwise_and(which, 127)
            blocks = table.shape[0] // 128
            got = jnp.zeros((128, lines), f32)
            for b in range(blocks):
                pick = jnp.where(row_iota + b * 128 == high, 1.0, 0.0).astype(bf16)
                for part in (part_a, part_b, part_c):
                    got = got + jnp.dot(part[:, b * 128:(b + 1) * 128], pick, preferred_element_type=f32)
            limit[:, k * lines:(k + 1) * lines] = jnp.sum(
                jnp.where(row_iota == low, got, 0.0), axis=0, keepdims=True
            )
            base[:, k * lines:(k + 1) * lines] = base_in[:, k, :]

    def take(it, c):
        for g in range(groups):
            other = c * groups + g

            @pl.when(jnp.logical_not(owner & (other == chip)))
            def _():
                ext_pass(it, other).wait_recv()

    def take_and_pass(it, c):
        take(it, c)

        @pl.when(owner & jnp.logical_not(both_cores(c)))
        def _():
            for g in range(groups):
                ext_pass(it, c * groups + g).start()

    def flow(x, w):
        return lax.dot_general(x, w, (((1,), (1,)), ((), ())), preferred_element_type=f32)

    def small_out(i):
        src, dst = ((price, out_price), (starts.at[0], out_levels), (starts.at[1], out_ramp))[i]
        return pltpu.make_async_copy(src, dst, pull_recv.at[i])

    def write_small():
        @pl.when(owner)
        def _():
            stat_wait(ITERS)
            absorb(ITERS, step_size * omega[0:1, 0:1])
            price_copy().start()

        for c in range(chunks):
            peer = (c * groups + home_group) * 2 + 1

            @pl.when(peer != me)
            def _():
                fin_copy(0, c, peer).wait_recv()

        for c in range(chunks):
            for which in range(2):
                starts[which, :, c * width:(c + 1) * width] = frag_in[c, which]
        small_out(1).start()
        small_out(2).start()

    turns = (chunks - 1) // 2
    blocks = ctgs * lines // 256

    def turn(first, last):
        @pl.loop(first * blocks, last * blocks)
        def _(i):
            j = lax.div(i, blocks)
            block = pl.ds(pl.multiple_of(lax.rem(i, blocks) * 256, 256), 256)
            turned[j, :, block] = masked[far_chunk(j), block, :].T

    @pl.loop(0, ITERS)
    def _(it):
        @pl.when(it > 0)
        def _():
            @pl.loop(0, chunks)
            def _(j):
                product(far_chunk(j))
                deliver(it, j)

                @pl.when((j == STAT) & owner)
                def _():
                    halo_ramp_start(it)
                    flow_stat_copy(it).wait_recv()
                    stats[it, chip, 3:4] = stats[it, chip, 3:4] + flow_stat[it, 0:1]
                    stat_start(it)

                forward(it, j - LAG)

            @pl.when(it < 3)
            def _():
                turn(1 + (it - 1) * turns, it * turns)

        @pl.when(it == 0)
        def _():
            turn(0, 1)

        pull_sent(it)

        @pl.when(owner)
        def _():
            primal(it)

        take(it, my_chunk)
        flow_acc[...] = flow(ext_half[it, my_chunk], masked[my_chunk])

        @pl.when(it == 0)
        def _():
            line_limits()

        @pl.when(it == 1)
        def _():
            turn(turns, turns + 1)

        near = my_pair * 2 + 1 - my_side
        take_and_pass(it, near)
        flow_acc[...] += flow(ext_half[it, near], masked[near])

        @pl.loop(1, pairs + AHEAD)
        def _(j):
            @pl.when(j < pairs)
            def _():
                c = near_pair(j) * 2
                take_and_pass(it, c)
                take_and_pass(it, c + 1)

            @pl.when((it == ITERS - 1) & (j == pairs))
            def _():
                write_small()

            @pl.when(j > AHEAD)
            def _():
                place = (pairs - 1 - j + AHEAD) * 2
                c, d = far_chunk(place), far_chunk(place + 1)
                x = jnp.concatenate([ext_half[it, c], ext_half[it, d]], axis=1)
                ready = (it > 1) | ((it == 1) & (place <= turns - 1))

                @pl.when(ready)
                def _():
                    w = jnp.concatenate([turned[place], turned[place + 1]], axis=0)
                    flow_acc[...] += jnp.dot(x, w, preferred_element_type=f32)

                @pl.when(jnp.logical_not(ready))
                def _():
                    w = jnp.concatenate([masked[c], masked[d]], axis=1)
                    flow_acc[...] += flow(x, w)

        @pl.when(owner)
        def _():
            @pl.loop(0, chunks)
            def _(c):
                for g in range(groups):
                    other = c * groups + g

                    @pl.when(other != chip)
                    def _():
                        ext_out(it, other * 2 + 1).wait_send()

                    @pl.when(both_cores(c))
                    def _():
                        ext_out(it, other * 2).wait_send()

                    @pl.when(jnp.logical_not(both_cores(c)))
                    def _():
                        ext_pass(it, other).wait_send()

            @pl.when(it > 0)
            def _():
                omega_copy().wait_send()

        @pl.when((it == 0) & owner)
        def _():
            stat_wait(0)
            first = stats[0, 0]
            for q in range(1, chips):
                first = first + stats[0, q]
            price[1:2] = first[0:1]

        @pl.when((it > 0) & jnp.logical_not(owner))
        def _():
            omega_copy().wait_recv()

        @pl.when(it == ITERS - 1)
        def _():
            @pl.when(jnp.logical_not(owner))
            def _():
                price_copy().wait_recv()

            small_out(0).start()

        sigma = step_size * omega[0:1, 0:1]
        old_dual = dual[...]
        trial = old_dual + sigma * flow_acc[...]
        bound = limit[...]
        dual_new = trial - jnp.clip(trial, sigma * (base[...] - bound), sigma * (base[...] + bound))
        dual[...] = dual_new
        dual_half[...] = dual_new.astype(bf16)

        @pl.when(it < ITERS - 1)
        def _():
            flow_sq = fold((dual_new - old_dual) ** 2)

            @pl.when(owner)
            def _():
                stats[it + 1, chip, 3:4] = flow_sq

            @pl.when(jnp.logical_not(owner))
            def _():
                @pl.when(it > 0)
                def _():
                    flow_stat_copy(it).wait_send()

                flow_stat[0] = jnp.broadcast_to(flow_sq, (8, 128))
                flow_stat_copy(it + 1).start()

    dual_out = pltpu.make_async_copy(dual, out_dual, ext_send.at[0])
    dual_out.start()

    @pl.when(owner)
    def _():
        for r in range(members):
            target = my_group * members + r

            @pl.when(target != me)
            def _():
                fin_copy(r, my_chunk, target).wait_send()

        price_copy().wait_send()

    @pl.when(jnp.logical_not(owner))
    def _():
        flow_stat_copy(0).wait_send()

    for i in range(3):
        small_out(i).wait()
    dual_out.wait()


def finish(
    levels, dual, ramp, price, out_levels, out_dual, out_ramp, out_price,
    level_box, dual_box, tile_box, ramp_box, price_box, own_price, in_sem, out_sem,
):
    hours, ctgs, lines = out_dual.shape
    hour_rows = own_price.shape[1]
    pieces = hours // 8

    def dual_in(p):
        return pltpu.make_async_copy(dual.at[p * 8:p * 8 + 8], dual_box.at[p], in_sem.at[3 + p])

    def dual_out(p):
        return pltpu.make_async_copy(tile_box.at[p], out_dual.at[p * 8:p * 8 + 8], out_sem.at[3 + p])

    small_in = (
        pltpu.make_async_copy(price, price_box, in_sem.at[0]),
        pltpu.make_async_copy(levels, level_box, in_sem.at[1]),
        pltpu.make_async_copy(ramp, ramp_box, in_sem.at[2]),
    )
    small_out = (
        pltpu.make_async_copy(own_price, out_price, out_sem.at[0]),
        pltpu.make_async_copy(level_box, out_levels, out_sem.at[1]),
        pltpu.make_async_copy(ramp_box, out_ramp, out_sem.at[2]),
    )
    for p in range(pieces):
        dual_in(p).start()
    for copy in small_in:
        copy.start()
    for p in range(pieces):
        dual_in(p).wait()
        for k in range(ctgs):
            tile_box[p, :, k, :] = dual_box[p, :, k * lines:(k + 1) * lines]
        dual_out(p).start()
    small_in[0].wait()
    lane = lax.broadcasted_iota(jnp.int32, (1, 128), 1) - lax.axis_index("ctg") * hour_rows
    for r in range(hour_rows):
        own_price[0:1, r:r + 1] = jnp.sum(
            jnp.where(lane == r, price_box[0:1], 0.0), axis=1, keepdims=True
        )
    small_out[0].start()
    for i in (1, 2):
        small_in[i].wait()
        small_out[i].start()
    for p in range(pieces):
        dual_out(p).wait()
    for copy in small_out:
        copy.wait()


def body(
    flow_tiles,
    tile_pattern,
    monitored,
    ratings,
    base_flow,
    unit_cost,
    unit_floor,
    unit_span,
    ramp_limit,
    ramp_mask,
    demand,
    start_output,
    start_flow_dual,
    start_ramp_dual,
):
    f32, bf16 = jnp.float32, jnp.bfloat16
    ctgs, lines, unit_count = flow_tiles.shape
    n = lax.axis_size("ctg")
    hour_rows = start_output.shape[0]
    hours = hour_rows * n
    groups = hours // ROWS
    chips = n // 2
    chunks = chips // groups
    members = ROWS // hour_rows
    width = unit_count // chunks
    flat = ctgs * lines
    step_size = 0.5 / (2.0 + math.sqrt(ctgs * n * lines / unit_count))
    balance = 1.0 / math.sqrt(unit_count)

    gate_rows = ctgs * tile_pattern.shape[1]

    vmem = pl.BlockSpec(memory_space=pltpu.VMEM)
    hbm = pl.BlockSpec(memory_space=pl.ANY)
    sem = pltpu.SemaphoreType.DMA
    out = pl.pallas_call(
        functools.partial(kernel, n, hour_rows, step_size, balance),
        out_shape=(
            jax.ShapeDtypeStruct((hour_rows, unit_count), f32),
            jax.ShapeDtypeStruct((hours, flat), f32),
            jax.ShapeDtypeStruct((hour_rows, unit_count), f32),
            jax.ShapeDtypeStruct((8, 128), f32),
        ),
        in_specs=[hbm] * 14,
        out_specs=(hbm,) * 4,
        scratch_shapes=[
            pltpu.VMEM((chunks, flat, width), bf16),
            pltpu.VMEM((chunks - 2, width, flat), bf16),
            pltpu.VMEM((chunks, gate_rows, width), f32),
            pltpu.VMEM(tile_pattern.shape, jnp.int32),
            pltpu.VMEM((gate_rows, tile_pattern.shape[2]), f32),
            pltpu.VMEM(monitored.shape, jnp.int32),
            pltpu.VMEM((ratings.shape[0] // 128, 128), f32),
            pltpu.VMEM(base_flow.shape, f32),
            pltpu.VMEM(start_flow_dual.shape, f32),
            pltpu.VMEM((3, 1, width), f32),
            pltpu.VMEM((1, width), jnp.int32),
            pltpu.VMEM((1, hour_rows), f32),
            pltpu.VMEM((hours, flat), f32),
            pltpu.VMEM((hours, flat), f32),
            pltpu.VMEM((4, hour_rows, unit_count), f32),
            pltpu.VMEM((1, flat), f32),
            pltpu.VMEM((hours, flat), bf16),
            pltpu.VMEM((hours, flat), f32),
            pltpu.VMEM((members, 4, hour_rows, width), f32),
            pltpu.VMEM((chunks, 2, hour_rows, width), f32),
            pltpu.VMEM((members, 2, hour_rows, width), f32),
            pltpu.VMEM((ROWS, width), f32),
            pltpu.VMEM((ROWS, width), f32),
            pltpu.VMEM((ROWS, width), f32),
            pltpu.VMEM((ROWS, width), f32),
            pltpu.VMEM((ITERS, 8, width), f32),
            pltpu.VMEM((ITERS, 8, width), f32),
            pltpu.VMEM((chunks, hours, width), bf16),
            pltpu.VMEM((ITERS, chunks, hours, width), bf16),
            pltpu.VMEM((chunks, hours, width), bf16),
            pltpu.VMEM((ITERS, n, ROWS, width), bf16),
            pltpu.VMEM((ITERS, chunks, hours, width), bf16),
            pltpu.VMEM((ITERS + 1, chips, 4, 128), f32),
            pltpu.VMEM((ITERS, 8, 128), f32),
            pltpu.VMEM((8, 128), f32),
            pltpu.VMEM((8, 128), f32),
            sem((chunks,)), sem((members,)), sem((chips,)), sem((n,)),
            sem((n,)), sem((chips,)), sem((max(chips, chunks),)), sem((2, chips)),
            sem((6,)), sem((4,)),
        ],
        compiler_params=pltpu.CompilerParams(collective_id=0, has_side_effects=True),
    )(
        flow_tiles.reshape(flat, unit_count),
        tile_pattern,
        monitored,
        ratings.reshape(-1, 128),
        base_flow,
        start_flow_dual,
        start_output,
        unit_cost,
        start_ramp_dual,
        demand[None],
        unit_floor[None],
        unit_span[None],
        ramp_limit[None],
        ramp_mask[None],
    )
    levels, dual, ramp, price = pl.pallas_call(
        finish,
        out_shape=(
            jax.ShapeDtypeStruct((hour_rows, unit_count), f32),
            jax.ShapeDtypeStruct((hours, ctgs, lines), f32),
            jax.ShapeDtypeStruct((hour_rows, unit_count), f32),
            jax.ShapeDtypeStruct((1, hour_rows), f32),
        ),
        in_specs=[hbm] * 4,
        out_specs=(hbm,) * 4,
        scratch_shapes=[
            pltpu.VMEM((hour_rows, unit_count), f32),
            pltpu.VMEM((hours // 8, 8, flat), f32),
            pltpu.VMEM((hours // 8, 8, ctgs, lines), f32),
            pltpu.VMEM((hour_rows, unit_count), f32),
            pltpu.VMEM((8, 128), f32),
            pltpu.VMEM((1, hour_rows), f32),
            sem((3 + hours // 8,)),
            sem((3 + hours // 8,)),
        ],
    )(*out)
    return levels, dual, ramp, price.reshape(hour_rows)


def solution(mesh):
    return jax.shard_map(
        body,
        mesh=mesh,
        in_specs=(
            P("ctg", None, None),
            P("ctg", None, None),
            P("ctg", None),
            P(),
            P("grp", "ctg", None),
            P(("grp", "ctg"), None),
            P(),
            P(),
            P(),
            P(),
            P(("grp", "ctg")),
            P(("grp", "ctg"), None),
            P("grp", "ctg", None),
            P(("grp", "ctg"), None),
        ),
        out_specs=(
            P(("grp", "ctg"), None),
            P("grp", "ctg", None),
            P(("grp", "ctg"), None),
            P(("grp", "ctg")),
        ),
        check_vma=False,
    )
```

```python
import functools
import math

import jax
import jax.numpy as jnp
from jax import lax
from jax.experimental import pallas as pl
from jax.experimental.pallas import tpu as pltpu
from jax.sharding import PartitionSpec as P

ITERS = 4
ROWS = 32
STAT = 5
LAG = 0
AHEAD = 1
IN_FLIGHT = 3


def send(src, dst, send_sem, recv_sem, target):
    return pltpu.make_async_remote_copy(
        src_ref=src,
        dst_ref=dst,
        send_sem=send_sem,
        recv_sem=recv_sem,
        device_id={"ctg": target},
        device_id_type=pl.DeviceIdType.MESH,
    )


def kernel(
    n, hour_rows, step_size, balance,
    tiles, pattern_hbm, index_hbm, table_hbm, base_hbm, dual_hbm, level_hbm, cost_hbm, ramp_hbm, demand_hbm,
    floor_hbm, span_hbm, ramp_limit_hbm, ramp_mask_hbm,
    out_levels, out_dual, out_ramp, out_price,
    masked, turned, gates, pattern, pattern_rows, index, table, base_in, dual_in, unit_rows, mask_row, demand,
    dual, base, starts, limit, dual_half, flow_acc,
    start_stage, frag_in, frag_out,
    cost, levels, ramp, extended, halo_ext, halo_ramp,
    pull_out, pair_in, pull_sum, pull_in, ext_half, stats, flow_stat, price, omega,
    frag_send, frag_recv, pull_send, pull_recv, ext_send, ext_recv, stat_send, stat_recv,
    core_sems, halo_sems,
):
    f32 = jnp.float32
    bf16 = jnp.bfloat16
    chips = n // 2
    members = ROWS // hour_rows
    groups = n // members
    chunks = chips // groups
    unit_count = tiles.shape[1]
    width = unit_count // chunks
    ctgs, lines = base_in.shape[1], base_in.shape[2]
    hours = groups * ROWS
    pairs = chunks // 2
    halves = lines // 128

    me = lax.axis_index("ctg")
    core = lax.rem(me, 2)
    chip = lax.div(me, 2)
    owner = core == 1
    partner = me + 1 - 2 * core
    my_chunk = lax.div(chip, groups)
    my_group = lax.rem(chip, groups)
    home_group = lax.div(me, members)
    home_row = lax.rem(me, members)
    my_pair = lax.div(my_chunk, 2)
    my_side = lax.rem(my_chunk, 2)
    my_rows = pl.ds(pl.multiple_of(my_group * ROWS, ROWS), ROWS)
    my_lanes = pl.ds(pl.multiple_of(my_chunk * width, 128), width)

    ahead = 1 - lax.div(my_pair, pairs // 2)

    def flip(place, length):
        return ahead * (length - 1 - place) + (1 - ahead) * place

    def skip(place, own, length):
        return place + lax.div(place + length - own, length)

    def far_pair(j):
        last = lax.div(j + 1, pairs)
        place = flip(skip(j, flip(my_pair, pairs), pairs), pairs)
        return last * my_pair + (1 - last) * place

    def near_pair(j):
        return far_pair(pairs - 1 - j)

    def far_chunk(j):
        second = lax.rem(j, 2)
        side = second * my_side + (1 - second) * (1 - my_side)
        return far_pair(lax.div(j, 2)) * 2 + side

    def sums_here(j):
        return (j >= EARLY) == owner

    def both_cores(c):
        return c == my_chunk

    def block_rows(g):
        return pl.ds(pl.multiple_of(g * ROWS, ROWS), ROWS)

    def tile_copy(j):
        c = far_chunk(j)
        return pltpu.make_async_copy(
            tiles.at[:, pl.ds(pl.multiple_of(c * width, 128), width)], masked.at[c], stat_send.at[j]
        )

    def staged(i):
        src, dst = (
            (pattern_hbm, pattern),
            (dual_hbm, dual_in),
            (demand_hbm, demand),
            (level_hbm, starts.at[0]),
            (cost_hbm, starts.at[1]),
            (ramp_hbm, starts.at[2]),
            (index_hbm, index),
            (table_hbm, table),
            (base_hbm, base_in),
            (floor_hbm.at[:, my_lanes], unit_rows.at[0]),
            (span_hbm.at[:, my_lanes], unit_rows.at[1]),
            (ramp_limit_hbm.at[:, my_lanes], unit_rows.at[2]),
            (ramp_mask_hbm.at[:, my_lanes], mask_row),
        )[i]
        return pltpu.make_async_copy(src, dst, core_sems.at[i - 3] if i in (6, 7, 8) else ext_send.at[i])

    for i in range(2):
        staged(i).start()
    tile_copy(0).start()

    barrier = pltpu.get_barrier_semaphore()

    @pl.loop(1, n)
    def _(d):
        pl.semaphore_signal(
            barrier, inc=1, device_id={"ctg": lax.rem(me + d, n)}, device_id_type=pl.DeviceIdType.MESH
        )

    for j in range(1, IN_FLIGHT):
        tile_copy(j).start()
    for i in range(2, 13):
        staged(i).start()

    omega[...] = jnp.ones_like(omega)
    price[...] = jnp.zeros_like(price)

    staged(0).wait()
    for k in range(ctgs):
        pattern_rows[k * halves:(k + 1) * halves, :] = pattern[k].astype(f32)
    for b in range(unit_count // 128):
        place = b * 128 % width
        gates[b * 128 // width, :, place:place + 128] = jnp.broadcast_to(
            pattern_rows[:, b:b + 1], (ctgs * halves, 128)
        )

    def frag_copy(c, target):
        return send(
            starts.at[:, :, pl.ds(pl.multiple_of(c * width, 128), width)],
            start_stage.at[home_row], frag_send.at[c], frag_recv.at[home_row], target,
        )

    def fin_copy(r, source_chunk, target):
        return send(
            frag_out.at[r], frag_in.at[source_chunk], frag_recv.at[r], frag_send.at[source_chunk], target
        )

    def stat_copy(slot, target_chip, sender_chip):
        return send(
            stats.at[slot, sender_chip], stats.at[slot, sender_chip],
            stat_send.at[target_chip], stat_recv.at[slot % 2, sender_chip], target_chip * 2 + 1,
        )

    def stat_start(slot):
        @pl.loop(1, chips)
        def _(d):
            stat_copy(slot, lax.rem(chip + d, chips), chip).start()

    def stat_wait(slot):
        @pl.loop(1, chips)
        def _(d):
            peer = lax.rem(chip + d, chips)
            stat_copy(slot, peer, chip).wait_send()
            stat_copy(slot, peer, peer).wait_recv()

    def flow_stat_copy(slot):
        return send(flow_stat.at[0], flow_stat.at[slot], core_sems.at[0], core_sems.at[1], partner)

    def omega_copy():
        return send(omega, omega, core_sems.at[2], core_sems.at[3], partner)

    def price_copy():
        return send(price, price, core_sems.at[4], core_sems.at[5], partner)

    def pair_copy(it, c):
        return send(pull_out.at[c], pair_in.at[it, c], pull_send.at[c * groups], pull_recv.at[c], partner)

    def pull_copy(it, src, target_chip, sender):
        c, g = lax.div(target_chip, groups), lax.rem(target_chip, groups)
        return send(
            src.at[c, block_rows(g)], pull_in.at[it, sender],
            pull_send.at[target_chip], pull_recv.at[sender], target_chip * 2 + 1,
        )

    def ext_copy(it, origin_chip, send_sem, target):
        c, g = lax.div(origin_chip, groups), lax.rem(origin_chip, groups)
        spot = ext_half.at[it, c, block_rows(g)]
        return send(spot, spot, send_sem, ext_recv.at[origin_chip], target)

    def ext_out(it, target):
        return ext_copy(it, chip, ext_send.at[target], target)

    def ext_pass(it, origin_chip):
        return ext_copy(it, origin_chip, ext_send.at[origin_chip * 2], partner)

    def halo_ext_copy(it, target):
        return send(extended.at[pl.ds(0, 8)], halo_ext.at[it], halo_sems.at[0], halo_sems.at[1], target)

    def halo_ramp_copy(it, target):
        return send(ramp.at[pl.ds(ROWS - 8, 8)], halo_ramp.at[it], halo_sems.at[2], halo_sems.at[3], target)

    def product(c):
        pull_out[c] = jnp.dot(dual_half[...], masked[c], preferred_element_type=f32).astype(bf16)

    def deliver(it, j):
        c = far_chunk(j)

        @pl.when((j < chunks // 2) & owner)
        def _():
            pair_copy(it, c).start()

        @pl.when(j >= chunks // 2)
        def _():
            for g in range(groups):
                target_chip = c * groups + g
                here = owner & (target_chip == chip)

                @pl.when(here)
                def _():
                    pull_in[it, me] = pull_out[c, g * ROWS:(g + 1) * ROWS, :]

                @pl.when(jnp.logical_not(here))
                def _():
                    pull_copy(it, pull_out, target_chip, me).start()

    def forward(it, j):
        @pl.when((j >= 0) & (j < chunks // 2) & jnp.logical_not(owner))
        def _():
            c = far_chunk(j)
            pair_copy(it, c).wait_recv()
            pull_sum[c] = (pull_out[c].astype(f32) + pair_in[it, c].astype(f32)).astype(bf16)
            for g in range(groups):
                pull_copy(it, pull_sum, c * groups + g, me).start()

    def pull_sent(it):
        @pl.loop(0, chunks)
        def _(j):
            c = far_chunk(j)
            paired = (j < chunks // 2) & owner

            @pl.when(paired)
            def _():
                pair_copy(it, c).wait_send()

            for g in range(groups):
                target_chip = c * groups + g
                here = owner & (target_chip == chip)

                @pl.when(jnp.logical_not(paired | here))
                def _():
                    pull_copy(it, pull_out, target_chip, me).wait_send()

    def mask(j):
        c = far_chunk(j)
        tile_copy(j).wait()

        @pl.when(j + IN_FLIGHT < chunks)
        def _():
            tile_copy(j + IN_FLIGHT).start()

        for r in range(ctgs * halves):
            gate = jnp.broadcast_to(gates[c, r:r + 1, :], (16, width)).astype(bf16)
            for q in range(8):
                where = slice(r * 128 + q * 16, r * 128 + q * 16 + 16)
                masked[c, where, :] = masked[c, where, :] * gate

    first_lag = 2

    @pl.loop(0, chunks + first_lag)
    def _(j):
        @pl.when(j < chunks)
        def _():
            mask(j)

        @pl.when(j == 0)
        def _():
            staged(1).wait()
            for k in range(ctgs):
                lanes = slice(k * lines, (k + 1) * lines)
                start_dual = dual_in[:, k, :]
                dual[:, lanes] = start_dual
                dual_half[:, lanes] = start_dual.astype(bf16)

        @pl.when(j < chunks)
        def _():
            product(far_chunk(j))

        @pl.when(j == 0)
        def _():
            for i in range(2, 6):
                staged(i).wait()
            for r in range(hour_rows):
                starts[3, r:r + 1] = jnp.broadcast_to(demand[0:1, r:r + 1], (1, unit_count))
            pl.semaphore_wait(barrier, n - 1)
            for c in range(chunks):
                target = (c * groups + home_group) * 2 + 1

                @pl.when(target != me)
                def _():
                    frag_copy(c, target).start()

                @pl.when(target == me)
                def _():
                    start_stage[home_row] = starts[:, :, c * width:(c + 1) * width]

        @pl.when(j < chunks)
        def _():
            deliver(0, j)

        forward(0, j - first_lag)

    for i in range(9, 13):
        staged(i).wait()

    block_row = lax.broadcasted_iota(jnp.int32, (ROWS, width), 0)
    lane_here = lax.broadcasted_iota(jnp.int32, (ROWS, 128), 1)
    row_here = lax.broadcasted_iota(jnp.int32, (ROWS, 128), 0) + my_group * ROWS
    diagonal = lane_here == row_here
    hour_lanes = lax.broadcasted_iota(jnp.int32, (1, 128), 1) < hours
    stat_row = lax.broadcasted_iota(jnp.int32, (4, 128), 0)

    def to_lanes(column):
        return jnp.sum(
            jnp.where(diagonal, jnp.broadcast_to(column, (ROWS, 128)), 0.0), axis=0, keepdims=True
        )

    def fold(x):
        rows, cols = x.shape
        out = None
        for r in range(0, rows, 8):
            for b in range(0, cols, 128):
                piece = x[r:r + 8, b:b + 128]
                out = piece if out is None else out + piece
        return jnp.sum(out, axis=0, keepdims=True)

    def halo_ramp_start(it):
        if groups > 1:
            @pl.when(my_group < groups - 1)
            def _():
                halo_ramp_copy(it, me + 2).start()

    @pl.when(owner)
    def _():
        for r in range(members):
            peer = my_group * members + r

            @pl.when(peer != me)
            def _():
                send(
                    starts.at[:, :, pl.ds(0, width)], start_stage.at[r],
                    frag_send.at[0], frag_recv.at[r], peer,
                ).wait_recv()

        demand_rows = []
        for r in range(members):
            rows = slice(r * hour_rows, (r + 1) * hour_rows)
            levels[rows, :] = start_stage[r, 0]
            cost[rows, :] = start_stage[r, 1]
            ramp[rows, :] = start_stage[r, 2]
            extended[rows, 0:128] = start_stage[r, 3, :, 0:128]
        lanes = to_lanes(extended[:, 0:1])
        mine = (stat_row == 0) & (jnp.full((4, 128), my_chunk) == 0)
        stats[0, chip] = jnp.where(mine, lanes, 0.0)
        stat_start(0)
        halo_ramp_start(0)

    for c in range(chunks):
        target = (c * groups + home_group) * 2 + 1

        @pl.when(target != me)
        def _():
            frag_copy(c, target).wait_send()

    def absorb(slot, sigma):
        total = stats[slot, 0]
        for q in range(1, chips):
            total = total + stats[slot, q]
        move = sigma * (balance * (total[0:1] - price[1:2]))
        move = jnp.where(hour_lanes, move, 0.0)
        price[0:1] = price[0:1] + move
        return total, jnp.sum(move * move, axis=1, keepdims=True)

    def primal(it):
        @pl.when(it > 0)
        def _():
            stat_wait(it)

        @pl.when(it > 0)
        def _():
            old = omega[0:1, 0:1]
            total, price_sq = absorb(it, step_size * old)
            sums = jnp.sum(total, axis=1, keepdims=True)
            dual_sq = sums[3:4] + sums[2:3] + price_sq
            ratio = (dual_sq + 1e-06) / (sums[1:2] + 1e-06)
            omega[...] = jnp.broadcast_to(jnp.sqrt(old) * jnp.sqrt(jnp.sqrt(ratio)), omega.shape)
            omega_copy().start()

        weight = omega[0:1, 0:1]
        tau = step_size / weight
        sigma = step_size * weight

        if groups > 1:
            @pl.when(my_group < groups - 1)
            def _():
                halo_ramp_copy(it, me + 2).wait_send()

            @pl.when(my_group > 0)
            def _():
                halo_ramp_copy(it, me - 2).wait_recv()

            @pl.when(my_group == 0)
            def _():
                halo_ramp[it] = jnp.zeros_like(halo_ramp[it])

            edge_ramp = halo_ramp[it][7:8]
        else:
            edge_ramp = jnp.zeros((1, width), f32)

        floor = unit_rows[0]
        ceiling = floor + unit_rows[1]
        ramp_limit = unit_rows[2]
        ramp_on = mask_row[...].astype(f32)
        ramp_now = ramp[...]
        before = jnp.where(block_row == 0, edge_ramp, pltpu.roll(ramp_now, 1, 0))
        price_here = jnp.sum(
            jnp.where(diagonal, jnp.broadcast_to(price[0:1], (ROWS, 128)), 0.0), axis=1, keepdims=True
        )
        known = cost[...] + ramp_on * (before - ramp_now) + balance * price_here

        first_near = lax.div(my_pair, pairs // 2) * (chips // 2)

        @pl.loop(0, chips)
        def _(q):
            pull_copy(it, pull_out, q, q * 2).wait_recv()

        @pl.loop(0, chips // 2)
        def _(q):
            @pl.when(first_near + q != chip)
            def _():
                pull_copy(it, pull_out, q, (first_near + q) * 2 + 1).wait_recv()

        pulled = pull_in[it, 0].astype(f32)
        for q in range(1, chips):
            pulled = pulled + pull_in[it, q * 2].astype(f32)
        for q in range(chips // 2):
            pulled = pulled + pull_in[it, (first_near + q) * 2 + 1].astype(f32)

        gradient = known + pulled
        old_levels = levels[...]
        moved = jnp.clip(old_levels - tau * gradient, floor, ceiling)
        ext = 2.0 * moved - old_levels
        levels[...] = moved
        ext_half[it, my_chunk, my_rows, :] = ext.astype(bf16)
        extended[...] = ext

        @pl.loop(0, chunks)
        def _(j):
            c = far_chunk(j)
            for g in range(groups):
                other = c * groups + g

                @pl.when(other != chip)
                def _():
                    ext_out(it, other * 2 + 1).start()

                @pl.when(both_cores(c))
                def _():
                    ext_out(it, other * 2).start()

        if groups > 1:
            @pl.when(my_group > 0)
            def _():
                halo_ext_copy(it, me - 2).start()
                halo_ext_copy(it, me - 2).wait_send()

            @pl.when(my_group < groups - 1)
            def _():
                halo_ext_copy(it, me + 2).wait_recv()

            @pl.when(my_group == groups - 1)
            def _():
                halo_ext[it] = jnp.zeros_like(halo_ext[it])

            edge_ext = halo_ext[it][0:1]
        else:
            edge_ext = jnp.zeros((1, width), f32)

        after = jnp.where(block_row == ROWS - 1, edge_ext, pltpu.roll(ext, ROWS - 1, 0))
        change = ramp_on * (after - ext)
        last_hour = block_row + my_group * ROWS == hours - 1
        change = jnp.where(last_hour, 0.0, change)
        trial = ramp_now + sigma * change
        ramp_new = trial - jnp.clip(trial, -sigma * ramp_limit, sigma * ramp_limit)
        ramp[...] = ramp_new

        row_sums = to_lanes(jnp.sum(ext, axis=1, keepdims=True))
        primal_sq = fold((moved - old_levels) ** 2)
        ramp_sq = fold((ramp_new - ramp_now) ** 2)
        stats[it + 1, chip] = jnp.where(
            stat_row == 0, row_sums,
            jnp.where(stat_row == 1, primal_sq, jnp.where(stat_row == 2, ramp_sq, 0.0)),
        )

        @pl.when(it == ITERS - 1)
        def _():
            stat_start(it + 1)
            for r in range(members):
                rows = slice(r * hour_rows, (r + 1) * hour_rows)
                frag_out[r, 0] = moved[rows, :]
                frag_out[r, 1] = ramp_new[rows, :]
            for r in range(members):
                target = my_group * members + r

                @pl.when(target != me)
                def _():
                    fin_copy(r, my_chunk, target).start()

                @pl.when(target == me)
                def _():
                    frag_in[my_chunk] = frag_out[r]

    def line_limits():
        for i in range(6, 9):
            staged(i).wait()

        row_iota = lax.broadcasted_iota(jnp.int32, (128, lines), 0)
        values = table[...].T
        part_a = values.astype(bf16)
        rest = values - part_a.astype(f32)
        part_b = rest.astype(bf16)
        part_c = (rest - part_b.astype(f32)).astype(bf16)
        for k in range(ctgs):
            which = index[k:k + 1, :]
            high = lax.shift_right_logical(which, 7)
            low = lax.bitwise_and(which, 127)
            blocks = table.shape[0] // 128
            got = jnp.zeros((128, lines), f32)
            for b in range(blocks):
                pick = jnp.where(row_iota + b * 128 == high, 1.0, 0.0).astype(bf16)
                for part in (part_a, part_b, part_c):
                    got = got + jnp.dot(part[:, b * 128:(b + 1) * 128], pick, preferred_element_type=f32)
            limit[:, k * lines:(k + 1) * lines] = jnp.sum(
                jnp.where(row_iota == low, got, 0.0), axis=0, keepdims=True
            )
            base[:, k * lines:(k + 1) * lines] = base_in[:, k, :]

    def take(it, c):
        for g in range(groups):
            other = c * groups + g

            @pl.when(jnp.logical_not(owner & (other == chip)))
            def _():
                ext_pass(it, other).wait_recv()

    def take_and_pass(it, c):
        take(it, c)

        @pl.when(owner & jnp.logical_not(both_cores(c)))
        def _():
            for g in range(groups):
                ext_pass(it, c * groups + g).start()

    def flow(x, w):
        return lax.dot_general(x, w, (((1,), (1,)), ((), ())), preferred_element_type=f32)

    def small_out(i):
        src, dst = ((price, out_price), (starts.at[0], out_levels), (starts.at[1], out_ramp))[i]
        return pltpu.make_async_copy(src, dst, pull_recv.at[i])

    def write_small():
        @pl.when(owner)
        def _():
            stat_wait(ITERS)
            absorb(ITERS, step_size * omega[0:1, 0:1])
            price_copy().start()

        for c in range(chunks):
            peer = (c * groups + home_group) * 2 + 1

            @pl.when(peer != me)
            def _():
                fin_copy(0, c, peer).wait_recv()

        for c in range(chunks):
            for which in range(2):
                starts[which, :, c * width:(c + 1) * width] = frag_in[c, which]
        small_out(1).start()
        small_out(2).start()

    turns = (chunks - 1) // 2
    blocks = ctgs * lines // 256

    def turn(first, last):
        @pl.loop(first * blocks, last * blocks)
        def _(i):
            j = lax.div(i, blocks)
            block = pl.ds(pl.multiple_of(lax.rem(i, blocks) * 256, 256), 256)
            turned[j, :, block] = masked[far_chunk(j), block, :].T

    @pl.loop(0, ITERS)
    def _(it):
        @pl.when(it > 0)
        def _():
            @pl.loop(0, chunks)
            def _(j):
                product(far_chunk(j))
                deliver(it, j)

                @pl.when((j == STAT) & owner)
                def _():
                    halo_ramp_start(it)
                    flow_stat_copy(it).wait_recv()
                    stats[it, chip, 3:4] = stats[it, chip, 3:4] + flow_stat[it, 0:1]
                    stat_start(it)

                forward(it, j - LAG)

            @pl.when(it == 1)
            def _():
                turn(1, turns)

            @pl.when(it == 2)
            def _():
                turn(turns + 1, 2 * turns - 1)

        @pl.when(it == 0)
        def _():
            turn(0, 1)

        pull_sent(it)

        @pl.when(owner)
        def _():
            primal(it)

        take(it, my_chunk)
        flow_acc[...] = flow(ext_half[it, my_chunk], masked[my_chunk])

        @pl.when(it == 0)
        def _():
            line_limits()

        @pl.when(it == 1)
        def _():
            turn(turns, turns + 1)

        @pl.when(it == 2)
        def _():
            turn(2 * turns - 1, 2 * turns)

        near = my_pair * 2 + 1 - my_side
        take_and_pass(it, near)
        flow_acc[...] += flow(ext_half[it, near], masked[near])

        @pl.loop(1, pairs + AHEAD)
        def _(j):
            @pl.when(j < pairs)
            def _():
                c = near_pair(j) * 2
                take_and_pass(it, c)
                take_and_pass(it, c + 1)

            @pl.when((it == ITERS - 1) & (j == pairs))
            def _():
                write_small()

            @pl.when(j > AHEAD)
            def _():
                place = (pairs - 1 - j + AHEAD) * 2
                c, d = far_chunk(place), far_chunk(place + 1)
                x = jnp.concatenate([ext_half[it, c], ext_half[it, d]], axis=1)
                ready = (it > 1) | ((it == 1) & (place <= turns - 1))

                @pl.when(ready)
                def _():
                    w = jnp.concatenate([turned[place], turned[place + 1]], axis=0)
                    flow_acc[...] += jnp.dot(x, w, preferred_element_type=f32)

                @pl.when(jnp.logical_not(ready))
                def _():
                    w = jnp.concatenate([masked[c], masked[d]], axis=1)
                    flow_acc[...] += flow(x, w)

        @pl.when(owner)
        def _():
            @pl.loop(0, chunks)
            def _(c):
                for g in range(groups):
                    other = c * groups + g

                    @pl.when(other != chip)
                    def _():
                        ext_out(it, other * 2 + 1).wait_send()

                    @pl.when(both_cores(c))
                    def _():
                        ext_out(it, other * 2).wait_send()

                    @pl.when(jnp.logical_not(both_cores(c)))
                    def _():
                        ext_pass(it, other).wait_send()

            @pl.when(it > 0)
            def _():
                omega_copy().wait_send()

        @pl.when((it == 0) & owner)
        def _():
            stat_wait(0)
            first = stats[0, 0]
            for q in range(1, chips):
                first = first + stats[0, q]
            price[1:2] = first[0:1]

        @pl.when((it > 0) & jnp.logical_not(owner))
        def _():
            omega_copy().wait_recv()

        @pl.when(it == ITERS - 1)
        def _():
            @pl.when(jnp.logical_not(owner))
            def _():
                price_copy().wait_recv()

            small_out(0).start()

        sigma = step_size * omega[0:1, 0:1]
        old_dual = dual[...]
        trial = old_dual + sigma * flow_acc[...]
        bound = limit[...]
        dual_new = trial - jnp.clip(trial, sigma * (base[...] - bound), sigma * (base[...] + bound))
        dual[...] = dual_new
        dual_half[...] = dual_new.astype(bf16)

        @pl.when(it < ITERS - 1)
        def _():
            flow_sq = fold((dual_new - old_dual) ** 2)

            @pl.when(owner)
            def _():
                stats[it + 1, chip, 3:4] = flow_sq

            @pl.when(jnp.logical_not(owner))
            def _():
                @pl.when(it > 0)
                def _():
                    flow_stat_copy(it).wait_send()

                flow_stat[0] = jnp.broadcast_to(flow_sq, (8, 128))
                flow_stat_copy(it + 1).start()

    dual_out = pltpu.make_async_copy(dual, out_dual, ext_send.at[0])
    dual_out.start()

    @pl.when(owner)
    def _():
        for r in range(members):
            target = my_group * members + r

            @pl.when(target != me)
            def _():
                fin_copy(r, my_chunk, target).wait_send()

        price_copy().wait_send()

    @pl.when(jnp.logical_not(owner))
    def _():
        flow_stat_copy(0).wait_send()

    for i in range(3):
        small_out(i).wait()
    dual_out.wait()


def finish(
    levels, dual, ramp, price, out_levels, out_dual, out_ramp, out_price,
    level_box, dual_box, tile_box, ramp_box, price_box, own_price, in_sem, out_sem,
):
    hours, ctgs, lines = out_dual.shape
    hour_rows = own_price.shape[1]
    pieces = hours // 8

    def dual_in(p):
        return pltpu.make_async_copy(dual.at[p * 8:p * 8 + 8], dual_box.at[p], in_sem.at[3 + p])

    def dual_out(p):
        return pltpu.make_async_copy(tile_box.at[p], out_dual.at[p * 8:p * 8 + 8], out_sem.at[3 + p])

    small_in = (
        pltpu.make_async_copy(price, price_box, in_sem.at[0]),
        pltpu.make_async_copy(levels, level_box, in_sem.at[1]),
        pltpu.make_async_copy(ramp, ramp_box, in_sem.at[2]),
    )
    small_out = (
        pltpu.make_async_copy(own_price, out_price, out_sem.at[0]),
        pltpu.make_async_copy(level_box, out_levels, out_sem.at[1]),
        pltpu.make_async_copy(ramp_box, out_ramp, out_sem.at[2]),
    )
    for p in range(pieces):
        dual_in(p).start()
    for copy in small_in:
        copy.start()
    for p in range(pieces):
        dual_in(p).wait()
        for k in range(ctgs):
            tile_box[p, :, k, :] = dual_box[p, :, k * lines:(k + 1) * lines]
        dual_out(p).start()
    small_in[0].wait()
    lane = lax.broadcasted_iota(jnp.int32, (1, 128), 1) - lax.axis_index("ctg") * hour_rows
    for r in range(hour_rows):
        own_price[0:1, r:r + 1] = jnp.sum(
            jnp.where(lane == r, price_box[0:1], 0.0), axis=1, keepdims=True
        )
    small_out[0].start()
    for i in (1, 2):
        small_in[i].wait()
        small_out[i].start()
    for p in range(pieces):
        dual_out(p).wait()
    for copy in small_out:
        copy.wait()


def body(
    flow_tiles,
    tile_pattern,
    monitored,
    ratings,
    base_flow,
    unit_cost,
    unit_floor,
    unit_span,
    ramp_limit,
    ramp_mask,
    demand,
    start_output,
    start_flow_dual,
    start_ramp_dual,
):
    f32, bf16 = jnp.float32, jnp.bfloat16
    ctgs, lines, unit_count = flow_tiles.shape
    n = lax.axis_size("ctg")
    hour_rows = start_output.shape[0]
    hours = hour_rows * n
    groups = hours // ROWS
    chips = n // 2
    chunks = chips // groups
    members = ROWS // hour_rows
    width = unit_count // chunks
    flat = ctgs * lines
    step_size = 0.5 / (2.0 + math.sqrt(ctgs * n * lines / unit_count))
    balance = 1.0 / math.sqrt(unit_count)

    gate_rows = ctgs * tile_pattern.shape[1]

    vmem = pl.BlockSpec(memory_space=pltpu.VMEM)
    hbm = pl.BlockSpec(memory_space=pl.ANY)
    sem = pltpu.SemaphoreType.DMA
    out = pl.pallas_call(
        functools.partial(kernel, n, hour_rows, step_size, balance),
        out_shape=(
            jax.ShapeDtypeStruct((hour_rows, unit_count), f32),
            jax.ShapeDtypeStruct((hours, flat), f32),
            jax.ShapeDtypeStruct((hour_rows, unit_count), f32),
            jax.ShapeDtypeStruct((8, 128), f32),
        ),
        in_specs=[hbm] * 14,
        out_specs=(hbm,) * 4,
        scratch_shapes=[
            pltpu.VMEM((chunks, flat, width), bf16),
            pltpu.VMEM((chunks - 2, width, flat), bf16),
            pltpu.VMEM((chunks, gate_rows, width), f32),
            pltpu.VMEM(tile_pattern.shape, jnp.int32),
            pltpu.VMEM((gate_rows, tile_pattern.shape[2]), f32),
            pltpu.VMEM(monitored.shape, jnp.int32),
            pltpu.VMEM((ratings.shape[0] // 128, 128), f32),
            pltpu.VMEM(base_flow.shape, f32),
            pltpu.VMEM(start_flow_dual.shape, f32),
            pltpu.VMEM((3, 1, width), f32),
            pltpu.VMEM((1, width), jnp.int32),
            pltpu.VMEM((1, hour_rows), f32),
            pltpu.VMEM((hours, flat), f32),
            pltpu.VMEM((hours, flat), f32),
            pltpu.VMEM((4, hour_rows, unit_count), f32),
            pltpu.VMEM((1, flat), f32),
            pltpu.VMEM((hours, flat), bf16),
            pltpu.VMEM((hours, flat), f32),
            pltpu.VMEM((members, 4, hour_rows, width), f32),
            pltpu.VMEM((chunks, 2, hour_rows, width), f32),
            pltpu.VMEM((members, 2, hour_rows, width), f32),
            pltpu.VMEM((ROWS, width), f32),
            pltpu.VMEM((ROWS, width), f32),
            pltpu.VMEM((ROWS, width), f32),
            pltpu.VMEM((ROWS, width), f32),
            pltpu.VMEM((ITERS, 8, width), f32),
            pltpu.VMEM((ITERS, 8, width), f32),
            pltpu.VMEM((chunks, hours, width), bf16),
            pltpu.VMEM((ITERS, chunks, hours, width), bf16),
            pltpu.VMEM((chunks, hours, width), bf16),
            pltpu.VMEM((ITERS, n, ROWS, width), bf16),
            pltpu.VMEM((ITERS, chunks, hours, width), bf16),
            pltpu.VMEM((ITERS + 1, chips, 4, 128), f32),
            pltpu.VMEM((ITERS, 8, 128), f32),
            pltpu.VMEM((8, 128), f32),
            pltpu.VMEM((8, 128), f32),
            sem((chunks,)), sem((members,)), sem((chips,)), sem((n,)),
            sem((n,)), sem((chips,)), sem((max(chips, chunks),)), sem((2, chips)),
            sem((6,)), sem((4,)),
        ],
        compiler_params=pltpu.CompilerParams(collective_id=0, has_side_effects=True),
    )(
        flow_tiles.reshape(flat, unit_count),
        tile_pattern,
        monitored,
        ratings.reshape(-1, 128),
        base_flow,
        start_flow_dual,
        start_output,
        unit_cost,
        start_ramp_dual,
        demand[None],
        unit_floor[None],
        unit_span[None],
        ramp_limit[None],
        ramp_mask[None],
    )
    levels, dual, ramp, price = pl.pallas_call(
        finish,
        out_shape=(
            jax.ShapeDtypeStruct((hour_rows, unit_count), f32),
            jax.ShapeDtypeStruct((hours, ctgs, lines), f32),
            jax.ShapeDtypeStruct((hour_rows, unit_count), f32),
            jax.ShapeDtypeStruct((1, hour_rows), f32),
        ),
        in_specs=[hbm] * 4,
        out_specs=(hbm,) * 4,
        scratch_shapes=[
            pltpu.VMEM((hour_rows, unit_count), f32),
            pltpu.VMEM((hours // 8, 8, flat), f32),
            pltpu.VMEM((hours // 8, 8, ctgs, lines), f32),
            pltpu.VMEM((hour_rows, unit_count), f32),
            pltpu.VMEM((8, 128), f32),
            pltpu.VMEM((1, hour_rows), f32),
            sem((3 + hours // 8,)),
            sem((3 + hours // 8,)),
        ],
    )(*out)
    return levels, dual, ramp, price.reshape(hour_rows)


def solution(mesh):
    return jax.shard_map(
        body,
        mesh=mesh,
        in_specs=(
            P("ctg", None, None),
            P("ctg", None, None),
            P("ctg", None),
            P(),
            P("grp", "ctg", None),
            P(("grp", "ctg"), None),
            P(),
            P(),
            P(),
            P(),
            P(("grp", "ctg")),
            P(("grp", "ctg"), None),
            P("grp", "ctg", None),
            P(("grp", "ctg"), None),
        ),
        out_specs=(
            P(("grp", "ctg"), None),
            P("grp", "ctg", None),
            P(("grp", "ctg"), None),
            P(("grp", "ctg")),
        ),
        check_vma=False,
    )
```

```python
import functools
import math

import jax
import jax.numpy as jnp
from jax import lax
from jax.experimental import pallas as pl
from jax.experimental.pallas import tpu as pltpu
from jax.sharding import PartitionSpec as P

ITERS = 4
ROWS = 32
STAT = 5
LAG = 0
AHEAD = 1
IN_FLIGHT = 3


def send(src, dst, send_sem, recv_sem, target):
    return pltpu.make_async_remote_copy(
        src_ref=src,
        dst_ref=dst,
        send_sem=send_sem,
        recv_sem=recv_sem,
        device_id={"ctg": target},
        device_id_type=pl.DeviceIdType.MESH,
    )


def kernel(
    n, hour_rows, step_size, balance,
    tiles, pattern_hbm, index_hbm, table_hbm, base_hbm, dual_hbm, level_hbm, cost_hbm, ramp_hbm, demand_hbm,
    floor_hbm, span_hbm, ramp_limit_hbm, ramp_mask_hbm,
    out_levels, out_dual, out_ramp, out_price,
    masked, turned, gates, pattern, pattern_rows, index, table, base_in, dual_in, unit_rows, mask_row, demand,
    dual, base, starts, limit, dual_half, flow_acc,
    start_stage, frag_in, frag_out,
    cost, levels, ramp, extended, halo_ext, halo_ramp,
    pull_out, pair_in, pull_sum, pull_in, ext_half, stats, flow_stat, price, omega,
    frag_send, frag_recv, pull_send, pull_recv, ext_send, ext_recv, stat_send, stat_recv,
    core_sems, halo_sems,
):
    f32 = jnp.float32
    bf16 = jnp.bfloat16
    chips = n // 2
    members = ROWS // hour_rows
    groups = n // members
    chunks = chips // groups
    unit_count = tiles.shape[1]
    width = unit_count // chunks
    ctgs, lines = base_in.shape[1], base_in.shape[2]
    hours = groups * ROWS
    pairs = chunks // 2
    halves = lines // 128

    me = lax.axis_index("ctg")
    core = lax.rem(me, 2)
    chip = lax.div(me, 2)
    owner = core == 1
    partner = me + 1 - 2 * core
    my_chunk = lax.div(chip, groups)
    my_group = lax.rem(chip, groups)
    home_group = lax.div(me, members)
    home_row = lax.rem(me, members)
    my_pair = lax.div(my_chunk, 2)
    my_side = lax.rem(my_chunk, 2)
    my_rows = pl.ds(pl.multiple_of(my_group * ROWS, ROWS), ROWS)
    my_lanes = pl.ds(pl.multiple_of(my_chunk * width, 128), width)

    ahead = 1 - lax.div(my_pair, pairs // 2)

    def flip(place, length):
        return ahead * (length - 1 - place) + (1 - ahead) * place

    def skip(place, own, length):
        return place + lax.div(place + length - own, length)

    def far_pair(j):
        last = lax.div(j + 1, pairs)
        place = flip(skip(j, flip(my_pair, pairs), pairs), pairs)
        return last * my_pair + (1 - last) * place

    def near_pair(j):
        return far_pair(pairs - 1 - j)

    def far_chunk(j):
        second = lax.rem(j, 2)
        side = second * my_side + (1 - second) * (1 - my_side)
        return far_pair(lax.div(j, 2)) * 2 + side

    def sums_here(j):
        return (j >= EARLY) == owner

    def both_cores(c):
        return c == my_chunk

    def block_rows(g):
        return pl.ds(pl.multiple_of(g * ROWS, ROWS), ROWS)

    def tile_copy(j):
        c = far_chunk(j)
        return pltpu.make_async_copy(
            tiles.at[:, pl.ds(pl.multiple_of(c * width, 128), width)], masked.at[c], stat_send.at[j]
        )

    def staged(i):
        src, dst = (
            (pattern_hbm, pattern),
            (dual_hbm, dual_in),
            (demand_hbm, demand),
            (level_hbm, starts.at[0]),
            (cost_hbm, starts.at[1]),
            (ramp_hbm, starts.at[2]),
            (index_hbm, index),
            (table_hbm, table),
            (base_hbm, base_in),
            (floor_hbm.at[:, my_lanes], unit_rows.at[0]),
            (span_hbm.at[:, my_lanes], unit_rows.at[1]),
            (ramp_limit_hbm.at[:, my_lanes], unit_rows.at[2]),
            (ramp_mask_hbm.at[:, my_lanes], mask_row),
        )[i]
        return pltpu.make_async_copy(src, dst, core_sems.at[i - 3] if i in (6, 7, 8) else ext_send.at[i])

    for i in range(2):
        staged(i).start()
    tile_copy(0).start()

    barrier = pltpu.get_barrier_semaphore()

    @pl.loop(1, n)
    def _(d):
        pl.semaphore_signal(
            barrier, inc=1, device_id={"ctg": lax.rem(me + d, n)}, device_id_type=pl.DeviceIdType.MESH
        )

    for j in range(1, IN_FLIGHT):
        tile_copy(j).start()
    for i in range(2, 13):
        staged(i).start()

    omega[...] = jnp.ones_like(omega)
    price[...] = jnp.zeros_like(price)

    staged(0).wait()
    for k in range(ctgs):
        pattern_rows[k * halves:(k + 1) * halves, :] = pattern[k].astype(f32)
    for b in range(unit_count // 128):
        place = b * 128 % width
        gates[b * 128 // width, :, place:place + 128] = jnp.broadcast_to(
            pattern_rows[:, b:b + 1], (ctgs * halves, 128)
        )

    def frag_copy(c, target):
        return send(
            starts.at[:, :, pl.ds(pl.multiple_of(c * width, 128), width)],
            start_stage.at[home_row], frag_send.at[c], frag_recv.at[home_row], target,
        )

    def fin_copy(r, source_chunk, target):
        return send(
            frag_out.at[r], frag_in.at[source_chunk], frag_recv.at[r], frag_send.at[source_chunk], target
        )

    def stat_copy(slot, target_chip, sender_chip):
        return send(
            stats.at[slot, sender_chip], stats.at[slot, sender_chip],
            stat_send.at[target_chip], stat_recv.at[slot % 2, sender_chip], target_chip * 2 + 1,
        )

    def stat_start(slot):
        @pl.loop(1, chips)
        def _(d):
            stat_copy(slot, lax.rem(chip + d, chips), chip).start()

    def stat_wait(slot):
        @pl.loop(1, chips)
        def _(d):
            peer = lax.rem(chip + d, chips)
            stat_copy(slot, peer, chip).wait_send()
            stat_copy(slot, peer, peer).wait_recv()

    def flow_stat_copy(slot):
        return send(flow_stat.at[0], flow_stat.at[slot], core_sems.at[0], core_sems.at[1], partner)

    def omega_copy():
        return send(omega, omega, core_sems.at[2], core_sems.at[3], partner)

    def price_copy():
        return send(price, price, core_sems.at[4], core_sems.at[5], partner)

    def pair_copy(it, c):
        return send(pull_out.at[c], pair_in.at[it, c], pull_send.at[c * groups], pull_recv.at[c], partner)

    def pull_copy(it, src, target_chip, sender):
        c, g = lax.div(target_chip, groups), lax.rem(target_chip, groups)
        return send(
            src.at[c, block_rows(g)], pull_in.at[it, sender],
            pull_send.at[target_chip], pull_recv.at[sender], target_chip * 2 + 1,
        )

    def ext_copy(it, origin_chip, send_sem, target):
        c, g = lax.div(origin_chip, groups), lax.rem(origin_chip, groups)
        spot = ext_half.at[it, c, block_rows(g)]
        return send(spot, spot, send_sem, ext_recv.at[origin_chip], target)

    def ext_out(it, target):
        return ext_copy(it, chip, ext_send.at[target], target)

    def ext_pass(it, origin_chip):
        return ext_copy(it, origin_chip, ext_send.at[origin_chip * 2], partner)

    def halo_ext_copy(it, target):
        return send(extended.at[pl.ds(0, 8)], halo_ext.at[it], halo_sems.at[0], halo_sems.at[1], target)

    def halo_ramp_copy(it, target):
        return send(ramp.at[pl.ds(ROWS - 8, 8)], halo_ramp.at[it], halo_sems.at[2], halo_sems.at[3], target)

    def product(c):
        pull_out[c] = jnp.dot(dual_half[...], masked[c], preferred_element_type=f32).astype(bf16)

    def deliver(it, j):
        c = far_chunk(j)

        @pl.when((j < chunks // 2) & owner)
        def _():
            pair_copy(it, c).start()

        @pl.when(j >= chunks // 2)
        def _():
            for g in range(groups):
                target_chip = c * groups + g
                here = owner & (target_chip == chip)

                @pl.when(here)
                def _():
                    pull_in[it, me] = pull_out[c, g * ROWS:(g + 1) * ROWS, :]

                @pl.when(jnp.logical_not(here))
                def _():
                    pull_copy(it, pull_out, target_chip, me).start()

    def forward(it, j):
        @pl.when((j >= 0) & (j < chunks // 2) & jnp.logical_not(owner))
        def _():
            c = far_chunk(j)
            pair_copy(it, c).wait_recv()
            pull_sum[c] = (pull_out[c].astype(f32) + pair_in[it, c].astype(f32)).astype(bf16)
            for g in range(groups):
                pull_copy(it, pull_sum, c * groups + g, me).start()

    def pull_sent(it):
        @pl.loop(0, chunks)
        def _(j):
            c = far_chunk(j)
            paired = (j < chunks // 2) & owner

            @pl.when(paired)
            def _():
                pair_copy(it, c).wait_send()

            for g in range(groups):
                target_chip = c * groups + g
                here = owner & (target_chip == chip)

                @pl.when(jnp.logical_not(paired | here))
                def _():
                    pull_copy(it, pull_out, target_chip, me).wait_send()

    def mask(j):
        c = far_chunk(j)
        tile_copy(j).wait()

        @pl.when(j + IN_FLIGHT < chunks)
        def _():
            tile_copy(j + IN_FLIGHT).start()

        for r in range(ctgs * halves):
            gate = jnp.broadcast_to(gates[c, r:r + 1, :], (16, width)).astype(bf16)
            for q in range(8):
                where = slice(r * 128 + q * 16, r * 128 + q * 16 + 16)
                masked[c, where, :] = masked[c, where, :] * gate

    first_lag = 2

    @pl.loop(0, chunks + first_lag)
    def _(j):
        @pl.when(j < chunks)
        def _():
            mask(j)

        @pl.when(j == 0)
        def _():
            staged(1).wait()
            for k in range(ctgs):
                lanes = slice(k * lines, (k + 1) * lines)
                start_dual = dual_in[:, k, :]
                dual[:, lanes] = start_dual
                dual_half[:, lanes] = start_dual.astype(bf16)

        @pl.when(j < chunks)
        def _():
            product(far_chunk(j))

        @pl.when(j == 0)
        def _():
            for i in range(2, 6):
                staged(i).wait()
            for r in range(hour_rows):
                starts[3, r:r + 1] = jnp.broadcast_to(demand[0:1, r:r + 1], (1, unit_count))
            pl.semaphore_wait(barrier, n - 1)
            for c in range(chunks):
                target = (c * groups + home_group) * 2 + 1

                @pl.when(target != me)
                def _():
                    frag_copy(c, target).start()

                @pl.when(target == me)
                def _():
                    start_stage[home_row] = starts[:, :, c * width:(c + 1) * width]

        @pl.when(j < chunks)
        def _():
            deliver(0, j)

        forward(0, j - first_lag)

    for i in range(9, 13):
        staged(i).wait()

    block_row = lax.broadcasted_iota(jnp.int32, (ROWS, width), 0)
    lane_here = lax.broadcasted_iota(jnp.int32, (ROWS, 128), 1)
    row_here = lax.broadcasted_iota(jnp.int32, (ROWS, 128), 0) + my_group * ROWS
    diagonal = lane_here == row_here
    hour_lanes = lax.broadcasted_iota(jnp.int32, (1, 128), 1) < hours
    stat_row = lax.broadcasted_iota(jnp.int32, (4, 128), 0)

    def to_lanes(column):
        return jnp.sum(
            jnp.where(diagonal, jnp.broadcast_to(column, (ROWS, 128)), 0.0), axis=0, keepdims=True
        )

    def fold(x):
        rows, cols = x.shape
        out = None
        for r in range(0, rows, 8):
            for b in range(0, cols, 128):
                piece = x[r:r + 8, b:b + 128]
                out = piece if out is None else out + piece
        return jnp.sum(out, axis=0, keepdims=True)

    def halo_ramp_start(it):
        if groups > 1:
            @pl.when(my_group < groups - 1)
            def _():
                halo_ramp_copy(it, me + 2).start()

    @pl.when(owner)
    def _():
        for r in range(members):
            peer = my_group * members + r

            @pl.when(peer != me)
            def _():
                send(
                    starts.at[:, :, pl.ds(0, width)], start_stage.at[r],
                    frag_send.at[0], frag_recv.at[r], peer,
                ).wait_recv()

        demand_rows = []
        for r in range(members):
            rows = slice(r * hour_rows, (r + 1) * hour_rows)
            levels[rows, :] = start_stage[r, 0]
            cost[rows, :] = start_stage[r, 1]
            ramp[rows, :] = start_stage[r, 2]
            extended[rows, 0:128] = start_stage[r, 3, :, 0:128]
        lanes = to_lanes(extended[:, 0:1])
        mine = (stat_row == 0) & (jnp.full((4, 128), my_chunk) == 0)
        stats[0, chip] = jnp.where(mine, lanes, 0.0)
        stat_start(0)
        halo_ramp_start(0)

    for c in range(chunks):
        target = (c * groups + home_group) * 2 + 1

        @pl.when(target != me)
        def _():
            frag_copy(c, target).wait_send()

    def absorb(slot, sigma):
        total = stats[slot, 0]
        for q in range(1, chips):
            total = total + stats[slot, q]
        move = sigma * (balance * (total[0:1] - price[1:2]))
        move = jnp.where(hour_lanes, move, 0.0)
        price[0:1] = price[0:1] + move
        return total, jnp.sum(move * move, axis=1, keepdims=True)

    def primal(it):
        @pl.when(it > 0)
        def _():
            stat_wait(it)

        @pl.when(it > 0)
        def _():
            old = omega[0:1, 0:1]
            total, price_sq = absorb(it, step_size * old)
            sums = jnp.sum(total, axis=1, keepdims=True)
            dual_sq = sums[3:4] + sums[2:3] + price_sq
            ratio = (dual_sq + 1e-06) / (sums[1:2] + 1e-06)
            omega[...] = jnp.broadcast_to(jnp.sqrt(old) * jnp.sqrt(jnp.sqrt(ratio)), omega.shape)
            omega_copy().start()

        weight = omega[0:1, 0:1]
        tau = step_size / weight
        sigma = step_size * weight

        if groups > 1:
            @pl.when(my_group < groups - 1)
            def _():
                halo_ramp_copy(it, me + 2).wait_send()

            @pl.when(my_group > 0)
            def _():
                halo_ramp_copy(it, me - 2).wait_recv()

            @pl.when(my_group == 0)
            def _():
                halo_ramp[it] = jnp.zeros_like(halo_ramp[it])

            edge_ramp = halo_ramp[it][7:8]
        else:
            edge_ramp = jnp.zeros((1, width), f32)

        floor = unit_rows[0]
        ceiling = floor + unit_rows[1]
        ramp_limit = unit_rows[2]
        ramp_on = mask_row[...].astype(f32)
        ramp_now = ramp[...]
        before = jnp.where(block_row == 0, edge_ramp, pltpu.roll(ramp_now, 1, 0))
        price_here = jnp.sum(
            jnp.where(diagonal, jnp.broadcast_to(price[0:1], (ROWS, 128)), 0.0), axis=1, keepdims=True
        )
        known = cost[...] + ramp_on * (before - ramp_now) + balance * price_here

        first_near = lax.div(my_pair, pairs // 2) * (chips // 2)

        @pl.loop(0, chips)
        def _(q):
            pull_copy(it, pull_out, q, q * 2).wait_recv()

        @pl.loop(0, chips // 2)
        def _(q):
            @pl.when(first_near + q != chip)
            def _():
                pull_copy(it, pull_out, q, (first_near + q) * 2 + 1).wait_recv()

        pulled = pull_in[it, 0].astype(f32)
        for q in range(1, chips):
            pulled = pulled + pull_in[it, q * 2].astype(f32)
        for q in range(chips // 2):
            pulled = pulled + pull_in[it, (first_near + q) * 2 + 1].astype(f32)

        gradient = known + pulled
        old_levels = levels[...]
        moved = jnp.clip(old_levels - tau * gradient, floor, ceiling)
        ext = 2.0 * moved - old_levels
        levels[...] = moved
        ext_half[it, my_chunk, my_rows, :] = ext.astype(bf16)
        extended[...] = ext

        @pl.loop(0, chunks)
        def _(j):
            c = far_chunk(j)
            for g in range(groups):
                other = c * groups + g

                @pl.when(other != chip)
                def _():
                    ext_out(it, other * 2 + 1).start()

                @pl.when(both_cores(c))
                def _():
                    ext_out(it, other * 2).start()

        if groups > 1:
            @pl.when(my_group > 0)
            def _():
                halo_ext_copy(it, me - 2).start()
                halo_ext_copy(it, me - 2).wait_send()

            @pl.when(my_group < groups - 1)
            def _():
                halo_ext_copy(it, me + 2).wait_recv()

            @pl.when(my_group == groups - 1)
            def _():
                halo_ext[it] = jnp.zeros_like(halo_ext[it])

            edge_ext = halo_ext[it][0:1]
        else:
            edge_ext = jnp.zeros((1, width), f32)

        after = jnp.where(block_row == ROWS - 1, edge_ext, pltpu.roll(ext, ROWS - 1, 0))
        change = ramp_on * (after - ext)
        last_hour = block_row + my_group * ROWS == hours - 1
        change = jnp.where(last_hour, 0.0, change)
        trial = ramp_now + sigma * change
        ramp_new = trial - jnp.clip(trial, -sigma * ramp_limit, sigma * ramp_limit)
        ramp[...] = ramp_new

        row_sums = to_lanes(jnp.sum(ext, axis=1, keepdims=True))
        primal_sq = fold((moved - old_levels) ** 2)
        ramp_sq = fold((ramp_new - ramp_now) ** 2)
        stats[it + 1, chip] = jnp.where(
            stat_row == 0, row_sums,
            jnp.where(stat_row == 1, primal_sq, jnp.where(stat_row == 2, ramp_sq, 0.0)),
        )

        @pl.when(it == ITERS - 1)
        def _():
            stat_start(it + 1)
            for r in range(members):
                rows = slice(r * hour_rows, (r + 1) * hour_rows)
                frag_out[r, 0] = moved[rows, :]
                frag_out[r, 1] = ramp_new[rows, :]
            for r in range(members):
                target = my_group * members + r

                @pl.when(target != me)
                def _():
                    fin_copy(r, my_chunk, target).start()

                @pl.when(target == me)
                def _():
                    frag_in[my_chunk] = frag_out[r]

    def line_limits():
        for i in range(6, 9):
            staged(i).wait()

        row_iota = lax.broadcasted_iota(jnp.int32, (128, lines), 0)
        values = table[...].T
        part_a = values.astype(bf16)
        rest = values - part_a.astype(f32)
        part_b = rest.astype(bf16)
        part_c = (rest - part_b.astype(f32)).astype(bf16)
        for k in range(ctgs):
            which = index[k:k + 1, :]
            high = lax.shift_right_logical(which, 7)
            low = lax.bitwise_and(which, 127)
            blocks = table.shape[0] // 128
            got = jnp.zeros((128, lines), f32)
            for b in range(blocks):
                pick = jnp.where(row_iota + b * 128 == high, 1.0, 0.0).astype(bf16)
                for part in (part_a, part_b, part_c):
                    got = got + jnp.dot(part[:, b * 128:(b + 1) * 128], pick, preferred_element_type=f32)
            limit[:, k * lines:(k + 1) * lines] = jnp.sum(
                jnp.where(row_iota == low, got, 0.0), axis=0, keepdims=True
            )
            base[:, k * lines:(k + 1) * lines] = base_in[:, k, :]

    def take(it, c):
        for g in range(groups):
            other = c * groups + g

            @pl.when(jnp.logical_not(owner & (other == chip)))
            def _():
                ext_pass(it, other).wait_recv()

    def take_and_pass(it, c):
        take(it, c)

        @pl.when(owner & jnp.logical_not(both_cores(c)))
        def _():
            for g in range(groups):
                ext_pass(it, c * groups + g).start()

    def flow(x, w):
        return lax.dot_general(x, w, (((1,), (1,)), ((), ())), preferred_element_type=f32)

    def small_out(i):
        src, dst = ((price, out_price), (starts.at[0], out_levels), (starts.at[1], out_ramp))[i]
        return pltpu.make_async_copy(src, dst, pull_recv.at[i])

    def write_small():
        @pl.when(owner)
        def _():
            stat_wait(ITERS)
            absorb(ITERS, step_size * omega[0:1, 0:1])
            price_copy().start()

        for c in range(chunks):
            peer = (c * groups + home_group) * 2 + 1

            @pl.when(peer != me)
            def _():
                fin_copy(0, c, peer).wait_recv()

        for c in range(chunks):
            for which in range(2):
                starts[which, :, c * width:(c + 1) * width] = frag_in[c, which]
        small_out(1).start()
        small_out(2).start()

    turns = (chunks - 1) // 2
    blocks = ctgs * lines // 256

    def turn(first, last):
        @pl.loop(first * blocks, last * blocks)
        def _(i):
            j = lax.div(i, blocks)
            block = pl.ds(pl.multiple_of(lax.rem(i, blocks) * 256, 256), 256)
            turned[j, :, block] = masked[far_chunk(j), block, :].T

    @pl.loop(0, ITERS)
    def _(it):
        @pl.when(it > 0)
        def _():
            @pl.loop(0, chunks)
            def _(j):
                product(far_chunk(j))
                deliver(it, j)

                @pl.when((j == STAT) & owner)
                def _():
                    halo_ramp_start(it)
                    flow_stat_copy(it).wait_recv()
                    stats[it, chip, 3:4] = stats[it, chip, 3:4] + flow_stat[it, 0:1]
                    stat_start(it)

                forward(it, j - LAG)

            @pl.when(it < 3)
            def _():
                turn(1 + (it - 1) * turns, it * turns)

        @pl.when(it == 0)
        def _():
            turn(0, 1)

        pull_sent(it)

        @pl.when(owner)
        def _():
            primal(it)

        take(it, my_chunk)
        flow_acc[...] = flow(ext_half[it, my_chunk], masked[my_chunk])

        @pl.when(it == 0)
        def _():
            line_limits()

        @pl.when(it == 1)
        def _():
            turn(turns, turns + 1)

        @pl.when(it == 2)
        def _():
            turn(2 * turns, 2 * turns + 1)

        near = my_pair * 2 + 1 - my_side
        take_and_pass(it, near)

        @pl.when(it < 2)
        def _():
            flow_acc[...] += flow(ext_half[it, near], masked[near])

        @pl.when(it > 1)
        def _():
            flow_acc[...] += jnp.dot(
                ext_half[it, near], turned[2 * turns], preferred_element_type=f32
            )

        @pl.loop(1, pairs + AHEAD)
        def _(j):
            @pl.when(j < pairs)
            def _():
                c = near_pair(j) * 2
                take_and_pass(it, c)
                take_and_pass(it, c + 1)

            @pl.when((it == ITERS - 1) & (j == pairs))
            def _():
                write_small()

            @pl.when(j > AHEAD)
            def _():
                place = (pairs - 1 - j + AHEAD) * 2
                c, d = far_chunk(place), far_chunk(place + 1)
                x = jnp.concatenate([ext_half[it, c], ext_half[it, d]], axis=1)
                ready = (it > 1) | ((it == 1) & (place <= turns - 1))

                @pl.when(ready)
                def _():
                    w = jnp.concatenate([turned[place], turned[place + 1]], axis=0)
                    flow_acc[...] += jnp.dot(x, w, preferred_element_type=f32)

                @pl.when(jnp.logical_not(ready))
                def _():
                    w = jnp.concatenate([masked[c], masked[d]], axis=1)
                    flow_acc[...] += flow(x, w)

        @pl.when(owner)
        def _():
            @pl.loop(0, chunks)
            def _(c):
                for g in range(groups):
                    other = c * groups + g

                    @pl.when(other != chip)
                    def _():
                        ext_out(it, other * 2 + 1).wait_send()

                    @pl.when(both_cores(c))
                    def _():
                        ext_out(it, other * 2).wait_send()

                    @pl.when(jnp.logical_not(both_cores(c)))
                    def _():
                        ext_pass(it, other).wait_send()

            @pl.when(it > 0)
            def _():
                omega_copy().wait_send()

        @pl.when((it == 0) & owner)
        def _():
            stat_wait(0)
            first = stats[0, 0]
            for q in range(1, chips):
                first = first + stats[0, q]
            price[1:2] = first[0:1]

        @pl.when((it > 0) & jnp.logical_not(owner))
        def _():
            omega_copy().wait_recv()

        @pl.when(it == ITERS - 1)
        def _():
            @pl.when(jnp.logical_not(owner))
            def _():
                price_copy().wait_recv()

            small_out(0).start()

        sigma = step_size * omega[0:1, 0:1]
        old_dual = dual[...]
        trial = old_dual + sigma * flow_acc[...]
        bound = limit[...]
        dual_new = trial - jnp.clip(trial, sigma * (base[...] - bound), sigma * (base[...] + bound))
        dual[...] = dual_new
        dual_half[...] = dual_new.astype(bf16)

        @pl.when(it < ITERS - 1)
        def _():
            flow_sq = fold((dual_new - old_dual) ** 2)

            @pl.when(owner)
            def _():
                stats[it + 1, chip, 3:4] = flow_sq

            @pl.when(jnp.logical_not(owner))
            def _():
                @pl.when(it > 0)
                def _():
                    flow_stat_copy(it).wait_send()

                flow_stat[0] = jnp.broadcast_to(flow_sq, (8, 128))
                flow_stat_copy(it + 1).start()

    dual_out = pltpu.make_async_copy(dual, out_dual, ext_send.at[0])
    dual_out.start()

    @pl.when(owner)
    def _():
        for r in range(members):
            target = my_group * members + r

            @pl.when(target != me)
            def _():
                fin_copy(r, my_chunk, target).wait_send()

        price_copy().wait_send()

    @pl.when(jnp.logical_not(owner))
    def _():
        flow_stat_copy(0).wait_send()

    for i in range(3):
        small_out(i).wait()
    dual_out.wait()


def finish(
    levels, dual, ramp, price, out_levels, out_dual, out_ramp, out_price,
    level_box, dual_box, tile_box, ramp_box, price_box, own_price, in_sem, out_sem,
):
    hours, ctgs, lines = out_dual.shape
    hour_rows = own_price.shape[1]
    pieces = hours // 8

    def dual_in(p):
        return pltpu.make_async_copy(dual.at[p * 8:p * 8 + 8], dual_box.at[p], in_sem.at[3 + p])

    def dual_out(p):
        return pltpu.make_async_copy(tile_box.at[p], out_dual.at[p * 8:p * 8 + 8], out_sem.at[3 + p])

    small_in = (
        pltpu.make_async_copy(price, price_box, in_sem.at[0]),
        pltpu.make_async_copy(levels, level_box, in_sem.at[1]),
        pltpu.make_async_copy(ramp, ramp_box, in_sem.at[2]),
    )
    small_out = (
        pltpu.make_async_copy(own_price, out_price, out_sem.at[0]),
        pltpu.make_async_copy(level_box, out_levels, out_sem.at[1]),
        pltpu.make_async_copy(ramp_box, out_ramp, out_sem.at[2]),
    )
    for p in range(pieces):
        dual_in(p).start()
    for copy in small_in:
        copy.start()
    for p in range(pieces):
        dual_in(p).wait()
        for k in range(ctgs):
            tile_box[p, :, k, :] = dual_box[p, :, k * lines:(k + 1) * lines]
        dual_out(p).start()
    small_in[0].wait()
    lane = lax.broadcasted_iota(jnp.int32, (1, 128), 1) - lax.axis_index("ctg") * hour_rows
    for r in range(hour_rows):
        own_price[0:1, r:r + 1] = jnp.sum(
            jnp.where(lane == r, price_box[0:1], 0.0), axis=1, keepdims=True
        )
    small_out[0].start()
    for i in (1, 2):
        small_in[i].wait()
        small_out[i].start()
    for p in range(pieces):
        dual_out(p).wait()
    for copy in small_out:
        copy.wait()


def body(
    flow_tiles,
    tile_pattern,
    monitored,
    ratings,
    base_flow,
    unit_cost,
    unit_floor,
    unit_span,
    ramp_limit,
    ramp_mask,
    demand,
    start_output,
    start_flow_dual,
    start_ramp_dual,
):
    f32, bf16 = jnp.float32, jnp.bfloat16
    ctgs, lines, unit_count = flow_tiles.shape
    n = lax.axis_size("ctg")
    hour_rows = start_output.shape[0]
    hours = hour_rows * n
    groups = hours // ROWS
    chips = n // 2
    chunks = chips // groups
    members = ROWS // hour_rows
    width = unit_count // chunks
    flat = ctgs * lines
    step_size = 0.5 / (2.0 + math.sqrt(ctgs * n * lines / unit_count))
    balance = 1.0 / math.sqrt(unit_count)

    gate_rows = ctgs * tile_pattern.shape[1]

    vmem = pl.BlockSpec(memory_space=pltpu.VMEM)
    hbm = pl.BlockSpec(memory_space=pl.ANY)
    sem = pltpu.SemaphoreType.DMA
    out = pl.pallas_call(
        functools.partial(kernel, n, hour_rows, step_size, balance),
        out_shape=(
            jax.ShapeDtypeStruct((hour_rows, unit_count), f32),
            jax.ShapeDtypeStruct((hours, flat), f32),
            jax.ShapeDtypeStruct((hour_rows, unit_count), f32),
            jax.ShapeDtypeStruct((8, 128), f32),
        ),
        in_specs=[hbm] * 14,
        out_specs=(hbm,) * 4,
        scratch_shapes=[
            pltpu.VMEM((chunks, flat, width), bf16),
            pltpu.VMEM((chunks - 1, width, flat), bf16),
            pltpu.VMEM((chunks, gate_rows, width), f32),
            pltpu.VMEM(tile_pattern.shape, jnp.int32),
            pltpu.VMEM((gate_rows, tile_pattern.shape[2]), f32),
            pltpu.VMEM(monitored.shape, jnp.int32),
            pltpu.VMEM((ratings.shape[0] // 128, 128), f32),
            pltpu.VMEM(base_flow.shape, f32),
            pltpu.VMEM(start_flow_dual.shape, f32),
            pltpu.VMEM((3, 1, width), f32),
            pltpu.VMEM((1, width), jnp.int32),
            pltpu.VMEM((1, hour_rows), f32),
            pltpu.VMEM((hours, flat), f32),
            pltpu.VMEM((hours, flat), f32),
            pltpu.VMEM((4, hour_rows, unit_count), f32),
            pltpu.VMEM((1, flat), f32),
            pltpu.VMEM((hours, flat), bf16),
            pltpu.VMEM((hours, flat), f32),
            pltpu.VMEM((members, 4, hour_rows, width), f32),
            pltpu.VMEM((chunks, 2, hour_rows, width), f32),
            pltpu.VMEM((members, 2, hour_rows, width), f32),
            pltpu.VMEM((ROWS, width), f32),
            pltpu.VMEM((ROWS, width), f32),
            pltpu.VMEM((ROWS, width), f32),
            pltpu.VMEM((ROWS, width), f32),
            pltpu.VMEM((ITERS, 8, width), f32),
            pltpu.VMEM((ITERS, 8, width), f32),
            pltpu.VMEM((chunks, hours, width), bf16),
            pltpu.VMEM((ITERS, chunks, hours, width), bf16),
            pltpu.VMEM((chunks, hours, width), bf16),
            pltpu.VMEM((ITERS, n, ROWS, width), bf16),
            pltpu.VMEM((ITERS, chunks, hours, width), bf16),
            pltpu.VMEM((ITERS + 1, chips, 4, 128), f32),
            pltpu.VMEM((ITERS, 8, 128), f32),
            pltpu.VMEM((8, 128), f32),
            pltpu.VMEM((8, 128), f32),
            sem((chunks,)), sem((members,)), sem((chips,)), sem((n,)),
            sem((n,)), sem((chips,)), sem((max(chips, chunks),)), sem((2, chips)),
            sem((6,)), sem((4,)),
        ],
        compiler_params=pltpu.CompilerParams(collective_id=0, has_side_effects=True),
    )(
        flow_tiles.reshape(flat, unit_count),
        tile_pattern,
        monitored,
        ratings.reshape(-1, 128),
        base_flow,
        start_flow_dual,
        start_output,
        unit_cost,
        start_ramp_dual,
        demand[None],
        unit_floor[None],
        unit_span[None],
        ramp_limit[None],
        ramp_mask[None],
    )
    levels, dual, ramp, price = pl.pallas_call(
        finish,
        out_shape=(
            jax.ShapeDtypeStruct((hour_rows, unit_count), f32),
            jax.ShapeDtypeStruct((hours, ctgs, lines), f32),
            jax.ShapeDtypeStruct((hour_rows, unit_count), f32),
            jax.ShapeDtypeStruct((1, hour_rows), f32),
        ),
        in_specs=[hbm] * 4,
        out_specs=(hbm,) * 4,
        scratch_shapes=[
            pltpu.VMEM((hour_rows, unit_count), f32),
            pltpu.VMEM((hours // 8, 8, flat), f32),
            pltpu.VMEM((hours // 8, 8, ctgs, lines), f32),
            pltpu.VMEM((hour_rows, unit_count), f32),
            pltpu.VMEM((8, 128), f32),
            pltpu.VMEM((1, hour_rows), f32),
            sem((3 + hours // 8,)),
            sem((3 + hours // 8,)),
        ],
    )(*out)
    return levels, dual, ramp, price.reshape(hour_rows)


def solution(mesh):
    return jax.shard_map(
        body,
        mesh=mesh,
        in_specs=(
            P("ctg", None, None),
            P("ctg", None, None),
            P("ctg", None),
            P(),
            P("grp", "ctg", None),
            P(("grp", "ctg"), None),
            P(),
            P(),
            P(),
            P(),
            P(("grp", "ctg")),
            P(("grp", "ctg"), None),
            P("grp", "ctg", None),
            P(("grp", "ctg"), None),
        ),
        out_specs=(
            P(("grp", "ctg"), None),
            P("grp", "ctg", None),
            P(("grp", "ctg"), None),
            P(("grp", "ctg")),
        ),
        check_vma=False,
    )
```
